256 devices in a mesh: rel: 8 (over x_lo, y), tgt: 32 (over x_hi, z, core).
Axes of the slice: x: 4 (x_hi: 2, x_lo: 2; x = x_hi * 2 + x_lo), y: 4, z: 8, core: 2. Of those that a mesh axis runs over, the one named last changes fastest.
Arguments:
- features: bfloat16 [8192, 768], P('tgt'), may hold values from -6 to 6
- weights: bfloat16 [16, 768, 768], P('rel'), may hold values from -0.109375 to 0.109375
- bias: float32 [768], replicated, may hold values from -3 to 3
- cotangent: bfloat16 [8192, 768], P('tgt'), may hold values from -0.52734375 to 0.52734375
- tile_values: int32 [16, 8192, 8, 128], P('rel', 'tgt'), may hold values from 0 to 3, as said below
- tile_count: int32 [16, 64], P('rel', 'tgt'), may hold values from 1 to 8, as said below
- tile_slot: int32 [16, 64, 8], P('rel', 'tgt'), may hold values from 0 to 31, as said below
- source_blocks: int32 [32, 32], replicated, may hold values from -1 to 1, as said below
Outputs:
- output: bfloat16 [8192, 768], P('tgt', 'rel')
- grad_weights: float32 [16, 768, 768], P('rel', 'tgt')
- grad_features: float32 [64, 128, 768], P('tgt', 'rel')
The draws below stay inside these ranges and needn't reach their ends.
Inputs may be any that keep to these rules, and one draw needn't show every extreme that they name: `tile_values`: entries in tile slots at or beyond the live count are arbitrary and take no part. `tile_count`: every relation has some tile row of targets with all 8 slots live. `tile_slot`: every tile slot, live or not, names an owner for which the target block's entry of source_blocks is not -1. `source_blocks`: entry [t, o] is a block index within owner o's 2 blocks, or -1 where target block t reads nothing from o; entry [t, t] is never -1.
All inputs are finite; a program needn't handle non-finite values.
Results may differ from the reference program's by a relative error of at most 0.01.
Values may be sent and summed in bfloat16 or wider, within the bound.
No kernel may reach another device: no remote copies, remote signals or barrier semaphores. Data moves between devices by JAX's collectives and lax.ppermute only.
A program may use at most 64 MiB of HBM per device.

```python
import jax
import jax.numpy as jnp
from jax import lax

D = 768
BLK = 128
SLOTS = 8
REL_DEV = 2
TGT_DEV = 256
REL = 16
OWNERS = 32
NODES = 8192
N_REL = 8


def source_table(key):
    picked = jax.random.randint(jax.random.fold_in(key, 11), (OWNERS, OWNERS), 0, TGT_DEV // BLK)
    keeper = jax.random.randint(jax.random.fold_in(key, 12), (OWNERS, OWNERS), 0, 4) > 0
    diagonal = jnp.eye(OWNERS, dtype=bool)
    return jnp.where(keeper | diagonal, picked, -1).astype(jnp.int32)


def draw_source_blocks(key, part):
    return source_table(key)


def draw_tile_slot(key, part):
    table = source_table(key)
    tile_rows = NODES // BLK
    wanted = jax.random.randint(jax.random.fold_in(key, 13), (REL, tile_rows, SLOTS), 0, OWNERS)
    home = (jnp.arange(tile_rows, dtype=jnp.int32) // (TGT_DEV // BLK))[None, :, None]
    home_full = jnp.broadcast_to(home, (REL, tile_rows, SLOTS))
    listed = table[home_full, wanted] >= 0
    return jnp.where(listed, wanted, home_full).astype(jnp.int32)


def draw_tile_count(key, part):
    tile_rows = NODES // BLK
    hotness = jax.random.randint(jax.random.fold_in(key, 21), (REL, OWNERS), 0, 4) == 0
    hot_rows = jnp.repeat(hotness, TGT_DEV // BLK, axis=1)
    higher = jax.random.randint(jax.random.fold_in(key, 22), (REL, tile_rows), SLOTS // 2 + 1, SLOTS + 1)
    lower_counts = jax.random.randint(jax.random.fold_in(key, 23), (REL, tile_rows), 1, SLOTS // 2 + 1)
    counts = jnp.where(hot_rows, higher, lower_counts)
    forced = jnp.arange(tile_rows)[None, :] == jnp.arange(REL)[:, None] * 5 % tile_rows
    return jnp.where(forced, SLOTS, counts).astype(jnp.int32)


def draw_tile_values(key, part):
    shape_all = (REL, NODES, SLOTS, BLK)
    uniform_ints = jax.random.randint(jax.random.fold_in(key, 31), shape_all, 0, 15)
    levels = jnp.where(uniform_ints < 9, 0, (uniform_ints - 9) // 2 + 1)
    row_alive = jax.random.randint(jax.random.fold_in(key, 33), (REL, NODES, 1, 1), 0, 16) > 0
    return (levels * row_alive).astype(jnp.int32)


def level_of(key, shape, shards, least, largest):
    factor_of, own = 1.0, jax.random.fold_in(key, 6)
    for dim, blocks in shards:
        heights = jnp.exp(jax.random.uniform(jax.random.fold_in(own, dim), (blocks,), jnp.float32, least / len(shards), largest / len(shards)))
        factor_of = factor_of * jnp.repeat(heights, shape[dim] // blocks).reshape([-1 if axis == dim else 1 for axis in range(len(shape))])
    return factor_of


def centred(stream_key, extent, deviation, reach, split=(), kind=jnp.bfloat16):
    drawn = jax.random.normal(stream_key, extent, jnp.float32) * deviation
    if len(split) > 0:
        drawn = level_of(stream_key, extent, split, -0.22, 0.18) * drawn
    return jnp.clip(drawn, min=-reach, max=reach).astype(kind)


def setup_inputs(seed: int = 0) -> dict:
    key_list = jax.random.split(jax.random.key(seed), 9)
    features = centred(key_list[0], (NODES, D), 1.0, 6.0, ((0, 32),))
    weights = centred(key_list[1], (REL, D, D), (4 * D) ** -0.5, 0.109375, ((0, 8),))
    bias = centred(key_list[2], (D,), 0.5, 3.0, (), jnp.float32)
    cotangent = centred(key_list[3], (NODES, D), (8.0 / NODES ** 0.5), 0.52734375, ((0, 32),))
    tile_values = draw_tile_values(jax.random.fold_in(key_list[8], 71), 0)
    tile_count = draw_tile_count(jax.random.fold_in(key_list[8], 71), 0)
    tile_slot = draw_tile_slot(jax.random.fold_in(key_list[8], 71), 0)
    source_blocks = draw_source_blocks(jax.random.fold_in(key_list[8], 71), 0)
    return {"features": features, "weights": weights, "bias": bias, "cotangent": cotangent, "tile_values": tile_values, "tile_count": tile_count, "tile_slot": tile_slot, "source_blocks": source_blocks}


HIGHEST = lax.Precision.HIGHEST

def silu_pair(values):
    sigmoid = jax.nn.sigmoid(values)
    return (values * sigmoid, sigmoid * (1.0 + values * (1.0 - sigmoid)))

def reference(features, weights, bias, cotangent, tile_values, tile_count, tile_slot, source_blocks):
    sections = TGT_DEV // BLK
    own_blocks = features.reshape(OWNERS, sections, BLK, D)
    weights_wide = weights.astype(jnp.float32)
    owner_ids = jnp.arange(OWNERS, dtype=jnp.int32)
    section_ids = jnp.arange(sections, dtype=jnp.int32)
    slot_ids = jnp.arange(SLOTS, dtype=jnp.int32)

    def one_block(state_pair, target):
        weight_sum, feature_sum = state_pair
        values = lax.dynamic_slice_in_dim(tile_values, target * TGT_DEV, TGT_DEV, 1)
        counts = lax.dynamic_slice_in_dim(tile_count, target * sections, sections, 1)
        slots_here = lax.dynamic_slice_in_dim(tile_slot, target * sections, sections, 1)
        requested = lax.dynamic_index_in_dim(source_blocks, target, 0, keepdims=False)
        cot_rows = lax.dynamic_slice_in_dim(cotangent, target * TGT_DEV, TGT_DEV, 0)
        chosen = own_blocks[owner_ids, jnp.maximum(requested, 0)]
        fetched = jnp.where((requested >= 0)[:, None, None], chosen, jnp.zeros_like(chosen))
        live_mask = (slot_ids[None, None, :] < counts[:, :, None]).astype(jnp.int32)
        counted = values.reshape(REL, sections, BLK, SLOTS, BLK) * live_mask[:, :, None, :, None]
        degree = lax.optimization_barrier(jnp.sum(counted, axis=(3, 4))).astype(jnp.float32)
        adjacency = (counted.astype(jnp.float32) / jnp.sqrt(jnp.maximum(degree, 1.0))[..., None, None]).astype(jnp.bfloat16)
        adj_wide = adjacency.astype(jnp.float32)
        sources = fetched[slots_here].astype(jnp.float32)
        messages = jnp.einsum('rqisc,rqscd->rqid', adj_wide, sources, precision=HIGHEST).astype(jnp.bfloat16)
        msg_wide = messages.reshape(REL, TGT_DEV, D).astype(jnp.float32)
        preact = jnp.einsum('rnd,rde->ne', msg_wide, weights_wide, precision=HIGHEST) + bias
        activated, derivative = silu_pair(preact)
        grad_pre = (cot_rows.astype(jnp.float32) * derivative).astype(jnp.bfloat16)
        grad_wide = grad_pre.astype(jnp.float32)
        grad_messages = jnp.einsum('ne,rde->rnd', grad_wide, weights_wide, precision=HIGHEST).astype(jnp.bfloat16)
        weight_sum = weight_sum + jnp.einsum('rnd,ne->rde', msg_wide, grad_wide, precision=HIGHEST)
        grads_blocked = grad_messages.astype(jnp.float32).reshape(REL, sections, BLK, D)
        contrib = jnp.einsum('rqisc,rqid->rqscd', adj_wide, grads_blocked, precision=HIGHEST)
        selector = (slots_here[..., None] == owner_ids).astype(jnp.float32)
        grouped = jnp.einsum('grqso,grqscd->gocd', selector.reshape(N_REL, REL_DEV, sections, SLOTS, OWNERS), contrib.reshape(N_REL, REL_DEV, sections, SLOTS, BLK, D), precision=HIGHEST)
        rounded = lax.optimization_barrier(grouped.astype(jnp.bfloat16)).astype(jnp.float32)
        per_owner = lax.optimization_barrier(jnp.sum(rounded, axis=0))
        placed = (requested[:, None] == section_ids[None, :]).astype(jnp.float32)
        feature_sum = feature_sum + jnp.einsum('ok,ocd->okcd', placed, per_owner, precision=HIGHEST)
        return ((weight_sum, feature_sum), activated.astype(jnp.bfloat16))
    initial = (jnp.zeros((REL, D, D), jnp.float32), jnp.zeros((OWNERS, sections, BLK, D), jnp.float32))
    finals, outputs = lax.scan(one_block, initial, jnp.arange(OWNERS, dtype=jnp.int32))
    weight_sum, feature_sum = finals
    return (outputs.reshape(NODES, D), weight_sum, feature_sum.reshape(NODES // BLK, BLK, D))
```

```python
import jax
import jax.numpy as jnp
from jax import lax
from jax.experimental import pallas as pl
from jax.experimental.pallas import tpu as pltpu
from jax.sharding import Mesh, PartitionSpec as P

F32 = jnp.float32
BF16 = jnp.bfloat16
BLK = 128
REL = ("xl", "y")
TGT = ("xh", "z", "core")
VMEM_LIMIT = 60 * 1024 * 1024


def params(*semantics):
    return pltpu.CompilerParams(
        dimension_semantics=semantics or None, vmem_limit_bytes=VMEM_LIMIT
    )


def smem():
    return pl.BlockSpec(memory_space=pltpu.MemorySpace.SMEM)


def vmem():
    return pl.BlockSpec(memory_space=pltpu.MemorySpace.VMEM)


def dot(a, b, ca, cb):
    return lax.dot_general(a, b, (((ca,), (cb,)), ((), ())), preferred_element_type=F32)


def adjacency_kernel(count_ref, values_ref, out_ref):
    r, q = pl.program_id(0), pl.program_id(1)
    count = count_ref[r, q]
    slots = values_ref.shape[2]
    live, degree = [], None
    for s in range(slots):
        v = values_ref[0, :, s, :]
        v = jnp.where(s < count, v, jnp.zeros_like(v)).astype(F32)
        live.append(v)
        degree = v if degree is None else degree + v
    total = jnp.sum(degree, axis=1, keepdims=True)
    scale = 1.0 / jnp.sqrt(jnp.maximum(total, 1.0))
    for s in range(slots):
        out_ref[0, :, s * BLK : (s + 1) * BLK] = (live[s] * scale).astype(BF16)


def adjacency_of(tile_values, tile_count):
    rels, rows, slots, cols = tile_values.shape
    return pl.pallas_call(
        adjacency_kernel,
        grid=(rels, rows // BLK),
        in_specs=[smem(), pl.BlockSpec((1, BLK, slots, cols), lambda r, q: (r, q, 0, 0))],
        out_specs=pl.BlockSpec((1, BLK, slots * cols), lambda r, q: (r, q, 0)),
        out_shape=jax.ShapeDtypeStruct((rels, rows, slots * cols), BF16),
        compiler_params=params("arbitrary", "arbitrary"),
        name="adjacency",
    )(tile_count, tile_values)


def outgoing_kernel(place_ref, table_ref, features_ref, out_ref, turned_ref):
    owner, first = place_ref[0], place_ref[1]
    turned_ref[...] = features_ref[...].T
    piece = turned_ref[pl.ds(pl.multiple_of(first, 32), 96), :]
    block0, block1 = piece[:, :BLK], piece[:, BLK:]
    for t in range(out_ref.shape[0]):
        k = table_ref[t, owner]
        picked = jnp.where(k == 1, block1, block0)
        out_ref[t] = jnp.where(k >= 0, picked, jnp.zeros_like(picked))


def outgoing_of(features, source_blocks, place):
    rows, width = features.shape
    return pl.pallas_call(
        outgoing_kernel,
        in_specs=[smem(), smem(), vmem()],
        out_specs=vmem(),
        out_shape=jax.ShapeDtypeStruct((source_blocks.shape[0], 96, BLK), BF16),
        scratch_shapes=[pltpu.VMEM((width, rows), BF16)],
        compiler_params=params(),
        name="outgoing",
    )(place, source_blocks, features)


def relation_of(i, place):
    core = place[2]
    return jnp.where(i < 4, 2 * i + core, 2 * (i - 4) + 1 - core)


def forward_kernel(
    place_ref, slot_ref, adj_ref, mine_ref, theirs_ref, w_mine_ref, w_theirs_ref,
    messages_ref, pre_ref, fetched_ref, acc_ref,
):
    i = pl.program_id(0)
    r = relation_of(i, place_ref)
    xl = place_ref[3]
    slots = 8

    @pl.when(i == 0)
    def _():
        fetched_ref[:, pl.ds(pl.multiple_of(xl * 96, 32), 96), :] = mine_ref[...]
        fetched_ref[:, pl.ds(pl.multiple_of((1 - xl) * 96, 32), 96), :] = theirs_ref[...]

    for q in range(2):
        base = (r * 2 + q) * slots
        wide = jnp.concatenate([fetched_ref[slot_ref[base + s]] for s in range(slots)], axis=1)
        part = adj_ref[0, q * BLK : (q + 1) * BLK, :]
        messages_ref[0, :, q * BLK : (q + 1) * BLK] = dot(wide, part, 1, 1).astype(BF16)

    @pl.when(i == 0)
    def _():
        acc_ref[...] = dot(w_mine_ref[0], messages_ref[0], 0, 0)

    @pl.when((i > 0) & (i < 4))
    def _():
        acc_ref[...] += dot(w_mine_ref[0], messages_ref[0], 0, 0)

    @pl.when(i >= 4)
    def _():
        acc_ref[...] += dot(w_theirs_ref[0], messages_ref[0], 0, 0)

    @pl.when(i == 7)
    def _():
        pre_ref[...] = acc_ref[...].astype(BF16)


def forward_of(place, slots, adjacency, mine, theirs, w_mine, w_theirs):
    rels, rows, wide = adjacency.shape
    width = w_mine.shape[2]
    spec = pltpu.PrefetchScalarGridSpec(
        num_scalar_prefetch=2,
        grid=(rels,),
        in_specs=[
            pl.BlockSpec((1, rows, wide), lambda i, p, s: (relation_of(i, p), 0, 0)),
            pl.BlockSpec(mine.shape, lambda i, p, s: (0, 0, 0)),
            pl.BlockSpec(mine.shape, lambda i, p, s: (0, 0, 0)),
            pl.BlockSpec((1, 192, width), lambda i, p, s: (jnp.minimum(i, 3), 0, 0)),
            pl.BlockSpec((1, 192, width), lambda i, p, s: (jnp.maximum(i - 4, 0), 0, 0)),
        ],
        out_specs=[
            pl.BlockSpec((1, 192, rows), lambda i, p, s: (relation_of(i, p), 0, 0)),
            pl.BlockSpec((width, rows), lambda i, p, s: (0, 0)),
        ],
        scratch_shapes=[pltpu.VMEM((mine.shape[0], 192, BLK), BF16), pltpu.VMEM((width, rows), F32)],
    )
    return pl.pallas_call(
        forward_kernel,
        grid_spec=spec,
        out_shape=[
            jax.ShapeDtypeStruct((rels, 192, rows), BF16),
            jax.ShapeDtypeStruct((width, rows), BF16),
        ],
        compiler_params=params("arbitrary"),
        name="forward",
    )(place, slots, adjacency, mine, theirs, w_mine, w_theirs)


def activation_kernel(arrived_ref, bias_ref, cotangent_ref, act_ref, grad_ref):
    pre = bias_ref[...]
    for g in range(arrived_ref.shape[0]):
        pre = pre + arrived_ref[g].astype(F32)
    sigmoid = jax.nn.sigmoid(pre)
    act_ref[...] = (pre * sigmoid).astype(BF16)
    derivative = sigmoid * (1.0 + pre * (1.0 - sigmoid))
    grad_ref[...] = (cotangent_ref[...].astype(F32) * derivative).astype(BF16)


def activation_of(arrived, bias, cotangent):
    shape = jax.ShapeDtypeStruct(arrived.shape[1:], BF16)
    return pl.pallas_call(
        activation_kernel,
        in_specs=[vmem()] * 3,
        out_specs=[vmem()] * 2,
        out_shape=[shape, shape],
        compiler_params=params(),
        name="activation",
    )(arrived, bias, cotangent)


def backward_kernel(
    place_ref, slot_ref, adj_ref, grad_ref, w_mine_ref, w_theirs_ref, keep_ref, send_ref, acc_ref
):
    i = pl.program_id(0)
    r = relation_of(i, place_ref)
    xl = place_ref[3]
    slots = 8

    @pl.when(i == 0)
    def _():
        acc_ref[...] = jnp.zeros_like(acc_ref)

    def spread(w):
        grads = dot(w, grad_ref[...], 1, 0).astype(BF16)
        for q in range(2):
            base = (r * 2 + q) * slots
            part = adj_ref[0, q * BLK : (q + 1) * BLK, :]
            wide = dot(grads[:, q * BLK : (q + 1) * BLK], part, 1, 0)
            for s in range(slots):
                acc_ref[slot_ref[base + s]] += wide[:, s * BLK : (s + 1) * BLK]

    @pl.when(i < 4)
    def _():
        spread(w_mine_ref[0])

    @pl.when(i >= 4)
    def _():
        spread(w_theirs_ref[0])

    @pl.when(i == 7)
    def _():
        keep_ref[...] = acc_ref[:, pl.ds(pl.multiple_of(xl * 96, 32), 96), :].astype(BF16)
        send_ref[...] = acc_ref[:, pl.ds(pl.multiple_of((1 - xl) * 96, 32), 96), :].astype(BF16)


def backward_of(place, slots, adjacency, grads, w_mine, w_theirs, owners):
    rels, rows, wide = adjacency.shape
    width = w_mine.shape[2]
    half = pl.BlockSpec((owners, 96, BLK), lambda i, p, s: (0, 0, 0))
    spec = pltpu.PrefetchScalarGridSpec(
        num_scalar_prefetch=2,
        grid=(rels,),
        in_specs=[
            pl.BlockSpec((1, rows, wide), lambda i, p, s: (relation_of(i, p), 0, 0)),
            pl.BlockSpec((width, rows), lambda i, p, s: (0, 0)),
            pl.BlockSpec((1, 192, width), lambda i, p, s: (jnp.minimum(i, 3), 0, 0)),
            pl.BlockSpec((1, 192, width), lambda i, p, s: (jnp.maximum(i - 4, 0), 0, 0)),
        ],
        out_specs=[half, half],
        scratch_shapes=[pltpu.VMEM((owners, 192, BLK), F32)],
    )
    shape = jax.ShapeDtypeStruct((owners, 96, BLK), BF16)
    return pl.pallas_call(
        backward_kernel,
        grid_spec=spec,
        out_shape=[shape, shape],
        compiler_params=params("arbitrary"),
        name="backward",
    )(place, slots, adjacency, grads, w_mine, w_theirs)


def weight_kernel(messages_ref, grad_ref, out_ref):
    first = dot(messages_ref[0], grad_ref[...], 1, 1)
    second = dot(messages_ref[1], grad_ref[...], 1, 1)
    for m in range(8):
        rows = slice(m * 24, (m + 1) * 24)
        piece = jnp.concatenate([first[rows], second[rows]], axis=0)
        out_ref[m % 2, 0, m // 2] = piece.astype(BF16)


def weight_terms_of(messages, grads):
    rels, deep, rows = messages.shape
    width = grads.shape[0]
    return pl.pallas_call(
        weight_kernel,
        grid=(rels // 2,),
        in_specs=[
            pl.BlockSpec((2, deep, rows), lambda j: (j, 0, 0)),
            pl.BlockSpec((width, rows), lambda j: (0, 0)),
        ],
        out_specs=pl.BlockSpec((2, 1, 4, 48, width), lambda j: (0, j, 0, 0, 0)),
        out_shape=jax.ShapeDtypeStruct((2, rels // 2, 4, 48, width), BF16),
        compiler_params=params("arbitrary"),
        name="weight_terms",
    )(messages, grads)


def owned_kernel(place_ref, table_ref, arrived_ref, out_ref):
    owner = place_ref[0]
    zero = jnp.zeros(arrived_ref.shape[1:], F32)
    sums = [zero, zero]
    for t in range(arrived_ref.shape[0]):
        k = table_ref[t, owner]
        v = arrived_ref[t].astype(F32)
        for b in range(2):
            sums[b] = sums[b] + jnp.where(k == b, v, zero)
    for b in range(2):
        turned = sums[b].T
        for g in range(out_ref.shape[0]):
            out_ref[g, b] = turned[g * 16 : (g + 1) * 16, :]


def owned_of(place, source_blocks, arrived, groups):
    return pl.pallas_call(
        owned_kernel,
        in_specs=[smem(), smem(), vmem()],
        out_specs=vmem(),
        out_shape=jax.ShapeDtypeStruct((groups, 2, BLK // groups, 96), F32),
        compiler_params=params(),
        name="owned",
    )(place, source_blocks, arrived)


def swap(value, axis):
    return lax.ppermute(value, axis, [(0, 1), (1, 0)])


def exchange(value, axis):
    return lax.all_to_all(value, axis, 0, 0, tiled=True)


def copies(value, axis, count):
    return exchange(jnp.broadcast_to(value[None], (count, *value.shape)), axis)


def to_owner():
    def place(y, xh, z, c):
        return ((y * 2 + xh) * 8 + z) * 2 + c
    moves = []
    for y in range(4):
        for xh in range(2):
            for z in range(8):
                for c in range(2):
                    target = place(2 * xh + z // 4, y // 2, 4 * (y % 2) + z % 4, c)
                    moves.append((place(y, xh, z, c), target))
    return moves


def per_device(
    features, weights, bias, cotangent, tile_values, tile_count, tile_slot, source_blocks
):
    groups = 8
    owners = source_blocks.shape[0]
    width = features.shape[1]
    xl, y, core = lax.axis_index("xl"), lax.axis_index("y"), lax.axis_index("core")
    owner = lax.axis_index(TGT)
    group = lax.axis_index(REL)
    place = jnp.stack([owner, 192 * y + 96 * xl, core, xl]).astype(jnp.int32)

    own_adjacency = adjacency_of(tile_values, tile_count)
    adjacency = lax.all_gather(own_adjacency, "y", axis=0, tiled=True)
    mine = exchange(outgoing_of(features, source_blocks, place), TGT)
    theirs = swap(mine, "xl")
    slots = copies(tile_slot.reshape(1, -1), "y", 4).reshape(-1)
    w_own = lax.dynamic_index_in_dim(weights, core, 0, keepdims=False)
    w_mine = exchange(w_own.reshape(4, 192, width), "y")
    w_theirs = swap(w_mine, "core")

    messages, part = forward_of(place, slots, adjacency, mine, theirs, w_mine, w_theirs)
    share = width // groups
    arrived = exchange(part.reshape(groups, share, -1), REL)
    bias_share = lax.dynamic_slice_in_dim(bias, group * share, share)[:, None]
    cotangent_share = lax.dynamic_slice_in_dim(cotangent, group * share, share, 1).T
    activated, grad_share = activation_of(arrived, bias_share, cotangent_share)
    output = activated.T
    grads = copies(grad_share, REL, groups).reshape(width, -1)

    keep, send = backward_of(place, slots, adjacency, grads, w_mine, w_theirs, owners)
    received = swap(send, "xl")
    partial = (keep.astype(F32) + received.astype(F32)).astype(BF16)
    returned = exchange(partial, TGT)
    cut = owned_of(place, source_blocks, returned, groups)
    columns = exchange(cut, REL).reshape(2, 4, 2, BLK // groups, 96)
    grad_features = columns.transpose(2, 3, 1, 0, 4).reshape(2, BLK // groups, width)

    terms = weight_terms_of(messages, grads)
    pair = exchange(terms, "core").astype(F32)
    chip = (pair[0] + pair[1]).astype(BF16).reshape(16, 48, width)
    pieces = exchange(chip, ("xh", "z"))
    piece = jnp.sum(pieces.astype(F32), axis=0).reshape(2, 24, width)
    grad_weights = lax.ppermute(piece, ("y", *TGT), to_owner())
    return (output, grad_weights, grad_features)


def solution(mesh):
    fine = Mesh(mesh.devices.reshape(2, 4, 2, 8, 2), (*REL, *TGT))
    placed = (
        P(TGT, None),
        P(REL, None, None),
        P(),
        P(TGT, None),
        P(REL, TGT, None, None),
        P(REL, TGT),
        P(REL, TGT, None),
        P(),
    )
    return jax.shard_map(
        per_device,
        mesh=fine,
        in_specs=placed,
        out_specs=(P(TGT, REL), P(REL, TGT, None), P(TGT, REL, None)),
        check_vma=False,
    )
```

```python
import jax
import jax.numpy as jnp
from jax import lax
from jax.experimental import pallas as pl
from jax.experimental.pallas import tpu as pltpu
from jax.sharding import Mesh, PartitionSpec as P

F32 = jnp.float32
BF16 = jnp.bfloat16
BLK = 128
REL = ("xl", "y")
TGT = ("xh", "z", "core")
VMEM_LIMIT = 60 * 1024 * 1024


def params(*semantics):
    return pltpu.CompilerParams(
        dimension_semantics=semantics or None, vmem_limit_bytes=VMEM_LIMIT
    )


def smem():
    return pl.BlockSpec(memory_space=pltpu.MemorySpace.SMEM)


def vmem():
    return pl.BlockSpec(memory_space=pltpu.MemorySpace.VMEM)


def dot(a, b, ca, cb):
    return lax.dot_general(a, b, (((ca,), (cb,)), ((), ())), preferred_element_type=F32)


def adjacency_kernel(count_ref, values_ref, out_ref):
    r, q = pl.program_id(0), pl.program_id(1)
    count = count_ref[r, q]
    slots = values_ref.shape[2]
    live, degree = [], None
    for s in range(slots):
        v = values_ref[0, :, s, :]
        v = jnp.where(s < count, v, jnp.zeros_like(v)).astype(F32)
        live.append(v)
        degree = v if degree is None else degree + v
    total = jnp.sum(degree, axis=1, keepdims=True)
    scale = 1.0 / jnp.sqrt(jnp.maximum(total, 1.0))
    for s in range(slots):
        out_ref[0, :, s * BLK : (s + 1) * BLK] = (live[s] * scale).astype(BF16)


def adjacency_of(tile_values, tile_count):
    rels, rows, slots, cols = tile_values.shape
    return pl.pallas_call(
        adjacency_kernel,
        grid=(rels, rows // BLK),
        in_specs=[smem(), pl.BlockSpec((1, BLK, slots, cols), lambda r, q: (r, q, 0, 0))],
        out_specs=pl.BlockSpec((1, BLK, slots * cols), lambda r, q: (r, q, 0)),
        out_shape=jax.ShapeDtypeStruct((rels, rows, slots * cols), BF16),
        compiler_params=params("arbitrary", "arbitrary"),
        name="adjacency",
    )(tile_count, tile_values)


def outgoing_kernel(place_ref, table_ref, features_ref, out_ref, turned_ref):
    owner, first = place_ref[0], place_ref[1]
    turned_ref[...] = features_ref[...].T
    piece = turned_ref[pl.ds(pl.multiple_of(first, 64), 192), :]
    block0, block1 = piece[:, :BLK], piece[:, BLK:]
    for t in range(out_ref.shape[0]):
        k = table_ref[t, owner]
        picked = jnp.where(k == 1, block1, block0)
        out_ref[t] = jnp.where(k >= 0, picked, jnp.zeros_like(picked))


def outgoing_of(features, source_blocks, place):
    rows, width = features.shape
    return pl.pallas_call(
        outgoing_kernel,
        in_specs=[smem(), smem(), vmem()],
        out_specs=vmem(),
        out_shape=jax.ShapeDtypeStruct((source_blocks.shape[0], 192, BLK), BF16),
        scratch_shapes=[pltpu.VMEM((width, rows), BF16)],
        compiler_params=params(),
        name="outgoing",
    )(place, source_blocks, features)


def relation_of(i, place):
    core, y = place[2], place[3]
    parity = jnp.where(i < 4, core, 1 - core)
    return 2 * ((y - i) & 3) + parity


def slots_at(i, place, q):
    core = place[2]
    parity = jnp.where(i < 4, core, 1 - core)
    return (((i & 3) * 2 + parity) * 2 + q) * 8


def forward_kernel(
    place_ref, slot_ref, adj_ref, fetched_ref, w_mine_ref, w_theirs_ref, messages_ref, pre_ref, acc_ref
):
    i = pl.program_id(0)
    slots = 8
    for q in range(2):
        base = slots_at(i, place_ref, q)
        wide = jnp.concatenate([fetched_ref[slot_ref[base + s]] for s in range(slots)], axis=1)
        part = adj_ref[0, q * BLK : (q + 1) * BLK, :]
        messages_ref[0, :, q * BLK : (q + 1) * BLK] = dot(wide, part, 1, 1).astype(BF16)

    @pl.when(i == 0)
    def _():
        acc_ref[...] = dot(w_mine_ref[0], messages_ref[0], 0, 0)

    @pl.when((i > 0) & (i < 4))
    def _():
        acc_ref[...] += dot(w_mine_ref[0], messages_ref[0], 0, 0)

    @pl.when(i >= 4)
    def _():
        acc_ref[...] += dot(w_theirs_ref[0], messages_ref[0], 0, 0)

    @pl.when(i == 7)
    def _():
        pre_ref[...] = acc_ref[...].astype(BF16)


def forward_of(place, slots, adjacency, fetched, w_mine, w_theirs):
    rels, rows, wide = adjacency.shape
    width = w_mine.shape[2]
    spec = pltpu.PrefetchScalarGridSpec(
        num_scalar_prefetch=2,
        grid=(rels,),
        in_specs=[
            pl.BlockSpec((1, rows, wide), lambda i, p, s: (relation_of(i, p), 0, 0)),
            pl.BlockSpec(fetched.shape, lambda i, p, s: (0, 0, 0)),
            pl.BlockSpec((1, 192, width), lambda i, p, s: (jnp.minimum(i, 3), 0, 0)),
            pl.BlockSpec((1, 192, width), lambda i, p, s: (jnp.maximum(i - 4, 0), 0, 0)),
        ],
        out_specs=[
            pl.BlockSpec((1, 192, rows), lambda i, p, s: (relation_of(i, p), 0, 0)),
            pl.BlockSpec((width, rows), lambda i, p, s: (0, 0)),
        ],
        scratch_shapes=[pltpu.VMEM((width, rows), F32)],
    )
    return pl.pallas_call(
        forward_kernel,
        grid_spec=spec,
        out_shape=[
            jax.ShapeDtypeStruct((rels, 192, rows), BF16),
            jax.ShapeDtypeStruct((width, rows), BF16),
        ],
        compiler_params=params("arbitrary"),
        name="forward",
    )(place, slots, adjacency, fetched, w_mine, w_theirs)


def activation_kernel(arrived_ref, bias_ref, cotangent_ref, act_ref, grad_ref):
    pre = bias_ref[...]
    for g in range(arrived_ref.shape[0]):
        pre = pre + arrived_ref[g].astype(F32)
    sigmoid = jax.nn.sigmoid(pre)
    act_ref[...] = (pre * sigmoid).astype(BF16)
    derivative = sigmoid * (1.0 + pre * (1.0 - sigmoid))
    grad = (cotangent_ref[...].astype(F32) * derivative).astype(BF16)
    for g in range(grad_ref.shape[0]):
        grad_ref[g] = grad


def activation_of(arrived, bias, cotangent):
    return pl.pallas_call(
        activation_kernel,
        in_specs=[vmem()] * 3,
        out_specs=[vmem()] * 2,
        out_shape=[
            jax.ShapeDtypeStruct(arrived.shape[1:], BF16),
            jax.ShapeDtypeStruct(arrived.shape, BF16),
        ],
        compiler_params=params(),
        name="activation",
    )(arrived, bias, cotangent)


def backward_kernel(
    place_ref, slot_ref, adj_ref, grad_ref, w_mine_ref, w_theirs_ref, out_ref, acc_ref
):
    i = pl.program_id(0)
    slots = 8

    @pl.when(i == 0)
    def _():
        acc_ref[...] = jnp.zeros_like(acc_ref)

    def spread(w):
        grads = dot(w, grad_ref[...], 1, 0).astype(BF16)
        for q in range(2):
            base = slots_at(i, place_ref, q)
            part = adj_ref[0, q * BLK : (q + 1) * BLK, :]
            wide = dot(grads[:, q * BLK : (q + 1) * BLK], part, 1, 0)
            for s in range(slots):
                acc_ref[slot_ref[base + s]] += wide[:, s * BLK : (s + 1) * BLK]

    @pl.when(i < 4)
    def _():
        spread(w_mine_ref[0])

    @pl.when(i >= 4)
    def _():
        spread(w_theirs_ref[0])

    @pl.when(i == 7)
    def _():
        out_ref[...] = acc_ref[...].astype(BF16)


def backward_of(place, slots, adjacency, grads, w_mine, w_theirs, owners):
    rels, rows, wide = adjacency.shape
    width = w_mine.shape[2]
    spec = pltpu.PrefetchScalarGridSpec(
        num_scalar_prefetch=2,
        grid=(rels,),
        in_specs=[
            pl.BlockSpec((1, rows, wide), lambda i, p, s: (relation_of(i, p), 0, 0)),
            pl.BlockSpec((width, rows), lambda i, p, s: (0, 0)),
            pl.BlockSpec((1, 192, width), lambda i, p, s: (jnp.minimum(i, 3), 0, 0)),
            pl.BlockSpec((1, 192, width), lambda i, p, s: (jnp.maximum(i - 4, 0), 0, 0)),
        ],
        out_specs=pl.BlockSpec((owners, 192, BLK), lambda i, p, s: (0, 0, 0)),
        scratch_shapes=[pltpu.VMEM((owners, 192, BLK), F32)],
    )
    return pl.pallas_call(
        backward_kernel,
        grid_spec=spec,
        out_shape=jax.ShapeDtypeStruct((owners, 192, BLK), BF16),
        compiler_params=params("arbitrary"),
        name="backward",
    )(place, slots, adjacency, grads, w_mine, w_theirs)


def weight_kernel(place_ref, messages_ref, grad_ref, keep_ref, send_ref):
    core = place_ref[2]
    first = dot(messages_ref[0], grad_ref[...], 1, 1)
    second = dot(messages_ref[1], grad_ref[...], 1, 1)

    def cut(even_ref, odd_ref):
        for m in range(8):
            rows = slice(m * 24, (m + 1) * 24)
            piece = jnp.concatenate([first[rows], second[rows]], axis=0)
            target = odd_ref if m % 2 else even_ref
            target[0, m // 2] = piece.astype(target.dtype)

    @pl.when(core == 0)
    def _():
        cut(keep_ref, send_ref)

    @pl.when(core == 1)
    def _():
        cut(send_ref, keep_ref)


def weight_terms_of(place, messages, grads):
    rels, deep, rows = messages.shape
    width = grads.shape[0]
    out = pl.BlockSpec((1, 4, 48, width), lambda j: (j, 0, 0, 0))
    return pl.pallas_call(
        weight_kernel,
        grid=(rels // 2,),
        in_specs=[
            smem(),
            pl.BlockSpec((2, deep, rows), lambda j: (j, 0, 0)),
            pl.BlockSpec((width, rows), lambda j: (0, 0)),
        ],
        out_specs=[out, out],
        out_shape=[
            jax.ShapeDtypeStruct((rels // 2, 4, 48, width), F32),
            jax.ShapeDtypeStruct((rels // 2, 4, 48, width), BF16),
        ],
        compiler_params=params("arbitrary"),
        name="weight_terms",
    )(place, messages, grads)


def owned_kernel(place_ref, table_ref, arrived_ref, out_ref):
    owner = place_ref[0]
    zero = jnp.zeros(arrived_ref.shape[1:], F32)
    sums = [zero, zero]
    for t in range(arrived_ref.shape[0]):
        k = table_ref[t, owner]
        v = arrived_ref[t].astype(F32)
        for b in range(2):
            sums[b] = sums[b] + jnp.where(k == b, v, zero)
    for b in range(2):
        turned = sums[b].T
        for g in range(out_ref.shape[0]):
            out_ref[g, b] = turned[g * 16 : (g + 1) * 16, :]


def owned_of(place, source_blocks, arrived, groups):
    return pl.pallas_call(
        owned_kernel,
        in_specs=[smem(), smem(), vmem()],
        out_specs=vmem(),
        out_shape=jax.ShapeDtypeStruct((groups, 2, BLK // groups, arrived.shape[1]), F32),
        compiler_params=params(),
        name="owned",
    )(place, source_blocks, arrived)


def swap(value, axis):
    return lax.ppermute(value, axis, [(0, 1), (1, 0)])


def exchange(value, axis):
    return lax.all_to_all(value, axis, 0, 0, tiled=True)


def around(values, axis, size):
    return [
        lax.ppermute(v, axis, [(i, (i + k) % size) for i in range(size)])
        for k, v in enumerate(values, 1)
    ]


def to_owner():
    def place(y, xh, z, c):
        return ((y * 2 + xh) * 8 + z) * 2 + c
    moves = []
    for y in range(4):
        for xh in range(2):
            for z in range(8):
                for c in range(2):
                    target = place(2 * xh + z // 4, y // 2, 4 * (y % 2) + z % 4, c)
                    moves.append((place(y, xh, z, c), target))
    return moves


def per_device(
    features, weights, bias, cotangent, tile_values, tile_count, tile_slot, source_blocks
):
    groups = 8
    owners = source_blocks.shape[0]
    width = features.shape[1]
    xl, y, core = lax.axis_index("xl"), lax.axis_index("y"), lax.axis_index("core")
    owner = lax.axis_index(TGT)
    group = lax.axis_index(REL)
    place = jnp.stack([owner, 192 * y, core, y]).astype(jnp.int32)

    own_adjacency = adjacency_of(tile_values, tile_count)
    adjacency = lax.all_gather(own_adjacency, "y", axis=0, tiled=True)
    fetched = exchange(outgoing_of(features, source_blocks, place), TGT)
    w_cut = [
        lax.dynamic_slice(weights, (core, ((y + k) & 3) * 192, 0), (1, 192, width))
        for k in range(4)
    ]
    w_mine = jnp.concatenate([w_cut[0], *around(w_cut[1:], "y", 4)], axis=0)
    w_theirs = swap(w_mine, "core")
    own_slots = tile_slot.reshape(-1)
    slots = jnp.concatenate([own_slots, *around([own_slots] * 3, "y", 4)])

    messages, part = forward_of(place, slots, adjacency, fetched, w_mine, w_theirs)
    share = width // groups
    arrived = exchange(part.reshape(groups, share, -1), REL)
    bias_share = lax.dynamic_slice_in_dim(bias, group * share, share)[:, None]
    cotangent_share = lax.dynamic_slice_in_dim(cotangent, group * share, share, 1).T
    activated, grad_copies = activation_of(arrived, bias_share, cotangent_share)
    output = activated.T
    grads = exchange(grad_copies, REL).reshape(width, -1)

    partial = backward_of(place, slots, adjacency, grads, w_mine, w_theirs, owners)
    returned = exchange(partial, TGT)
    cut = owned_of(place, source_blocks, returned, groups)
    columns = exchange(cut, REL).reshape(2, 4, 2, BLK // groups, 192).sum(axis=0)
    grad_features = columns.transpose(1, 2, 0, 3).reshape(2, BLK // groups, width)

    late_grads, _ = lax.optimization_barrier((grads, partial))
    keep, send = weight_terms_of(place, messages, late_grads)
    chip = (keep + swap(send, "core").astype(F32)).reshape(16, 48, width)
    piece = lax.psum_scatter(chip, ("xh", "z"), scatter_dimension=0, tiled=True)
    grad_weights = lax.ppermute(piece.reshape(2, 24, width), ("y", *TGT), to_owner())
    return (output, grad_weights, grad_features)


def solution(mesh):
    fine = Mesh(mesh.devices.reshape(2, 4, 2, 8, 2), (*REL, *TGT))
    placed = (
        P(TGT, None),
        P(REL, None, None),
        P(),
        P(TGT, None),
        P(REL, TGT, None, None),
        P(REL, TGT),
        P(REL, TGT, None),
        P(),
    )
    return jax.shard_map(
        per_device,
        mesh=fine,
        in_specs=placed,
        out_specs=(P(TGT, REL), P(REL, TGT, None), P(TGT, REL, None)),
        check_vma=False,
    )
```

```python
import functools

import jax
import jax.numpy as jnp
from jax import lax
from jax.experimental import pallas as pl
from jax.experimental.pallas import tpu as pltpu
from jax.sharding import Mesh, PartitionSpec as P

F32 = jnp.float32
BF16 = jnp.bfloat16
BLK = 128
REL = ("xl", "y")
TGT = ("xh", "z", "core")
VMEM_LIMIT = 60 * 1024 * 1024


def params(*semantics):
    return pltpu.CompilerParams(
        dimension_semantics=semantics or None, vmem_limit_bytes=VMEM_LIMIT
    )


def smem():
    return pl.BlockSpec(memory_space=pltpu.MemorySpace.SMEM)


def vmem():
    return pl.BlockSpec(memory_space=pltpu.MemorySpace.VMEM)


def dot(a, b, ca, cb):
    return lax.dot_general(a, b, (((ca,), (cb,)), ((), ())), preferred_element_type=F32)


def adjacency_kernel(count_ref, values_ref, out_ref, *, relation):
    count = count_ref[relation, pl.program_id(0)]
    slots = values_ref.shape[2]
    live, degree = [], None
    for s in range(slots):
        v = values_ref[0, :, s, :]
        v = jnp.where(s < count, v, jnp.zeros_like(v)).astype(F32)
        live.append(v)
        degree = v if degree is None else degree + v
    total = jnp.sum(degree, axis=1, keepdims=True)
    scale = 1.0 / jnp.sqrt(jnp.maximum(total, 1.0))
    for s in range(slots):
        out_ref[:, s * BLK : (s + 1) * BLK] = (live[s] * scale).astype(BF16)


def adjacency_of(tile_values, tile_count, relation):
    _, rows, slots, cols = tile_values.shape
    return pl.pallas_call(
        functools.partial(adjacency_kernel, relation=relation),
        grid=(rows // BLK,),
        in_specs=[smem(), pl.BlockSpec((1, BLK, slots, cols), lambda q: (relation, q, 0, 0))],
        out_specs=pl.BlockSpec((BLK, slots * cols), lambda q: (q, 0)),
        out_shape=jax.ShapeDtypeStruct((rows, slots * cols), BF16),
        compiler_params=params("arbitrary"),
        name="adjacency",
    )(tile_count, tile_values)


def outgoing_kernel(place_ref, table_ref, features_ref, out_ref, turned_ref):
    owner, first = place_ref[0], place_ref[1]
    turned_ref[...] = features_ref[...].T
    piece = turned_ref[pl.ds(pl.multiple_of(first, 64), 192), :]
    block0, block1 = piece[:, :BLK], piece[:, BLK:]
    for t in range(out_ref.shape[0]):
        k = table_ref[t, owner]
        picked = jnp.where(k == 1, block1, block0)
        out_ref[t] = jnp.where(k >= 0, picked, jnp.zeros_like(picked))


def outgoing_of(features, source_blocks, place):
    rows, width = features.shape
    return pl.pallas_call(
        outgoing_kernel,
        in_specs=[smem(), smem(), vmem()],
        out_specs=vmem(),
        out_shape=jax.ShapeDtypeStruct((source_blocks.shape[0], 192, BLK), BF16),
        scratch_shapes=[pltpu.VMEM((width, rows), BF16)],
        compiler_params=params(),
        name="outgoing",
    )(place, source_blocks, features)


def start_loads(place_ref, steps, adj_refs, adj_buf, w_mine_ref, w_theirs_ref, w_buf, sems):
    core = place_ref[2]
    loads = []
    ks = sorted({k for k, _ in steps}, key=[k for k, _ in steps].index)
    for n, k in enumerate(ks):
        for half, ref in ((core, w_mine_ref), (1 - core, w_theirs_ref)):
            loads.append(pltpu.make_async_copy(ref.at[k], w_buf.at[2 * n + half], sems.at[len(loads)]))
        for p in range(2):
            at = steps.index((k, p))
            loads.append(pltpu.make_async_copy(adj_refs[at], adj_buf.at[at], sems.at[len(loads)]))
    for load in loads:
        load.start()
    return [loads[4 * n : 4 * n + 4] for n in range(len(ks))]


def forward_kernel(place_ref, slot_ref, *refs, steps, first, last):
    count = len(steps)
    adj_refs, refs = refs[:count], refs[count:]
    fetched_ref, w_mine_ref, w_theirs_ref, *refs = refs
    if not first:
        before_ref, *refs = refs
    messages_ref, pre_ref, adj_buf, w_buf, acc_ref, sems = refs
    groups = start_loads(
        place_ref, steps, adj_refs, adj_buf, w_mine_ref, w_theirs_ref, w_buf, sems
    )
    for n, (k, p) in enumerate(steps):
        if p == 0:
            for load in groups[n // 2]:
                load.wait()
        for q in range(2):
            base = ((k * 2 + p) * 2 + q) * 8
            wide = jnp.concatenate([fetched_ref[slot_ref[base + s]] for s in range(8)], axis=1)
            part = adj_buf[n, q * BLK : (q + 1) * BLK, :]
            messages_ref[n, :, q * BLK : (q + 1) * BLK] = dot(wide, part, 1, 1).astype(BF16)
        if p == 1:
            deep = 2 * w_buf.shape[1]
            w = w_buf[n - 1 : n + 1].reshape(deep, w_buf.shape[2])
            term = dot(w, messages_ref[n - 1 : n + 1].reshape(deep, -1), 0, 0)
            if n == 1 and not first:
                term = term + before_ref[...]
            if n + 1 == count:
                total = term if n == 1 else acc_ref[...] + term
                pre_ref[...] = total.astype(pre_ref.dtype)
            elif n == 1:
                acc_ref[...] = term
            else:
                acc_ref[...] += term


def anywhere():
    return pl.BlockSpec(memory_space=pl.ANY)


def forward_of(place, slots, steps, adjacencies, fetched, w_mine, w_theirs, before, last):
    rows, wide = adjacencies[0].shape
    width = w_mine.shape[2]
    count = len(steps)
    extra = [] if before is None else [before]
    return pl.pallas_call(
        functools.partial(forward_kernel, steps=steps, first=before is None, last=last),
        in_specs=[smem(), smem()] + [anywhere()] * count + [vmem(), anywhere(), anywhere()] + [vmem()] * len(extra),
        out_specs=[vmem(), vmem()],
        out_shape=[
            jax.ShapeDtypeStruct((count, 192, rows), BF16),
            jax.ShapeDtypeStruct((width, rows), BF16 if last else F32),
        ],
        scratch_shapes=[
            pltpu.VMEM((count, rows, wide), BF16),
            pltpu.VMEM((count, 192, width), BF16),
            pltpu.VMEM((width, rows), F32),
            pltpu.SemaphoreType.DMA((2 * count,)),
        ],
        compiler_params=params(),
        name="forward",
    )(place, slots, *adjacencies, fetched, w_mine, w_theirs, *extra)


def activation_kernel(arrived_ref, bias_ref, cotangent_ref, act_ref, grad_ref):
    pre = bias_ref[...]
    for g in range(arrived_ref.shape[0]):
        pre = pre + arrived_ref[g].astype(F32)
    sigmoid = jax.nn.sigmoid(pre)
    act_ref[...] = (pre * sigmoid).astype(BF16)
    derivative = sigmoid * (1.0 + pre * (1.0 - sigmoid))
    grad = (cotangent_ref[...].astype(F32) * derivative).astype(BF16)
    for g in range(grad_ref.shape[0]):
        grad_ref[g] = grad


def activation_of(arrived, bias, cotangent):
    return pl.pallas_call(
        activation_kernel,
        in_specs=[vmem()] * 3,
        out_specs=[vmem()] * 2,
        out_shape=[
            jax.ShapeDtypeStruct(arrived.shape[1:], BF16),
            jax.ShapeDtypeStruct(arrived.shape, BF16),
        ],
        compiler_params=params(),
        name="activation",
    )(arrived, bias, cotangent)


def backward_kernel(place_ref, slot_ref, *refs, steps):
    count = len(steps)
    adj_refs, refs = refs[:count], refs[count:]
    grad_ref, w_mine_ref, w_theirs_ref, out_ref, adj_buf, w_buf, acc_ref, sems = refs
    groups = start_loads(
        place_ref, steps, adj_refs, adj_buf, w_mine_ref, w_theirs_ref, w_buf, sems
    )
    acc_ref[...] = jnp.zeros_like(acc_ref)
    for n, (k, p) in enumerate(steps):
        if p == 0:
            for load in groups[n // 2]:
                load.wait()
        grads = dot(w_buf[n], grad_ref[...], 1, 0).astype(BF16)
        for q in range(2):
            base = ((k * 2 + p) * 2 + q) * 8
            part = adj_buf[n, q * BLK : (q + 1) * BLK, :]
            wide = dot(grads[:, q * BLK : (q + 1) * BLK], part, 1, 0)
            for s in range(8):
                acc_ref[slot_ref[base + s]] += wide[:, s * BLK : (s + 1) * BLK]
    out_ref[...] = acc_ref[...].astype(BF16)


def backward_of(place, slots, steps, adjacencies, grads, w_mine, w_theirs, owners):
    rows, wide = adjacencies[0].shape
    width = w_mine.shape[2]
    count = len(steps)
    return pl.pallas_call(
        functools.partial(backward_kernel, steps=steps),
        in_specs=[smem(), smem()] + [anywhere()] * count + [vmem(), anywhere(), anywhere()],
        out_specs=vmem(),
        out_shape=jax.ShapeDtypeStruct((owners, 192, BLK), BF16),
        scratch_shapes=[
            pltpu.VMEM((count, rows, wide), BF16),
            pltpu.VMEM((count, 192, width), BF16),
            pltpu.VMEM((owners, 192, BLK), F32),
            pltpu.SemaphoreType.DMA((2 * count,)),
        ],
        compiler_params=params(),
        name="backward",
    )(place, slots, *adjacencies, grads, w_mine, w_theirs)


def weight_kernel(place_ref, early_ref, late_ref, grad_ref, keep_ref, send_ref):
    core = place_ref[2]

    def cut(first, second, even_ref, odd_ref):
        for m in range(8):
            rows = slice(m * 24, (m + 1) * 24)
            piece = jnp.concatenate([first[rows], second[rows]], axis=0)
            target = odd_ref if m % 2 else even_ref
            target[0, m // 2] = piece.astype(target.dtype)

    def terms(messages_ref):
        first = dot(messages_ref[0], grad_ref[...], 1, 1)
        second = dot(messages_ref[1], grad_ref[...], 1, 1)

        @pl.when(core == 0)
        def _():
            cut(first, second, keep_ref, send_ref)

        @pl.when(core == 1)
        def _():
            cut(first, second, send_ref, keep_ref)

    @pl.when(pl.program_id(0) < 3)
    def _():
        terms(early_ref)

    @pl.when(pl.program_id(0) == 3)
    def _():
        terms(late_ref)


def weight_terms_of(place, early, late, grads):
    _, deep, rows = early.shape
    width = grads.shape[0]
    out = pl.BlockSpec((1, 4, 48, width), lambda i, p: ((p[3] - (i ^ (i >> 1))) & 3, 0, 0, 0))
    spec = pltpu.PrefetchScalarGridSpec(
        num_scalar_prefetch=1,
        grid=(4,),
        in_specs=[
            pl.BlockSpec((2, deep, rows), lambda i, p: (jnp.minimum(i, 2), 0, 0)),
            pl.BlockSpec((2, deep, rows), lambda i, p: (0, 0, 0)),
            pl.BlockSpec((width, rows), lambda i, p: (0, 0)),
        ],
        out_specs=[out, out],
    )
    return pl.pallas_call(
        weight_kernel,
        grid_spec=spec,
        out_shape=[
            jax.ShapeDtypeStruct((4, 4, 48, width), F32),
            jax.ShapeDtypeStruct((4, 4, 48, width), BF16),
        ],
        compiler_params=params("arbitrary"),
        name="weight_terms",
    )(place, early, late, grads)


def halve_kernel(bit_ref, keep_ref, came_ref, next_ref, send_ref, *, stride):
    bit = bit_ref[0]
    for i in range(next_ref.shape[0]):
        low = (i // stride) * 2 * stride + i % stride
        mine = low + bit * stride
        other = low + (1 - bit) * stride
        send_ref[i] = (keep_ref[other] + came_ref[other].astype(F32)).astype(BF16)
        next_ref[i] = keep_ref[mine] + came_ref[mine].astype(F32)


def halve(bit, keep, came, stride):
    shape = (keep.shape[0] // 2, *keep.shape[1:])
    return pl.pallas_call(
        functools.partial(halve_kernel, stride=stride),
        in_specs=[smem(), vmem(), vmem()],
        out_specs=[vmem(), vmem()],
        out_shape=[jax.ShapeDtypeStruct(shape, F32), jax.ShapeDtypeStruct(shape, BF16)],
        compiler_params=params(),
        name="halve",
    )(bit.astype(jnp.int32).reshape(1), keep, came)


def owned_kernel(place_ref, table_ref, arrived_ref, out_ref):
    owner = place_ref[0]
    zero = jnp.zeros(arrived_ref.shape[1:], F32)
    sums = [zero, zero]
    for t in range(arrived_ref.shape[0]):
        k = table_ref[t, owner]
        v = arrived_ref[t].astype(F32)
        for b in range(2):
            sums[b] = sums[b] + jnp.where(k == b, v, zero)
    for b in range(2):
        turned = sums[b].T
        for g in range(out_ref.shape[0]):
            out_ref[g, b] = turned[g * 16 : (g + 1) * 16, :]


def owned_of(place, source_blocks, arrived, groups):
    return pl.pallas_call(
        owned_kernel,
        in_specs=[smem(), smem(), vmem()],
        out_specs=vmem(),
        out_shape=jax.ShapeDtypeStruct((groups, 2, BLK // groups, arrived.shape[1]), F32),
        compiler_params=params(),
        name="owned",
    )(place, source_blocks, arrived)


def swap(value, axis, size=2, flip=1):
    return lax.ppermute(value, axis, [(i, i ^ flip) for i in range(size)])


def pass_on(value, axis, size, by):
    return lax.ppermute(value, axis, [(i, (i + by) % size) for i in range(size)])


def exchange(value, axis):
    return lax.all_to_all(value, axis, 0, 0, tiled=True)


def around(values, axis, size):
    return [
        lax.ppermute(v, axis, [(i, (i + k) % size) for i in range(size)])
        for k, v in enumerate(values, 1)
    ]


def to_owner():
    def place(y, xh, z, c):
        return ((y * 2 + xh) * 8 + z) * 2 + c
    moves = []
    for y in range(4):
        for xh in range(2):
            for z in range(8):
                for c in range(2):
                    target = place(2 * xh + z // 4, y // 2, 4 * (y % 2) + z % 4, c)
                    moves.append((place(y, xh, z, c), target))
    return moves


def per_device(
    features, weights, bias, cotangent, tile_values, tile_count, tile_slot, source_blocks
):
    groups = 8
    owners = source_blocks.shape[0]
    width = features.shape[1]
    xl, y, core = lax.axis_index("xl"), lax.axis_index("y"), lax.axis_index("core")
    owner = lax.axis_index(TGT)
    group = lax.axis_index(REL)
    place = jnp.stack([owner, 192 * y, core, y]).astype(jnp.int32)

    xh, z = lax.axis_index("xh"), lax.axis_index("z")
    own0 = adjacency_of(tile_values, tile_count, 0)
    own1 = adjacency_of(tile_values, tile_count, 1)
    features, own0, own1 = lax.optimization_barrier((features, own0, own1))
    back0, fore1 = pass_on(own0, "y", 4, 1), pass_on(own1, "y", 4, 3)
    back1, fore0 = pass_on(own1, "y", 4, 1), pass_on(own0, "y", 4, 3)
    fetched = exchange(outgoing_of(features, source_blocks, place), TGT)
    w_cut = [
        lax.dynamic_slice(weights, (core, ((y + k) & 3) * 192 + 96 * xh, 0), (1, 96, width))
        for k in range(4)
    ]
    w_part = jnp.concatenate([w_cut[0], *around(w_cut[1:], "y", 4)], axis=0)
    w_part, back0, fore1 = lax.optimization_barrier((w_part, back0, fore1))
    far0, far1 = pass_on(back0, "y", 4, 1), pass_on(fore1, "y", 4, 3)
    w_other = swap(w_part, "xh")
    w_mine = jnp.concatenate(
        [jnp.where(xh == 0, w_part, w_other), jnp.where(xh == 0, w_other, w_part)], axis=1
    )
    w_mine, back1, fore0 = lax.optimization_barrier((w_mine, back1, fore0))
    w_theirs = swap(w_mine, "core")
    own_slots = tile_slot.reshape(-1)
    slots = jnp.concatenate([own_slots, *around([own_slots] * 3, "y", 4)])

    near = ((0, 0), (0, 1), (1, 0), (1, 1), (3, 0), (3, 1))
    far = ((2, 0), (2, 1))
    adjacencies = (own0, own1, back0, back1, fore0, fore1, far0, far1)
    early, partway = forward_of(
        place, slots, near, adjacencies[:6], fetched, w_mine, w_theirs, None, False
    )
    late, part = forward_of(
        place, slots, far, adjacencies[6:], fetched, w_mine, w_theirs, partway, True
    )
    share = width // groups
    arrived = exchange(part.reshape(groups, share, -1), REL)
    bias_share = lax.dynamic_slice_in_dim(bias, group * share, share)[:, None]
    cotangent_share = lax.dynamic_slice_in_dim(cotangent, group * share, share, 1).T
    activated, grad_copies = activation_of(arrived, bias_share, cotangent_share)
    output = activated.T
    grads = exchange(grad_copies, REL).reshape(width, -1)

    partial = backward_of(
        place, slots, near + far, adjacencies, grads, w_mine, w_theirs, owners
    )
    returned = exchange(partial, TGT)
    cut = owned_of(place, source_blocks, returned, groups)
    columns = exchange(cut, REL).reshape(2, 4, 2, BLK // groups, 192).sum(axis=0)
    grad_features = columns.transpose(1, 2, 0, 3).reshape(2, BLK // groups, width)

    late_grads, _ = lax.optimization_barrier((grads, partial))
    keep, send = weight_terms_of(place, early, late, late_grads)
    keep, came = keep.reshape(16, 48, width), swap(send, "core").reshape(16, 48, width)
    keep, send = halve(xh, keep, came, 8)
    keep, send = halve(z & 1, keep, swap(send, "xh"), 1)
    keep, send = halve((z >> 1) & 1, keep, swap(send, "z", 8, 1), 1)
    keep, send = halve(z >> 2, keep, swap(send, "z", 8, 2), 1)
    piece = keep + swap(send, "z", 8, 4).astype(F32)
    grad_weights = lax.ppermute(piece.reshape(2, 24, width), ("y", *TGT), to_owner())
    return (output, grad_weights, grad_features)


def solution(mesh):
    fine = Mesh(mesh.devices.reshape(2, 4, 2, 8, 2), (*REL, *TGT))
    placed = (
        P(TGT, None),
        P(REL, None, None),
        P(),
        P(TGT, None),
        P(REL, TGT, None, None),
        P(REL, TGT),
        P(REL, TGT, None),
        P(),
    )
    return jax.shard_map(
        per_device,
        mesh=fine,
        in_specs=placed,
        out_specs=(P(TGT, REL), P(REL, TGT, None), P(TGT, REL, None)),
        check_vma=False,
    )
```

```python
import functools

import jax
import jax.numpy as jnp
from jax import lax
from jax.experimental import pallas as pl
from jax.experimental.pallas import tpu as pltpu
from jax.sharding import Mesh, PartitionSpec as P

F32 = jnp.float32
BF16 = jnp.bfloat16
BLK = 128
REL = ("xl", "y")
TGT = ("xh", "z", "core")
VMEM_LIMIT = 36 * 1024 * 1024


def resident(value):
    return pltpu.with_memory_space_constraint(value, pltpu.MemorySpace.VMEM)


def params(*semantics):
    return pltpu.CompilerParams(
        dimension_semantics=semantics or None, vmem_limit_bytes=VMEM_LIMIT
    )


def smem():
    return pl.BlockSpec(memory_space=pltpu.MemorySpace.SMEM)


def vmem():
    return pl.BlockSpec(memory_space=pltpu.MemorySpace.VMEM)


def dot(a, b, ca, cb):
    return lax.dot_general(a, b, (((ca,), (cb,)), ((), ())), preferred_element_type=F32)


def adjacency_kernel(count_ref, values_ref, out_ref):
    count = count_ref[pl.program_id(0), pl.program_id(1)]
    slots = values_ref.shape[2]
    live, degree = [], None
    for s in range(slots):
        v = values_ref[0, :, s, :]
        v = jnp.where(s < count, v, jnp.zeros_like(v)).astype(F32)
        live.append(v)
        degree = v if degree is None else degree + v
    total = jnp.sum(degree, axis=1, keepdims=True)
    scale = 1.0 / jnp.sqrt(jnp.maximum(total, 1.0))
    for s in range(slots):
        out_ref[0, :, s * BLK : (s + 1) * BLK] = (live[s] * scale).astype(BF16)


def adjacency_of(tile_values, tile_count):
    rels, rows, slots, cols = tile_values.shape
    return pl.pallas_call(
        adjacency_kernel,
        grid=(rels, rows // BLK),
        in_specs=[smem(), pl.BlockSpec((1, BLK, slots, cols), lambda r, q: (r, q, 0, 0))],
        out_specs=pl.BlockSpec((1, BLK, slots * cols), lambda r, q: (r, q, 0)),
        out_shape=jax.ShapeDtypeStruct((rels, rows, slots * cols), BF16),
        compiler_params=params("arbitrary", "arbitrary"),
        name="adjacency",
    )(tile_count, tile_values)


def outgoing_kernel(place_ref, table_ref, features_ref, out_ref, turned_ref):
    owner, first = place_ref[0], place_ref[1]
    turned_ref[...] = features_ref[...].T
    piece = turned_ref[pl.ds(pl.multiple_of(first, 64), 192), :]
    block0, block1 = piece[:, :BLK], piece[:, BLK:]
    for t in range(out_ref.shape[0]):
        k = table_ref[t, owner]
        picked = jnp.where(k == 1, block1, block0)
        out_ref[t] = jnp.where(k >= 0, picked, jnp.zeros_like(picked))


def outgoing_of(features, source_blocks, place):
    rows, width = features.shape
    return pl.pallas_call(
        outgoing_kernel,
        in_specs=[smem(), smem(), vmem()],
        out_specs=vmem(),
        out_shape=jax.ShapeDtypeStruct((source_blocks.shape[0], 192, BLK), BF16),
        scratch_shapes=[pltpu.VMEM((width, rows), BF16)],
        compiler_params=params(),
        name="outgoing",
    )(place, source_blocks, features)


STEPS = tuple((k, p) for k in range(4) for p in range(2))


def start_loads(place_ref, adj_ref, adj_buf, w_mine_ref, w_theirs_ref, w_buf, sems):
    core, y = place_ref[2], place_ref[3]
    loads = []
    for k in range(4):
        group = [
            pltpu.make_async_copy(
                adj_ref.at[pl.ds(2 * ((y - k) & 3), 2)], adj_buf.at[pl.ds(2 * k, 2)], sems.at[3 * k]
            )
        ]
        for n, (half, ref) in enumerate(((core, w_mine_ref), (1 - core, w_theirs_ref)), 1):
            group.append(pltpu.make_async_copy(ref.at[k], w_buf.at[2 * k + half], sems.at[3 * k + n]))
        for load in group:
            load.start()
        loads.append(group)
    return loads


def load_scratch(rows, wide, width):
    return [
        pltpu.VMEM((8, rows, wide), BF16),
        pltpu.VMEM((8, 192, width), BF16),
        pltpu.SemaphoreType.DMA((12,)),
    ]


def anywhere():
    return pl.BlockSpec(memory_space=pl.ANY)


def forward_kernel(
    place_ref, slot_ref, adj_ref, fetched_ref, w_mine_ref, w_theirs_ref,
    messages_ref, pre_ref, adj_buf, w_buf, sems, acc_ref,
):
    y = place_ref[3]
    loads = start_loads(place_ref, adj_ref, adj_buf, w_mine_ref, w_theirs_ref, w_buf, sems)
    for k in range(4):
        for load in loads[k]:
            load.wait()
        pair = pl.ds(2 * ((y - k) & 3), 2)
        both = []
        for p in range(2):
            halves = []
            for q in range(2):
                base = ((k * 2 + p) * 2 + q) * 8
                wide = jnp.concatenate([fetched_ref[slot_ref[base + s]] for s in range(8)], axis=1)
                part = adj_buf[2 * k + p, q * BLK : (q + 1) * BLK, :]
                halves.append(dot(wide, part, 1, 1).astype(BF16))
            both.append(jnp.concatenate(halves, axis=1))
        both = jnp.stack(both)
        messages_ref[pair] = both
        deep = 2 * w_buf.shape[1]
        term = dot(w_buf[2 * k : 2 * k + 2].reshape(deep, -1), both.reshape(deep, -1), 0, 0)
        if k == 0:
            acc_ref[...] = term
        elif k < 3:
            acc_ref[...] += term
        else:
            pre_ref[...] = (acc_ref[...] + term).astype(BF16)


def forward_of(place, slots, adjacency, fetched, w_mine, w_theirs):
    rels, rows, wide = adjacency.shape
    width = w_mine.shape[2]
    return pl.pallas_call(
        forward_kernel,
        in_specs=[smem(), smem(), anywhere(), vmem(), anywhere(), anywhere()],
        out_specs=[vmem(), vmem()],
        out_shape=[
            jax.ShapeDtypeStruct((rels, 192, rows), BF16),
            jax.ShapeDtypeStruct((width, rows), BF16),
        ],
        scratch_shapes=load_scratch(rows, wide, width) + [pltpu.VMEM((width, rows), F32)],
        compiler_params=params(),
        name="forward",
    )(place, slots, adjacency, fetched, w_mine, w_theirs)


def activation_kernel(arrived_ref, bias_ref, cotangent_ref, act_ref, grad_ref):
    pre = bias_ref[...]
    for g in range(arrived_ref.shape[0]):
        pre = pre + arrived_ref[g].astype(F32)
    sigmoid = jax.nn.sigmoid(pre)
    act_ref[...] = (pre * sigmoid).astype(BF16)
    derivative = sigmoid * (1.0 + pre * (1.0 - sigmoid))
    grad = (cotangent_ref[...].astype(F32) * derivative).astype(BF16)
    for g in range(grad_ref.shape[0]):
        grad_ref[g] = grad


def activation_of(arrived, bias, cotangent):
    return pl.pallas_call(
        activation_kernel,
        in_specs=[vmem()] * 3,
        out_specs=[vmem()] * 2,
        out_shape=[
            jax.ShapeDtypeStruct(arrived.shape[1:], BF16),
            jax.ShapeDtypeStruct(arrived.shape, BF16),
        ],
        compiler_params=params(),
        name="activation",
    )(arrived, bias, cotangent)


def backward_kernel(
    place_ref, slot_ref, adj_ref, grad_ref, w_mine_ref, w_theirs_ref, out_ref,
    adj_buf, w_buf, sems, acc_ref,
):
    loads = start_loads(place_ref, adj_ref, adj_buf, w_mine_ref, w_theirs_ref, w_buf, sems)
    acc_ref[...] = jnp.zeros_like(acc_ref)
    for n, (k, p) in enumerate(STEPS):
        if p == 0:
            for load in loads[k]:
                load.wait()
        grads = dot(w_buf[n], grad_ref[...], 1, 0).astype(BF16)
        for q in range(2):
            base = (n * 2 + q) * 8
            part = adj_buf[n, q * BLK : (q + 1) * BLK, :]
            wide = dot(grads[:, q * BLK : (q + 1) * BLK], part, 1, 0)
            for s in range(8):
                acc_ref[slot_ref[base + s]] += wide[:, s * BLK : (s + 1) * BLK]
    out_ref[...] = acc_ref[...].astype(BF16)


def backward_of(place, slots, adjacency, grads, w_mine, w_theirs, owners):
    rels, rows, wide = adjacency.shape
    width = w_mine.shape[2]
    return pl.pallas_call(
        backward_kernel,
        in_specs=[smem(), smem(), anywhere(), vmem(), anywhere(), anywhere()],
        out_specs=vmem(),
        out_shape=jax.ShapeDtypeStruct((owners, 192, BLK), BF16),
        scratch_shapes=load_scratch(rows, wide, width) + [pltpu.VMEM((owners, 192, BLK), F32)],
        compiler_params=params(),
        name="backward",
    )(place, slots, adjacency, grads, w_mine, w_theirs)


def weight_kernel(place_ref, messages_ref, grad_ref, keep_ref, send_ref):
    core = place_ref[2]
    first = dot(messages_ref[0], grad_ref[...], 1, 1)
    second = dot(messages_ref[1], grad_ref[...], 1, 1)

    def cut(even_ref, odd_ref):
        for m in range(8):
            rows = slice(m * 24, (m + 1) * 24)
            piece = jnp.concatenate([first[rows], second[rows]], axis=0)
            target = odd_ref if m % 2 else even_ref
            target[m // 2] = piece.astype(target.dtype)

    @pl.when(core == 0)
    def _():
        cut(keep_ref, send_ref)

    @pl.when(core == 1)
    def _():
        cut(send_ref, keep_ref)


def weight_terms_of(place, messages, grads):
    rels, deep, rows = messages.shape
    width = grads.shape[0]
    out = pl.BlockSpec((4, 48, width), lambda j: (j, 0, 0))
    return pl.pallas_call(
        weight_kernel,
        grid=(rels // 2,),
        in_specs=[
            smem(),
            pl.BlockSpec((2, deep, rows), lambda j: (j, 0, 0)),
            pl.BlockSpec((width, rows), lambda j: (0, 0)),
        ],
        out_specs=[out, out],
        out_shape=[
            jax.ShapeDtypeStruct((2 * rels, 48, width), F32),
            jax.ShapeDtypeStruct((2 * rels, 48, width), BF16),
        ],
        compiler_params=params("arbitrary"),
        name="weight_terms",
    )(place, messages, grads)


def owned_kernel(place_ref, table_ref, arrived_ref, out_ref):
    owner = place_ref[0]
    zero = jnp.zeros(arrived_ref.shape[1:], F32)
    sums = [zero, zero]
    for t in range(arrived_ref.shape[0]):
        k = table_ref[t, owner]
        v = arrived_ref[t].astype(F32)
        for b in range(2):
            sums[b] = sums[b] + jnp.where(k == b, v, zero)
    for b in range(2):
        turned = sums[b].T
        for g in range(out_ref.shape[0]):
            out_ref[g, b] = turned[g * 16 : (g + 1) * 16, :]


def owned_of(place, source_blocks, arrived, groups):
    return pl.pallas_call(
        owned_kernel,
        in_specs=[smem(), smem(), vmem()],
        out_specs=vmem(),
        out_shape=jax.ShapeDtypeStruct((groups, 2, BLK // groups, arrived.shape[1]), F32),
        compiler_params=params(),
        name="owned",
    )(place, source_blocks, arrived)


def halve(bit, keep, came, stride):
    shape = (-1, 2, stride, *keep.shape[1:])

    def take(which):
        total = [
            lax.dynamic_index_in_dim(v.reshape(shape), which, 1, keepdims=False).astype(F32)
            for v in (keep, came)
        ]
        return (total[0] + total[1]).reshape(-1, *keep.shape[1:])

    return take(bit), take(1 - bit).astype(BF16)


def swap(value, axis, size=2, flip=1):
    return lax.ppermute(value, axis, [(i, i ^ flip) for i in range(size)])


def exchange(value, axis):
    return lax.all_to_all(value, axis, 0, 0, tiled=True)


def around(values, axis, size):
    return [
        lax.ppermute(v, axis, [(i, (i + k) % size) for i in range(size)])
        for k, v in enumerate(values, 1)
    ]


def to_owner():
    def place(y, xh, z, c):
        return ((y * 2 + xh) * 8 + z) * 2 + c
    moves = []
    for y in range(4):
        for xh in range(2):
            for z in range(8):
                for c in range(2):
                    target = place(2 * xh + z // 4, y // 2, 4 * (y % 2) + z % 4, c)
                    moves.append((place(y, xh, z, c), target))
    return moves


def per_device(
    features, weights, bias, cotangent, tile_values, tile_count, tile_slot, source_blocks
):
    groups = 8
    owners = source_blocks.shape[0]
    width = features.shape[1]
    xl, y, core = lax.axis_index("xl"), lax.axis_index("y"), lax.axis_index("core")
    owner = lax.axis_index(TGT)
    group = lax.axis_index(REL)
    place = jnp.stack([owner, 192 * y, core, y]).astype(jnp.int32)

    xh, z = lax.axis_index("xh"), lax.axis_index("z")
    own_adjacency = adjacency_of(tile_values, tile_count)
    adjacency = lax.all_gather(own_adjacency, "y", axis=0, tiled=True)
    features, weights, _ = lax.optimization_barrier((features, weights, own_adjacency))
    fetched = resident(exchange(outgoing_of(features, source_blocks, place), TGT))
    w_cut = [
        lax.dynamic_slice(weights, (core, ((y + k) & 3) * 192 + 96 * xh, 0), (1, 96, width))
        for k in range(4)
    ]
    w_part = jnp.concatenate([w_cut[0], *around(w_cut[1:], "y", 4)], axis=0)
    w_other = swap(w_part, "xh")
    w_mine = jnp.concatenate(
        [jnp.where(xh == 0, w_part, w_other), jnp.where(xh == 0, w_other, w_part)], axis=1
    )
    w_theirs = swap(w_mine, "core")
    own_slots = tile_slot.reshape(-1)
    slots = jnp.concatenate([own_slots, *around([own_slots] * 3, "y", 4)])

    messages, part = forward_of(place, slots, adjacency, fetched, w_mine, w_theirs)
    share = width // groups
    arrived = resident(exchange(part.reshape(groups, share, -1), REL))
    bias_share = lax.dynamic_slice_in_dim(bias, group * share, share)[:, None]
    cotangent_share = lax.dynamic_slice_in_dim(cotangent, group * share, share, 1).T
    activated, grad_copies = activation_of(arrived, bias_share, cotangent_share)
    output = activated.T
    grads = exchange(grad_copies, REL).reshape(width, -1)

    partial = backward_of(place, slots, adjacency, grads, w_mine, w_theirs, owners)
    returned = resident(exchange(partial, TGT))
    cut = owned_of(place, source_blocks, returned, groups)
    columns = exchange(cut, REL).reshape(2, 4, 2, BLK // groups, 192).sum(axis=0)
    grad_features = columns.transpose(1, 2, 0, 3).reshape(2, BLK // groups, width)

    late_grads, _ = lax.optimization_barrier((grads, partial))
    keep, send = weight_terms_of(place, messages, late_grads)
    keep, send = halve(z & 1, keep, swap(send, "core"), 1)
    keep, send = halve(xh, keep, swap(send, "z", 8, 1), 4)
    keep, send = halve((z >> 1) & 1, keep, swap(send, "xh"), 1)
    keep, send = halve(z >> 2, keep, swap(send, "z", 8, 2), 1)
    piece = keep + swap(send, "z", 8, 4).astype(F32)
    grad_weights = lax.ppermute(piece.reshape(2, 24, width), ("y", *TGT), to_owner())
    return (output, grad_weights, grad_features)


def solution(mesh):
    fine = Mesh(mesh.devices.reshape(2, 4, 2, 8, 2), (*REL, *TGT))
    placed = (
        P(TGT, None),
        P(REL, None, None),
        P(),
        P(TGT, None),
        P(REL, TGT, None, None),
        P(REL, TGT),
        P(REL, TGT, None),
        P(),
    )
    return jax.shard_map(
        per_device,
        mesh=fine,
        in_specs=placed,
        out_specs=(P(TGT, REL), P(REL, TGT, None), P(TGT, REL, None)),
        check_vma=False,
    )
```

```python
import functools

import jax
import jax.numpy as jnp
from jax import lax
from jax.experimental import pallas as pl
from jax.experimental.pallas import tpu as pltpu
from jax.sharding import Mesh, PartitionSpec as P

F32 = jnp.float32
BF16 = jnp.bfloat16
BLK = 128
REL = ("xl", "y")
TGT = ("xh", "z", "core")
VMEM_LIMIT = 58 * 1024 * 1024


def in_hbm(value):
    return pltpu.with_memory_space_constraint(value, pltpu.MemorySpace.HBM)


def resident(value):
    return pltpu.with_memory_space_constraint(value, pltpu.MemorySpace.VMEM)


def params(*semantics):
    return pltpu.CompilerParams(
        dimension_semantics=semantics or None, vmem_limit_bytes=VMEM_LIMIT
    )


def smem():
    return pl.BlockSpec(memory_space=pltpu.MemorySpace.SMEM)


def vmem():
    return pl.BlockSpec(memory_space=pltpu.MemorySpace.VMEM)


def dot(a, b, ca, cb):
    return lax.dot_general(a, b, (((ca,), (cb,)), ((), ())), preferred_element_type=F32)


def adjacency_kernel(count_ref, values_ref, out_ref):
    count = count_ref[pl.program_id(0), pl.program_id(1)]
    slots = values_ref.shape[2]
    live, degree = [], None
    for s in range(slots):
        v = values_ref[0, :, s, :]
        v = jnp.where(s < count, v, jnp.zeros_like(v)).astype(F32)
        live.append(v)
        degree = v if degree is None else degree + v
    total = jnp.sum(degree, axis=1, keepdims=True)
    scale = 1.0 / jnp.sqrt(jnp.maximum(total, 1.0))
    for s in range(slots):
        out_ref[0, :, s * BLK : (s + 1) * BLK] = (live[s] * scale).astype(BF16)


def adjacency_of(tile_values, tile_count):
    rels, rows, slots, cols = tile_values.shape
    return pl.pallas_call(
        adjacency_kernel,
        grid=(rels, rows // BLK),
        in_specs=[smem(), pl.BlockSpec((1, BLK, slots, cols), lambda r, q: (r, q, 0, 0))],
        out_specs=pl.BlockSpec((1, BLK, slots * cols), lambda r, q: (r, q, 0)),
        out_shape=jax.ShapeDtypeStruct((rels, rows, slots * cols), BF16),
        compiler_params=params("arbitrary", "arbitrary"),
        name="adjacency",
    )(tile_count, tile_values)


def outgoing_kernel(place_ref, table_ref, features_ref, out_ref, turned_ref):
    owner, first = place_ref[0], place_ref[1]
    turned_ref[...] = features_ref[...].T
    piece = turned_ref[pl.ds(pl.multiple_of(first, 64), 192), :]
    block0, block1 = piece[:, :BLK], piece[:, BLK:]
    for t in range(out_ref.shape[0]):
        k = table_ref[t, owner]
        picked = jnp.where(k == 1, block1, block0)
        out_ref[t] = jnp.where(k >= 0, picked, jnp.zeros_like(picked))


def outgoing_of(features, source_blocks, place):
    rows, width = features.shape
    return pl.pallas_call(
        outgoing_kernel,
        in_specs=[smem(), smem(), vmem()],
        out_specs=vmem(),
        out_shape=jax.ShapeDtypeStruct((source_blocks.shape[0], 192, BLK), BF16),
        scratch_shapes=[pltpu.VMEM((width, rows), BF16)],
        compiler_params=params(),
        name="outgoing",
    )(place, source_blocks, features)


STEPS = tuple((k, p) for k in range(4) for p in range(2))


def start_loads(place_ref, adj_ref, adj_buf, w_mine_ref, w_theirs_ref, w_buf, sems):
    core, y = place_ref[2], place_ref[3]
    loads = []
    for k in range(4):
        group = [
            pltpu.make_async_copy(
                adj_ref.at[pl.ds(2 * ((y - k) & 3), 2)], adj_buf.at[pl.ds(2 * k, 2)], sems.at[3 * k]
            )
        ]
        for n, (half, ref) in enumerate(((core, w_mine_ref), (1 - core, w_theirs_ref)), 1):
            group.append(pltpu.make_async_copy(ref.at[k], w_buf.at[2 * k + half], sems.at[3 * k + n]))
        for load in group:
            load.start()
        loads.append(group)
    return loads


def load_scratch(rows, wide, width):
    return [
        pltpu.VMEM((8, rows, wide), BF16),
        pltpu.VMEM((8, 192, width), BF16),
        pltpu.SemaphoreType.DMA((12,)),
    ]


def hbm():
    return pl.BlockSpec(memory_space=pltpu.MemorySpace.HBM)


def anywhere():
    return pl.BlockSpec(memory_space=pl.ANY)


def forward_kernel(
    place_ref, slot_ref, adj_ref, fetched_ref, w_mine_ref, w_theirs_ref,
    keep_ref, send_ref, pre_ref, adj_buf, w_buf, sems, acc_ref,
):
    core, y = place_ref[2], place_ref[3]
    loads = start_loads(place_ref, adj_ref, adj_buf, w_mine_ref, w_theirs_ref, w_buf, sems)
    for k in range(4):
        for load in loads[k]:
            load.wait()
        pair = pl.ds(2 * ((y - k) & 3), 2)
        both = []
        for p in range(2):
            halves = []
            for q in range(2):
                base = ((k * 2 + p) * 2 + q) * 8
                wide = jnp.concatenate([fetched_ref[slot_ref[base + s]] for s in range(8)], axis=1)
                part = adj_buf[2 * k + p, q * BLK : (q + 1) * BLK, :]
                halves.append(dot(wide, part, 1, 1).astype(BF16))
            both.append(jnp.concatenate(halves, axis=1))
        both = jnp.stack(both)

        @pl.when(core == 0)
        def _():
            keep_ref[pair] = both[:, :96]
            send_ref[pair] = both[:, 96:]

        @pl.when(core == 1)
        def _():
            keep_ref[pair] = both[:, 96:]
            send_ref[pair] = both[:, :96]

        deep = 2 * w_buf.shape[1]
        term = dot(w_buf[2 * k : 2 * k + 2].reshape(deep, -1), both.reshape(deep, -1), 0, 0)
        if k == 0:
            acc_ref[...] = term
        elif k < 3:
            acc_ref[...] += term
        else:
            pre_ref[...] = (acc_ref[...] + term).astype(BF16)


def forward_of(place, slots, adjacency, fetched, w_mine, w_theirs):
    rels, rows, wide = adjacency.shape
    width = w_mine.shape[2]
    return pl.pallas_call(
        forward_kernel,
        in_specs=[smem(), smem(), hbm(), vmem(), anywhere(), anywhere()],
        out_specs=[vmem()] * 3,
        out_shape=[
            jax.ShapeDtypeStruct((rels, 96, rows), BF16),
            jax.ShapeDtypeStruct((rels, 96, rows), BF16),
            jax.ShapeDtypeStruct((width, rows), BF16),
        ],
        scratch_shapes=load_scratch(rows, wide, width) + [pltpu.VMEM((width, rows), F32)],
        compiler_params=params(),
        name="forward",
    )(place, slots, adjacency, fetched, w_mine, w_theirs)


def activation_kernel(arrived_ref, bias_ref, cotangent_ref, act_ref, grad_ref):
    pre = bias_ref[...]
    for g in range(arrived_ref.shape[0]):
        pre = pre + arrived_ref[g].astype(F32)
    sigmoid = jax.nn.sigmoid(pre)
    act_ref[...] = (pre * sigmoid).astype(BF16)
    derivative = sigmoid * (1.0 + pre * (1.0 - sigmoid))
    grad = (cotangent_ref[...].astype(F32) * derivative).astype(BF16)
    for g in range(grad_ref.shape[0]):
        grad_ref[g] = grad


def activation_of(arrived, bias, cotangent):
    return pl.pallas_call(
        activation_kernel,
        in_specs=[vmem()] * 3,
        out_specs=[vmem()] * 2,
        out_shape=[
            jax.ShapeDtypeStruct(arrived.shape[1:], BF16),
            jax.ShapeDtypeStruct(arrived.shape, BF16),
        ],
        compiler_params=params(),
        name="activation",
    )(arrived, bias, cotangent)


def backward_kernel(
    place_ref, slot_ref, adj_ref, grad_ref, w_mine_ref, w_theirs_ref, out_ref,
    adj_buf, w_buf, sems, acc_ref,
):
    loads = start_loads(place_ref, adj_ref, adj_buf, w_mine_ref, w_theirs_ref, w_buf, sems)
    acc_ref[...] = jnp.zeros_like(acc_ref)
    for n, (k, p) in enumerate(STEPS):
        if p == 0:
            for load in loads[k]:
                load.wait()
        grads = dot(w_buf[n], grad_ref[...], 1, 0).astype(BF16)
        for q in range(2):
            base = (n * 2 + q) * 8
            part = adj_buf[n, q * BLK : (q + 1) * BLK, :]
            wide = dot(grads[:, q * BLK : (q + 1) * BLK], part, 1, 0)
            for s in range(8):
                acc_ref[slot_ref[base + s]] += wide[:, s * BLK : (s + 1) * BLK]
    out_ref[...] = acc_ref[...].astype(BF16)


def backward_of(place, slots, adjacency, grads, w_mine, w_theirs, owners):
    rels, rows, wide = adjacency.shape
    width = w_mine.shape[2]
    return pl.pallas_call(
        backward_kernel,
        in_specs=[smem(), smem(), hbm(), vmem(), anywhere(), anywhere()],
        out_specs=vmem(),
        out_shape=jax.ShapeDtypeStruct((owners, 192, BLK), BF16),
        scratch_shapes=load_scratch(rows, wide, width) + [pltpu.VMEM((owners, 192, BLK), F32)],
        compiler_params=params(),
        name="backward",
    )(place, slots, adjacency, grads, w_mine, w_theirs)


def weight_kernel(place_ref, mine_ref, theirs_ref, grad_ref, their_grad_ref, keep_ref, send_ref):
    xh = place_ref[4]
    grads = jnp.concatenate([grad_ref[...], their_grad_ref[...]], axis=1)
    for target, x in ((send_ref, 1 - xh), (keep_ref, xh)):
        for half in range(2):
            terms = []
            for p in range(2):
                r = 4 * x + 2 * half + p
                wide = jnp.concatenate([mine_ref[r], theirs_ref[r]], axis=1)
                terms.append(dot(wide, grads, 1, 1))
            for m in range(4):
                rows = slice(m * 24, (m + 1) * 24)
                piece = jnp.concatenate([terms[0][rows], terms[1][rows]], axis=0)
                target[4 * half + m] = piece.astype(target.dtype)


def weight_terms_of(place, mine, theirs, grads, their_grads):
    rels = mine.shape[0]
    width = grads.shape[0]
    return pl.pallas_call(
        weight_kernel,
        in_specs=[smem()] + [vmem()] * 4,
        out_specs=[vmem(), vmem()],
        out_shape=[
            jax.ShapeDtypeStruct((rels, 48, width), F32),
            jax.ShapeDtypeStruct((rels, 48, width), BF16),
        ],
        compiler_params=params(),
        name="weight_terms",
    )(place, mine, theirs, grads, their_grads)


def owned_kernel(place_ref, table_ref, arrived_ref, out_ref):
    owner = place_ref[0]
    zero = jnp.zeros(arrived_ref.shape[1:], F32)
    sums = [zero, zero]
    for t in range(arrived_ref.shape[0]):
        k = table_ref[t, owner]
        v = arrived_ref[t].astype(F32)
        for b in range(2):
            sums[b] = sums[b] + jnp.where(k == b, v, zero)
    for b in range(2):
        turned = sums[b].T
        for g in range(out_ref.shape[0]):
            out_ref[g, b] = turned[g * 16 : (g + 1) * 16, :]


def owned_of(place, source_blocks, arrived, groups):
    return pl.pallas_call(
        owned_kernel,
        in_specs=[smem(), smem(), vmem()],
        out_specs=vmem(),
        out_shape=jax.ShapeDtypeStruct((groups, 2, BLK // groups, arrived.shape[1]), F32),
        compiler_params=params(),
        name="owned",
    )(place, source_blocks, arrived)


def halve(bit, keep, came, stride):
    shape = (-1, 2, stride, *keep.shape[1:])

    def take(which):
        total = [
            lax.dynamic_index_in_dim(v.reshape(shape), which, 1, keepdims=False).astype(F32)
            for v in (keep, came)
        ]
        return (total[0] + total[1]).reshape(-1, *keep.shape[1:])

    return take(bit), take(1 - bit).astype(BF16)


def swap(value, axis, size=2, flip=1):
    return lax.ppermute(value, axis, [(i, i ^ flip) for i in range(size)])


def exchange(value, axis):
    return lax.all_to_all(value, axis, 0, 0, tiled=True)


def around(values, axis, size):
    return [
        lax.ppermute(v, axis, [(i, (i + k) % size) for i in range(size)])
        for k, v in enumerate(values, 1)
    ]


def to_owner():
    def place(y, xh, z, c):
        return ((y * 2 + xh) * 8 + z) * 2 + c
    moves = []
    for y in range(4):
        for xh in range(2):
            for z in range(8):
                for c in range(2):
                    m = 4 * c + z % 4
                    target = place(2 * xh + z // 4, y // 2, 4 * (y % 2) + m // 2, m % 2)
                    moves.append((place(y, xh, z, c), target))
    return moves


def per_device(
    features, weights, bias, cotangent, tile_values, tile_count, tile_slot, source_blocks
):
    groups = 8
    owners = source_blocks.shape[0]
    width = features.shape[1]
    xl, y, core = lax.axis_index("xl"), lax.axis_index("y"), lax.axis_index("core")
    owner = lax.axis_index(TGT)
    group = lax.axis_index(REL)
    xh, z = lax.axis_index("xh"), lax.axis_index("z")
    place = jnp.stack([owner, 192 * y, core, y, xh]).astype(jnp.int32)

    w_cut = [
        lax.dynamic_slice(weights, (core, ((y + k) & 3) * 192 + 96 * xh, 0), (1, 96, width))
        for k in range(4)
    ]
    w_cut, tile_values = lax.optimization_barrier((w_cut, tile_values))
    w_came = around(w_cut[1:], "y", 4)
    own_slots = tile_slot.reshape(-1)
    slots = jnp.concatenate([own_slots, *around([own_slots] * 3, "y", 4)])
    own_adjacency = adjacency_of(tile_values, tile_count)
    adjacency = in_hbm(lax.all_gather(own_adjacency, "y", axis=0, tiled=True))
    features, _ = lax.optimization_barrier((features, own_adjacency))
    fetched = resident(exchange(outgoing_of(features, source_blocks, place), TGT))
    w_came, slots = lax.optimization_barrier((w_came, slots))
    w_part = jnp.concatenate([w_cut[0], *w_came], axis=0)
    w_other = swap(w_part, "xh")
    w_mine = jnp.concatenate(
        [jnp.where(xh == 0, w_part, w_other), jnp.where(xh == 0, w_other, w_part)], axis=1
    )
    w_theirs = swap(w_mine, "core")

    messages, for_partner, part = forward_of(place, slots, adjacency, fetched, w_mine, w_theirs)
    from_partner = swap(for_partner, "core")
    share = width // groups
    arrived = resident(exchange(part.reshape(groups, share, -1), REL))
    bias_share = lax.dynamic_slice_in_dim(bias, group * share, share)[:, None]
    cotangent_share = lax.dynamic_slice_in_dim(cotangent, group * share, share, 1).T
    activated, grad_copies = activation_of(arrived, bias_share, cotangent_share)
    output = activated.T
    grads = exchange(grad_copies, REL).reshape(width, -1)

    partial = backward_of(place, slots, adjacency, grads, w_mine, w_theirs, owners)
    returned = resident(exchange(in_hbm(partial), TGT))
    cut = owned_of(place, source_blocks, returned, groups)
    columns = exchange(cut, REL).reshape(2, 4, 2, BLK // groups, 192).sum(axis=0)
    grad_features = columns.transpose(1, 2, 0, 3).reshape(2, BLK // groups, width)

    their_grads, _ = lax.optimization_barrier((swap(grads, "core"), partial))
    keep, send = weight_terms_of(place, messages, from_partner, grads, their_grads)
    keep, send = halve(z & 1, keep, swap(send, "xh"), 1)
    keep, send = halve((z >> 1) & 1, keep, swap(send, "z", 8, 1), 1)
    keep, send = halve(z >> 2, keep, swap(send, "z", 8, 2), 1)
    piece = keep + swap(send, "z", 8, 4).astype(F32)
    grad_weights = lax.ppermute(piece.reshape(2, 24, width), ("y", *TGT), to_owner())
    return (output, grad_weights, grad_features)


def solution(mesh):
    fine = Mesh(mesh.devices.reshape(2, 4, 2, 8, 2), (*REL, *TGT))
    placed = (
        P(TGT, None),
        P(REL, None, None),
        P(),
        P(TGT, None),
        P(REL, TGT, None, None),
        P(REL, TGT),
        P(REL, TGT, None),
        P(),
    )
    return jax.shard_map(
        per_device,
        mesh=fine,
        in_specs=placed,
        out_specs=(P(TGT, REL), P(REL, TGT, None), P(TGT, REL, None)),
        check_vma=False,
    )
```

```python
import functools

import jax
import jax.numpy as jnp
from jax import lax
from jax.experimental import pallas as pl
from jax.experimental.pallas import tpu as pltpu
from jax.sharding import Mesh, PartitionSpec as P

F32 = jnp.float32
BF16 = jnp.bfloat16
BLK = 128
REL = ("xl", "y")
TGT = ("xh", "z", "core")
VMEM_LIMIT = 44 * 1024 * 1024


def in_hbm(value):
    return pltpu.with_memory_space_constraint(value, pltpu.MemorySpace.HBM)


def resident(value):
    return pltpu.with_memory_space_constraint(value, pltpu.MemorySpace.VMEM)


def params(*semantics):
    return pltpu.CompilerParams(
        dimension_semantics=semantics or None, vmem_limit_bytes=VMEM_LIMIT
    )


def smem():
    return pl.BlockSpec(memory_space=pltpu.MemorySpace.SMEM)


def vmem():
    return pl.BlockSpec(memory_space=pltpu.MemorySpace.VMEM)


def dot(a, b, ca, cb):
    return lax.dot_general(a, b, (((ca,), (cb,)), ((), ())), preferred_element_type=F32)


def adjacency_kernel(count_ref, values_ref, out_ref):
    count = count_ref[pl.program_id(0), pl.program_id(1)]
    slots = values_ref.shape[2]
    live, degree = [], None
    for s in range(slots):
        v = values_ref[0, :, s, :]
        v = jnp.where(s < count, v, jnp.zeros_like(v)).astype(F32)
        live.append(v)
        degree = v if degree is None else degree + v
    total = jnp.sum(degree, axis=1, keepdims=True)
    scale = 1.0 / jnp.sqrt(jnp.maximum(total, 1.0))
    for s in range(slots):
        out_ref[0, :, s * BLK : (s + 1) * BLK] = (live[s] * scale).astype(BF16)


def adjacency_of(tile_values, tile_count):
    rels, rows, slots, cols = tile_values.shape
    return pl.pallas_call(
        adjacency_kernel,
        grid=(rels, rows // BLK),
        in_specs=[smem(), pl.BlockSpec((1, BLK, slots, cols), lambda r, q: (r, q, 0, 0))],
        out_specs=pl.BlockSpec((1, BLK, slots * cols), lambda r, q: (r, q, 0)),
        out_shape=jax.ShapeDtypeStruct((rels, rows, slots * cols), BF16),
        compiler_params=params("arbitrary", "arbitrary"),
        name="adjacency",
    )(tile_count, tile_values)


def outgoing_kernel(place_ref, table_ref, features_ref, out_ref, turned_ref):
    owner, first = place_ref[0], place_ref[1]
    turned_ref[...] = features_ref[...].T
    piece = turned_ref[pl.ds(pl.multiple_of(first, 64), 192), :]
    block0, block1 = piece[:, :BLK], piece[:, BLK:]
    for t in range(out_ref.shape[0]):
        k = table_ref[t, owner]
        picked = jnp.where(k == 1, block1, block0)
        out_ref[t] = jnp.where(k >= 0, picked, jnp.zeros_like(picked))


def outgoing_of(features, source_blocks, place):
    rows, width = features.shape
    return pl.pallas_call(
        outgoing_kernel,
        in_specs=[smem(), smem(), vmem()],
        out_specs=vmem(),
        out_shape=jax.ShapeDtypeStruct((source_blocks.shape[0], 192, BLK), BF16),
        scratch_shapes=[pltpu.VMEM((width, rows), BF16)],
        compiler_params=params(),
        name="outgoing",
    )(place, source_blocks, features)


ORDER = (0, 1, 3, 2)


def start_loads(adj_refs, adj_buf, sems):
    own, back, fore, far0, far1 = adj_refs
    loads = []
    for n, ref in enumerate((own, back, fore)):
        loads.append([pltpu.make_async_copy(ref, adj_buf.at[pl.ds(2 * n, 2)], sems.at[n])])
    loads.append(
        [pltpu.make_async_copy(ref, adj_buf.at[pl.ds(6 + n, 1)], sems.at[3 + n]) for n, ref in enumerate((far0, far1))]
    )
    for group in loads:
        for load in group:
            load.start()
    return loads


def load_scratch(rows, wide):
    return [pltpu.VMEM((8, rows, wide), BF16), pltpu.SemaphoreType.DMA((5,))]


def hbm():
    return pl.BlockSpec(memory_space=pltpu.MemorySpace.HBM)


def forward_kernel(
    place_ref, slot_ref, own_ref, back_ref, fore_ref, far0_ref, far1_ref, fetched_ref, w_mine_ref, w_theirs_ref,
    keep_ref, send_ref, pre_ref, adj_buf, sems, both_ref, acc_ref,
):
    core, y = place_ref[2], place_ref[3]
    loads = start_loads((own_ref, back_ref, fore_ref, far0_ref, far1_ref), adj_buf, sems)
    for n, k in enumerate(ORDER):
        for load in loads[n]:
            load.wait()
        for p in range(2):
            for q in range(2):
                base = ((k * 2 + p) * 2 + q) * 8
                wide = jnp.concatenate([fetched_ref[slot_ref[base + s]] for s in range(8)], axis=1)
                part = adj_buf[2 * n + p, q * BLK : (q + 1) * BLK, :]
                both_ref[p, :, q * BLK : (q + 1) * BLK] = dot(wide, part, 1, 1).astype(BF16)
        pair = pl.ds(2 * ((y - k) & 3), 2)

        @pl.when(core == 0)
        def _():
            keep_ref[pair] = both_ref[:, :96]
            send_ref[pair] = both_ref[:, 96:]

        @pl.when(core == 1)
        def _():
            keep_ref[pair] = both_ref[:, 96:]
            send_ref[pair] = both_ref[:, :96]

        term = dot(w_mine_ref[k], both_ref[core], 0, 0) + dot(w_theirs_ref[k], both_ref[1 - core], 0, 0)
        if n == 0:
            acc_ref[...] = term
        elif n < 3:
            acc_ref[...] += term
        else:
            pre_ref[...] = (acc_ref[...] + term).astype(BF16)


def forward_of(place, slots, adjacency, fetched, w_mine, w_theirs):
    _, rows, wide = adjacency[0].shape
    width = w_mine.shape[2]
    half = jax.ShapeDtypeStruct((8, 96, rows), BF16)
    return pl.pallas_call(
        forward_kernel,
        in_specs=[smem(), smem()] + [hbm()] * 5 + [vmem()] * 3,
        out_specs=[vmem()] * 3,
        out_shape=[half, half, jax.ShapeDtypeStruct((width, rows), BF16)],
        scratch_shapes=load_scratch(rows, wide)
        + [pltpu.VMEM((2, 192, rows), BF16), pltpu.VMEM((width, rows), F32)],
        compiler_params=params(),
        name="forward",
    )(place, slots, *adjacency, fetched, w_mine, w_theirs)


def activation_kernel(arrived_ref, bias_ref, cotangent_ref, act_ref, grad_ref):
    pre = bias_ref[...]
    for g in range(arrived_ref.shape[0]):
        pre = pre + arrived_ref[g].astype(F32)
    sigmoid = jax.nn.sigmoid(pre)
    act_ref[...] = (pre * sigmoid).astype(BF16)
    derivative = sigmoid * (1.0 + pre * (1.0 - sigmoid))
    grad = (cotangent_ref[...].astype(F32) * derivative).astype(BF16)
    for g in range(grad_ref.shape[0]):
        grad_ref[g] = grad


def activation_of(arrived, bias, cotangent):
    return pl.pallas_call(
        activation_kernel,
        in_specs=[vmem()] * 3,
        out_specs=[vmem()] * 2,
        out_shape=[
            jax.ShapeDtypeStruct(arrived.shape[1:], BF16),
            jax.ShapeDtypeStruct(arrived.shape, BF16),
        ],
        compiler_params=params(),
        name="activation",
    )(arrived, bias, cotangent)


def backward_kernel(
    place_ref, slot_ref, own_ref, back_ref, fore_ref, far0_ref, far1_ref, grad_ref, w_mine_ref, w_theirs_ref,
    out_ref, adj_buf, sems, both_ref, acc_ref,
):
    core = place_ref[2]
    loads = start_loads((own_ref, back_ref, fore_ref, far0_ref, far1_ref), adj_buf, sems)
    acc_ref[...] = jnp.zeros_like(acc_ref)
    for n, k in enumerate(ORDER):
        both_ref[core] = dot(w_mine_ref[k], grad_ref[...], 1, 0).astype(BF16)
        both_ref[1 - core] = dot(w_theirs_ref[k], grad_ref[...], 1, 0).astype(BF16)
        for load in loads[n]:
            load.wait()
        for p in range(2):
            for q in range(2):
                base = ((k * 2 + p) * 2 + q) * 8
                part = adj_buf[2 * n + p, q * BLK : (q + 1) * BLK, :]
                wide = dot(both_ref[p, :, q * BLK : (q + 1) * BLK], part, 1, 0)
                for s in range(8):
                    acc_ref[slot_ref[base + s]] += wide[:, s * BLK : (s + 1) * BLK]
    out_ref[...] = acc_ref[...].astype(BF16)


def backward_of(place, slots, adjacency, grads, w_mine, w_theirs, owners):
    _, rows, wide = adjacency[0].shape
    return pl.pallas_call(
        backward_kernel,
        in_specs=[smem(), smem()] + [hbm()] * 5 + [vmem()] * 3,
        out_specs=vmem(),
        out_shape=jax.ShapeDtypeStruct((owners, 192, BLK), BF16),
        scratch_shapes=load_scratch(rows, wide)
        + [pltpu.VMEM((2, 192, rows), BF16), pltpu.VMEM((owners, 192, BLK), F32)],
        compiler_params=params(),
        name="backward",
    )(place, slots, *adjacency, grads, w_mine, w_theirs)


def weight_kernel(place_ref, mine_ref, theirs_ref, grad_ref, their_grad_ref, keep_ref, send_ref):
    xh = place_ref[4]
    grads = jnp.concatenate([grad_ref[...], their_grad_ref[...]], axis=1)
    for target, x in ((send_ref, 1 - xh), (keep_ref, xh)):
        for half in range(2):
            terms = []
            for p in range(2):
                r = 4 * x + 2 * half + p
                wide = jnp.concatenate([mine_ref[r], theirs_ref[r]], axis=1)
                terms.append(dot(wide, grads, 1, 1))
            for m in range(4):
                rows = slice(m * 24, (m + 1) * 24)
                piece = jnp.concatenate([terms[0][rows], terms[1][rows]], axis=0)
                target[4 * half + m] = piece.astype(target.dtype)


def weight_terms_of(place, mine, theirs, grads, their_grads):
    rels = mine.shape[0]
    width = grads.shape[0]
    return pl.pallas_call(
        weight_kernel,
        in_specs=[smem()] + [vmem()] * 4,
        out_specs=[vmem(), vmem()],
        out_shape=[
            jax.ShapeDtypeStruct((rels, 48, width), F32),
            jax.ShapeDtypeStruct((rels, 48, width), BF16),
        ],
        compiler_params=params(),
        name="weight_terms",
    )(place, mine, theirs, grads, their_grads)


def owned_kernel(place_ref, table_ref, arrived_ref, out_ref):
    owner = place_ref[0]
    zero = jnp.zeros(arrived_ref.shape[1:], F32)
    sums = [zero, zero]
    for t in range(arrived_ref.shape[0]):
        k = table_ref[t, owner]
        v = arrived_ref[t].astype(F32)
        for b in range(2):
            sums[b] = sums[b] + jnp.where(k == b, v, zero)
    for b in range(2):
        turned = sums[b].T
        for g in range(out_ref.shape[0]):
            out_ref[g, b] = turned[g * 16 : (g + 1) * 16, :]


def owned_of(place, source_blocks, arrived, groups):
    return pl.pallas_call(
        owned_kernel,
        in_specs=[smem(), smem(), vmem()],
        out_specs=vmem(),
        out_shape=jax.ShapeDtypeStruct((groups, 2, BLK // groups, arrived.shape[1]), F32),
        compiler_params=params(),
        name="owned",
    )(place, source_blocks, arrived)


def halve(bit, keep, came, stride):
    shape = (-1, 2, stride, *keep.shape[1:])

    def take(which):
        total = [
            lax.dynamic_index_in_dim(v.reshape(shape), which, 1, keepdims=False).astype(F32)
            for v in (keep, came)
        ]
        return (total[0] + total[1]).reshape(-1, *keep.shape[1:])

    return take(bit), take(1 - bit).astype(BF16)


def step(value, by):
    return lax.ppermute(value, "y", [(i, (i + by) % 4) for i in range(4)])


def swap(value, axis, size=2, flip=1):
    return lax.ppermute(value, axis, [(i, i ^ flip) for i in range(size)])


def exchange(value, axis):
    return lax.all_to_all(value, axis, 0, 0, tiled=True)


def around(values, axis, size):
    return [
        lax.ppermute(v, axis, [(i, (i + k) % size) for i in range(size)])
        for k, v in enumerate(values, 1)
    ]


def to_owner():
    def place(y, xh, z, c):
        return ((y * 2 + xh) * 8 + z) * 2 + c
    moves = []
    for y in range(4):
        for xh in range(2):
            for z in range(8):
                for c in range(2):
                    m = 4 * c + z % 4
                    target = place(2 * xh + z // 4, y // 2, 4 * (y % 2) + m // 2, m % 2)
                    moves.append((place(y, xh, z, c), target))
    return moves


def per_device(
    features, weights, bias, cotangent, tile_values, tile_count, tile_slot, source_blocks
):
    groups = 8
    owners = source_blocks.shape[0]
    width = features.shape[1]
    xl, y, core = lax.axis_index("xl"), lax.axis_index("y"), lax.axis_index("core")
    owner = lax.axis_index(TGT)
    group = lax.axis_index(REL)
    xh, z = lax.axis_index("xh"), lax.axis_index("z")
    xh, z = lax.axis_index("xh"), lax.axis_index("z")
    place = in_hbm(jnp.stack([owner, 192 * y, core, y, xh]).astype(jnp.int32))

    own = adjacency_of(in_hbm(tile_values), in_hbm(tile_count))
    back, fore = step(own, 1), step(own, -1)
    far0, far1 = step(back[:1], 1), step(fore[1:], -1)
    adjacency = [in_hbm(a) for a in (own, back, fore, far0, far1)]
    features, weights, _ = lax.optimization_barrier((features, weights, own))
    source_blocks = in_hbm(source_blocks)
    outgoing = outgoing_of(in_hbm(features), source_blocks, place)
    fetched = resident(exchange(outgoing, TGT))

    own_slots = jnp.pad(tile_slot.reshape(1, 1, -1), ((0, 0), (0, 15), (0, width - 32))).astype(BF16)
    pieces = []
    for k in range(4):
        cut = lax.dynamic_slice(weights, (core, ((y + k) & 3) * 192, 0), (1, 192, width))
        pieces.append(jnp.concatenate([cut, own_slots], axis=1) if k else cut)
    came = around(pieces[1:], "y", 4)
    slots = jnp.concatenate([tile_slot.reshape(-1)] + [c[0, 192, :32].astype(jnp.int32) for c in came])
    slots = in_hbm(slots)
    w_mine = jnp.concatenate([pieces[0]] + [c[:, :192] for c in came], axis=0)
    w_mine, w_theirs = resident(w_mine), resident(swap(w_mine, "core"))

    messages, for_partner, part = forward_of(place, slots, adjacency, fetched, w_mine, w_theirs)
    from_partner = swap(for_partner, "core")
    share = width // groups
    arrived = resident(exchange(part.reshape(groups, share, -1), REL))
    bias_share = lax.dynamic_slice_in_dim(bias, group * share, share)[:, None]
    cotangent_share = lax.dynamic_slice_in_dim(cotangent, group * share, share, 1).T
    activated, grad_copies = activation_of(arrived, bias_share, cotangent_share)
    output = activated.T
    grads = exchange(grad_copies, REL).reshape(width, -1)

    partial = backward_of(place, slots, adjacency, resident(grads), w_mine, w_theirs, owners)
    returned = resident(exchange(in_hbm(partial), TGT))
    cut = owned_of(place, source_blocks, returned, groups)
    columns = exchange(cut, REL).reshape(2, 4, 2, BLK // groups, 192).sum(axis=0)
    grad_features = columns.transpose(1, 2, 0, 3).reshape(2, BLK // groups, width)

    their_grads, _ = lax.optimization_barrier((swap(grads, "core"), partial))
    keep, send = weight_terms_of(place, messages, from_partner, grads, their_grads)
    keep, send = halve(z & 1, keep, swap(send, "xh"), 1)
    keep, send = halve((z >> 1) & 1, keep, swap(send, "z", 8, 1), 1)
    keep, send = halve(z >> 2, keep, swap(send, "z", 8, 2), 1)
    piece = keep + swap(send, "z", 8, 4).astype(F32)
    grad_weights = lax.ppermute(piece.reshape(2, 24, width), ("y", *TGT), to_owner())
    return (output, grad_weights, grad_features)


def solution(mesh):
    fine = Mesh(mesh.devices.reshape(2, 4, 2, 8, 2), (*REL, *TGT))
    placed = (
        P(TGT, None),
        P(REL, None, None),
        P(),
        P(TGT, None),
        P(REL, TGT, None, None),
        P(REL, TGT),
        P(REL, TGT, None),
        P(),
    )
    return jax.shard_map(
        per_device,
        mesh=fine,
        in_specs=placed,
        out_specs=(P(TGT, REL), P(REL, TGT, None), P(TGT, REL, None)),
        check_vma=False,
    )
```

```python
import functools

import jax
import jax.numpy as jnp
from jax import lax
from jax.experimental import pallas as pl
from jax.experimental.pallas import tpu as pltpu
from jax.sharding import Mesh, PartitionSpec as P

F32 = jnp.float32
BF16 = jnp.bfloat16
BLK = 128
REL = ("xl", "y")
TGT = ("xh", "z", "core")
VMEM_LIMIT = 44 * 1024 * 1024


def in_hbm(value):
    return pltpu.with_memory_space_constraint(value, pltpu.MemorySpace.HBM)


def resident(value):
    return pltpu.with_memory_space_constraint(value, pltpu.MemorySpace.VMEM)


def params(*semantics):
    return pltpu.CompilerParams(
        dimension_semantics=semantics or None, vmem_limit_bytes=VMEM_LIMIT
    )


def smem():
    return pl.BlockSpec(memory_space=pltpu.MemorySpace.SMEM)


def vmem():
    return pl.BlockSpec(memory_space=pltpu.MemorySpace.VMEM)


def dot(a, b, ca, cb):
    return lax.dot_general(a, b, (((ca,), (cb,)), ((), ())), preferred_element_type=F32)


def adjacency_kernel(count_ref, values_ref, out_ref):
    count = count_ref[pl.program_id(0), pl.program_id(1)]
    slots = values_ref.shape[2]
    live, degree = [], None
    for s in range(slots):
        v = values_ref[0, :, s, :]
        v = jnp.where(s < count, v, jnp.zeros_like(v)).astype(F32)
        live.append(v)
        degree = v if degree is None else degree + v
    total = jnp.sum(degree, axis=1, keepdims=True)
    scale = 1.0 / jnp.sqrt(jnp.maximum(total, 1.0))
    for s in range(slots):
        out_ref[0, :, s * BLK : (s + 1) * BLK] = (live[s] * scale).astype(BF16)


def adjacency_of(tile_values, tile_count):
    rels, rows, slots, cols = tile_values.shape
    return pl.pallas_call(
        adjacency_kernel,
        grid=(rels, rows // BLK),
        in_specs=[smem(), pl.BlockSpec((1, BLK, slots, cols), lambda r, q: (r, q, 0, 0))],
        out_specs=pl.BlockSpec((1, BLK, slots * cols), lambda r, q: (r, q, 0)),
        out_shape=jax.ShapeDtypeStruct((rels, rows, slots * cols), BF16),
        compiler_params=params("arbitrary", "arbitrary"),
        name="adjacency",
    )(tile_count, tile_values)


def outgoing_kernel(place_ref, table_ref, features_ref, out_ref, turned_ref):
    owner, first = place_ref[0], place_ref[1]
    turned_ref[...] = features_ref[...].T
    piece = turned_ref[pl.ds(pl.multiple_of(first, 64), 192), :]
    block0, block1 = piece[:, :BLK], piece[:, BLK:]
    for t in range(out_ref.shape[0]):
        k = table_ref[t, owner]
        picked = jnp.where(k == 1, block1, block0)
        out_ref[t] = jnp.where(k >= 0, picked, jnp.zeros_like(picked))


def outgoing_of(features, source_blocks, place):
    rows, width = features.shape
    return pl.pallas_call(
        outgoing_kernel,
        in_specs=[smem(), smem(), vmem()],
        out_specs=vmem(),
        out_shape=jax.ShapeDtypeStruct((source_blocks.shape[0], 192, BLK), BF16),
        scratch_shapes=[pltpu.VMEM((width, rows), BF16)],
        compiler_params=params(),
        name="outgoing",
    )(place, source_blocks, features)


ORDER = (0, 1, 3, 2)


def start_loads(adj_refs, adj_buf, sems):
    own, back, fore, far0, far1 = adj_refs
    loads = []
    for n, ref in enumerate((own, back, fore)):
        loads.append([pltpu.make_async_copy(ref, adj_buf.at[pl.ds(2 * n, 2)], sems.at[n])])
    loads.append(
        [pltpu.make_async_copy(ref, adj_buf.at[pl.ds(6 + n, 1)], sems.at[3 + n]) for n, ref in enumerate((far0, far1))]
    )
    for group in loads:
        for load in group:
            load.start()
    return loads


def load_scratch(rows, wide):
    return [pltpu.VMEM((8, rows, wide), BF16), pltpu.SemaphoreType.DMA((5,))]


def hbm():
    return pl.BlockSpec(memory_space=pltpu.MemorySpace.HBM)


def forward_kernel(
    place_ref, slot_ref, own_ref, back_ref, fore_ref, far0_ref, far1_ref, fetched_ref, w_mine_ref, w_theirs_ref,
    keep_ref, send_ref, pre_ref, adj_buf, sems, both_ref, acc_ref,
):
    core, y = place_ref[2], place_ref[3]
    loads = start_loads((own_ref, back_ref, fore_ref, far0_ref, far1_ref), adj_buf, sems)
    for n, k in enumerate(ORDER):
        for load in loads[n]:
            load.wait()
        for p in range(2):
            for q in range(2):
                base = ((k * 2 + p) * 2 + q) * 8
                wide = jnp.concatenate([fetched_ref[slot_ref[base + s]] for s in range(8)], axis=1)
                part = adj_buf[2 * n + p, q * BLK : (q + 1) * BLK, :]
                both_ref[p, :, q * BLK : (q + 1) * BLK] = dot(wide, part, 1, 1).astype(BF16)
        j = (y - k) & 3
        side, pair = (j >> 1) ^ place_ref[4], pl.ds(2 * (j & 1), 2)

        @pl.when(core == 0)
        def _():
            keep_ref[side, pair] = both_ref[:, :96]
            send_ref[side, pair] = both_ref[:, 96:]

        @pl.when(core == 1)
        def _():
            keep_ref[side, pair] = both_ref[:, 96:]
            send_ref[side, pair] = both_ref[:, :96]

        term = dot(w_mine_ref[k], both_ref[core], 0, 0) + dot(w_theirs_ref[k], both_ref[1 - core], 0, 0)
        if n == 0:
            acc_ref[...] = term
        elif n < 3:
            acc_ref[...] += term
        else:
            pre_ref[...] = (acc_ref[...] + term).astype(BF16)


def forward_of(place, slots, adjacency, fetched, w_mine, w_theirs):
    _, rows, wide = adjacency[0].shape
    width = w_mine.shape[2]
    half = jax.ShapeDtypeStruct((2, 4, 96, rows), BF16)
    return pl.pallas_call(
        forward_kernel,
        in_specs=[smem(), smem()] + [hbm()] * 5 + [vmem()] * 3,
        out_specs=[vmem()] * 3,
        out_shape=[half, half, jax.ShapeDtypeStruct((width, rows), BF16)],
        scratch_shapes=load_scratch(rows, wide)
        + [pltpu.VMEM((2, 192, rows), BF16), pltpu.VMEM((width, rows), F32)],
        compiler_params=params(),
        name="forward",
    )(place, slots, *adjacency, fetched, w_mine, w_theirs)


def activation_kernel(arrived_ref, bias_ref, cotangent_ref, act_ref, grad_ref):
    pre = bias_ref[...]
    for g in range(arrived_ref.shape[0]):
        pre = pre + arrived_ref[g].astype(F32)
    sigmoid = jax.nn.sigmoid(pre)
    act_ref[...] = (pre * sigmoid).astype(BF16)
    derivative = sigmoid * (1.0 + pre * (1.0 - sigmoid))
    grad = (cotangent_ref[...].astype(F32) * derivative).astype(BF16)
    for g in range(grad_ref.shape[0]):
        grad_ref[g] = grad


def activation_of(arrived, bias, cotangent):
    return pl.pallas_call(
        activation_kernel,
        in_specs=[vmem()] * 3,
        out_specs=[vmem()] * 2,
        out_shape=[
            jax.ShapeDtypeStruct(arrived.shape[1:], BF16),
            jax.ShapeDtypeStruct(arrived.shape, BF16),
        ],
        compiler_params=params(),
        name="activation",
    )(arrived, bias, cotangent)


def backward_kernel(
    place_ref, slot_ref, own_ref, back_ref, fore_ref, far0_ref, far1_ref, grad_ref, w_mine_ref, w_theirs_ref,
    out_ref, adj_buf, sems, both_ref, acc_ref,
):
    core = place_ref[2]
    loads = start_loads((own_ref, back_ref, fore_ref, far0_ref, far1_ref), adj_buf, sems)
    acc_ref[...] = jnp.zeros_like(acc_ref)
    for n, k in enumerate(ORDER):
        both_ref[core] = dot(w_mine_ref[k], grad_ref[...], 1, 0).astype(BF16)
        both_ref[1 - core] = dot(w_theirs_ref[k], grad_ref[...], 1, 0).astype(BF16)
        for load in loads[n]:
            load.wait()
        for p in range(2):
            for q in range(2):
                base = ((k * 2 + p) * 2 + q) * 8
                part = adj_buf[2 * n + p, q * BLK : (q + 1) * BLK, :]
                wide = dot(both_ref[p, :, q * BLK : (q + 1) * BLK], part, 1, 0)
                for s in range(8):
                    acc_ref[slot_ref[base + s]] += wide[:, s * BLK : (s + 1) * BLK]
    out_ref[...] = acc_ref[...].astype(BF16)


def backward_of(place, slots, adjacency, grads, w_mine, w_theirs, owners):
    _, rows, wide = adjacency[0].shape
    return pl.pallas_call(
        backward_kernel,
        in_specs=[smem(), smem()] + [hbm()] * 5 + [vmem()] * 3,
        out_specs=vmem(),
        out_shape=jax.ShapeDtypeStruct((owners, 192, BLK), BF16),
        scratch_shapes=load_scratch(rows, wide)
        + [pltpu.VMEM((2, 192, rows), BF16), pltpu.VMEM((owners, 192, BLK), F32)],
        compiler_params=params(),
        name="backward",
    )(place, slots, *adjacency, grads, w_mine, w_theirs)


def weight_kernel(
    place_ref, own_ref, core_ref, far_ref, grad_ref, core_grad_ref, far_grad_ref, far_core_grad_ref, keep_ref, send_ref
):
    bit = place_ref[5]
    grads = jnp.concatenate(
        [grad_ref[...], core_grad_ref[...], far_grad_ref[...], far_core_grad_ref[...]], axis=1
    )
    for half in range(2):
        terms = []
        for p in range(2):
            r = 2 * half + p
            wide = jnp.concatenate([own_ref[0, r], core_ref[0, r], far_ref[0, r], far_ref[1, r]], axis=1)
            terms.append(dot(wide, grads, 1, 1))

        def piece(m):
            rows = slice(m * 24, (m + 1) * 24)
            return jnp.concatenate([terms[0][rows], terms[1][rows]], axis=0)

        def cut(even_ref, odd_ref):
            for m in range(4):
                target = odd_ref if m % 2 else even_ref
                target[2 * half + m // 2] = piece(m).astype(target.dtype)

        @pl.when(bit == 0)
        def _():
            cut(keep_ref, send_ref)

        @pl.when(bit == 1)
        def _():
            cut(send_ref, keep_ref)


def weight_terms_of(place, *operands):
    width = operands[-1].shape[0]
    return pl.pallas_call(
        weight_kernel,
        in_specs=[smem()] + [vmem()] * 7,
        out_specs=[vmem(), vmem()],
        out_shape=[
            jax.ShapeDtypeStruct((4, 48, width), F32),
            jax.ShapeDtypeStruct((4, 48, width), BF16),
        ],
        compiler_params=params(),
        name="weight_terms",
    )(place, *operands)


def owned_kernel(place_ref, table_ref, arrived_ref, out_ref):
    owner = place_ref[0]
    zero = jnp.zeros(arrived_ref.shape[1:], F32)
    sums = [zero, zero]
    for t in range(arrived_ref.shape[0]):
        k = table_ref[t, owner]
        v = arrived_ref[t].astype(F32)
        for b in range(2):
            sums[b] = sums[b] + jnp.where(k == b, v, zero)
    for b in range(2):
        turned = sums[b].T
        for g in range(out_ref.shape[0]):
            out_ref[g, b] = turned[g * 16 : (g + 1) * 16, :]


def owned_of(place, source_blocks, arrived, groups):
    return pl.pallas_call(
        owned_kernel,
        in_specs=[smem(), smem(), vmem()],
        out_specs=vmem(),
        out_shape=jax.ShapeDtypeStruct((groups, 2, BLK // groups, arrived.shape[1]), F32),
        compiler_params=params(),
        name="owned",
    )(place, source_blocks, arrived)


def halve(bit, keep, came, stride):
    shape = (-1, 2, stride, *keep.shape[1:])

    def take(which):
        total = [
            lax.dynamic_index_in_dim(v.reshape(shape), which, 1, keepdims=False).astype(F32)
            for v in (keep, came)
        ]
        return (total[0] + total[1]).reshape(-1, *keep.shape[1:])

    return take(bit), take(1 - bit).astype(BF16)


def step(value, by):
    return lax.ppermute(value, "y", [(i, (i + by) % 4) for i in range(4)])


def swap(value, axis, size=2, flip=1):
    return lax.ppermute(value, axis, [(i, i ^ flip) for i in range(size)])


def exchange(value, axis):
    return lax.all_to_all(value, axis, 0, 0, tiled=True)


def around(values, axis, size):
    return [
        lax.ppermute(v, axis, [(i, (i + k) % size) for i in range(size)])
        for k, v in enumerate(values, 1)
    ]


def to_owner():
    def place(y, xh, z, c):
        return ((y * 2 + xh) * 8 + z) * 2 + c
    moves = []
    for y in range(4):
        for xh in range(2):
            for z in range(8):
                for c in range(2):
                    m = 4 * c + z % 4
                    target = place(2 * xh + z // 4, y // 2, 4 * (y % 2) + m // 2, m % 2)
                    moves.append((place(y, xh, z, c), target))
    return moves


def per_device(
    features, weights, bias, cotangent, tile_values, tile_count, tile_slot, source_blocks
):
    groups = 8
    owners = source_blocks.shape[0]
    width = features.shape[1]
    xl, y, core = lax.axis_index("xl"), lax.axis_index("y"), lax.axis_index("core")
    owner = lax.axis_index(TGT)
    group = lax.axis_index(REL)
    xh, z = lax.axis_index("xh"), lax.axis_index("z")
    xh, z = lax.axis_index("xh"), lax.axis_index("z")
    place = in_hbm(jnp.stack([owner, 192 * y, core, y, xh, z & 1]).astype(jnp.int32))

    own = adjacency_of(in_hbm(tile_values), in_hbm(tile_count))
    back, fore = step(own, 1), step(own, -1)
    far0, far1 = step(back[:1], 1), step(fore[1:], -1)
    features, weights, _ = lax.optimization_barrier((features, weights, own))
    source_blocks = in_hbm(source_blocks)
    outgoing = outgoing_of(in_hbm(features), source_blocks, place)
    fetched = resident(exchange(outgoing, TGT))

    own_slots = jnp.pad(tile_slot.reshape(1, 1, -1), ((0, 0), (0, 15), (0, width - 32))).astype(BF16)
    pieces = []
    for k in range(4):
        cut = lax.dynamic_slice(weights, (core, ((y + k) & 3) * 192 + 96 * xh, 0), (1, 96, width))
        pieces.append(jnp.concatenate([cut, own_slots], axis=1) if k else cut)
    came = around(pieces[1:], "y", 4)
    slots = jnp.concatenate([tile_slot.reshape(-1)] + [c[0, 96, :32].astype(jnp.int32) for c in came])
    w_part = jnp.concatenate([pieces[0]] + [c[:, :96] for c in came], axis=0)
    w_other = swap(w_part, "xh")
    w_part, w_other, far0, far1 = lax.optimization_barrier((w_part, w_other, far0, far1))
    w_mine = jnp.concatenate(
        [jnp.where(xh == 0, w_part, w_other), jnp.where(xh == 0, w_other, w_part)], axis=1
    )
    w_mine, w_theirs = resident(w_mine), resident(swap(w_mine, "core"))
    adjacency = [in_hbm(a) for a in (own, back, fore, far0, far1)]

    share = width // groups
    bias_share = lax.dynamic_slice_in_dim(bias, group * share, share)[:, None]
    cotangent_share = lax.dynamic_slice_in_dim(cotangent, group * share, share, 1).T
    slots, bias_share, cotangent_share = lax.optimization_barrier((slots, bias_share, cotangent_share))
    slots, bias_share, cotangent_share = in_hbm(slots), in_hbm(bias_share), in_hbm(cotangent_share)
    messages, for_core, part = forward_of(place, slots, adjacency, fetched, w_mine, w_theirs)
    of_core = swap(for_core, "core")
    arrived, of_core = lax.optimization_barrier((exchange(part.reshape(groups, share, -1), REL), of_core))
    arrived = resident(arrived)
    activated, grad_copies = activation_of(arrived, bias_share, cotangent_share)
    output = activated.T
    of_far = swap(jnp.stack([messages[1], of_core[1]]), "xh")
    grads, of_far = lax.optimization_barrier((exchange(grad_copies, REL).reshape(width, -1), of_far))

    partial = backward_of(place, slots, adjacency, resident(grads), w_mine, w_theirs, owners)
    returned = resident(exchange(in_hbm(partial), TGT))
    cut = owned_of(place, source_blocks, returned, groups)
    columns = exchange(cut, REL).reshape(2, 4, 2, BLK // groups, 192).sum(axis=0)
    grad_features = columns.transpose(1, 2, 0, 3).reshape(2, BLK // groups, width)

    far_grads = swap(grads, "xh")
    keep, send = weight_terms_of(
        place, messages, of_core, of_far, grads, swap(grads, "core"), far_grads, swap(far_grads, "core")
    )
    keep, send = halve((z >> 1) & 1, keep, swap(send, "z", 8, 1), 1)
    keep, send = halve(z >> 2, keep, swap(send, "z", 8, 2), 1)
    piece = keep + swap(send, "z", 8, 4).astype(F32)
    grad_weights = lax.ppermute(piece.reshape(2, 24, width), ("y", *TGT), to_owner())
    return (output, grad_weights, grad_features)


def solution(mesh):
    fine = Mesh(mesh.devices.reshape(2, 4, 2, 8, 2), (*REL, *TGT))
    placed = (
        P(TGT, None),
        P(REL, None, None),
        P(),
        P(TGT, None),
        P(REL, TGT, None, None),
        P(REL, TGT),
        P(REL, TGT, None),
        P(),
    )
    return jax.shard_map(
        per_device,
        mesh=fine,
        in_specs=placed,
        out_specs=(P(TGT, REL), P(REL, TGT, None), P(TGT, REL, None)),
        check_vma=False,
    )
```

```python
import functools

import jax
import jax.numpy as jnp
from jax import lax
from jax.experimental import pallas as pl
from jax.experimental.pallas import tpu as pltpu
from jax.sharding import Mesh, PartitionSpec as P

F32 = jnp.float32
BF16 = jnp.bfloat16
BLK = 128
REL = ("xl", "y")
TGT = ("xh", "z", "core")
VMEM_LIMIT = 44 * 1024 * 1024


def in_hbm(value):
    return pltpu.with_memory_space_constraint(value, pltpu.MemorySpace.HBM)


def resident(value):
    return pltpu.with_memory_space_constraint(value, pltpu.MemorySpace.VMEM)


def params(*semantics):
    return pltpu.CompilerParams(
        dimension_semantics=semantics or None, vmem_limit_bytes=VMEM_LIMIT
    )


def smem():
    return pl.BlockSpec(memory_space=pltpu.MemorySpace.SMEM)


def vmem():
    return pl.BlockSpec(memory_space=pltpu.MemorySpace.VMEM)


def dot(a, b, ca, cb):
    return lax.dot_general(a, b, (((ca,), (cb,)), ((), ())), preferred_element_type=F32)


def adjacency_kernel(count_ref, values_ref, out_ref):
    count = count_ref[pl.program_id(0), pl.program_id(1)]
    slots = values_ref.shape[2]
    live, degree = [], None
    for s in range(slots):
        v = values_ref[0, :, s, :]
        v = jnp.where(s < count, v, jnp.zeros_like(v)).astype(F32)
        live.append(v)
        degree = v if degree is None else degree + v
    total = jnp.sum(degree, axis=1, keepdims=True)
    scale = 1.0 / jnp.sqrt(jnp.maximum(total, 1.0))
    for s in range(slots):
        out_ref[0, :, s * BLK : (s + 1) * BLK] = (live[s] * scale).astype(BF16)


def adjacency_of(tile_values, tile_count):
    rels, rows, slots, cols = tile_values.shape
    return pl.pallas_call(
        adjacency_kernel,
        grid=(rels, rows // BLK),
        in_specs=[smem(), pl.BlockSpec((1, BLK, slots, cols), lambda r, q: (r, q, 0, 0))],
        out_specs=pl.BlockSpec((1, BLK, slots * cols), lambda r, q: (r, q, 0)),
        out_shape=jax.ShapeDtypeStruct((rels, rows, slots * cols), BF16),
        compiler_params=params("arbitrary", "arbitrary"),
        name="adjacency",
    )(tile_count, tile_values)


def outgoing_kernel(place_ref, table_ref, features_ref, out_ref, turned_ref):
    owner, first = place_ref[0], place_ref[1]
    turned_ref[...] = features_ref[...].T
    piece = turned_ref[pl.ds(pl.multiple_of(first, 64), 192), :]
    block0, block1 = piece[:, :BLK], piece[:, BLK:]
    for t in range(out_ref.shape[0]):
        k = table_ref[t, owner]
        picked = jnp.where(k == 1, block1, block0)
        out_ref[t] = jnp.where(k >= 0, picked, jnp.zeros_like(picked))


def outgoing_of(features, source_blocks, place):
    rows, width = features.shape
    return pl.pallas_call(
        outgoing_kernel,
        in_specs=[smem(), smem(), vmem()],
        out_specs=vmem(),
        out_shape=jax.ShapeDtypeStruct((source_blocks.shape[0], 192, BLK), BF16),
        scratch_shapes=[pltpu.VMEM((width, rows), BF16)],
        compiler_params=params(),
        name="outgoing",
    )(place, source_blocks, features)


ORDER = (0, 1, 3, 2)


def start_loads(adj_refs, adj_buf, sems):
    own, back, fore, far0, far1 = adj_refs
    loads = []
    for n, ref in enumerate((own, back, fore)):
        loads.append([pltpu.make_async_copy(ref, adj_buf.at[pl.ds(2 * n, 2)], sems.at[n])])
    loads.append(
        [pltpu.make_async_copy(ref, adj_buf.at[pl.ds(6 + n, 1)], sems.at[3 + n]) for n, ref in enumerate((far0, far1))]
    )
    for group in loads:
        for load in group:
            load.start()
    return loads


def load_scratch(rows, wide):
    return [pltpu.VMEM((8, rows, wide), BF16), pltpu.SemaphoreType.DMA((5,))]


def hbm():
    return pl.BlockSpec(memory_space=pltpu.MemorySpace.HBM)


def forward_kernel(
    place_ref, slot_ref, own_ref, back_ref, fore_ref, far0_ref, far1_ref, fetched_ref, w_mine_ref, w_theirs_ref,
    keep_ref, keep_far_ref, send_ref, send_far_ref, pre_ref, adj_buf, sems, both_ref, acc_ref,
):
    core, y = place_ref[2], place_ref[3]
    loads = start_loads((own_ref, back_ref, fore_ref, far0_ref, far1_ref), adj_buf, sems)
    for n, k in enumerate(ORDER):
        for load in loads[n]:
            load.wait()
        for p in range(2):
            for q in range(2):
                base = ((k * 2 + p) * 2 + q) * 8
                wide = jnp.concatenate([fetched_ref[slot_ref[base + s]] for s in range(8)], axis=1)
                part = adj_buf[2 * n + p, q * BLK : (q + 1) * BLK, :]
                both_ref[p, :, q * BLK : (q + 1) * BLK] = dot(wide, part, 1, 1).astype(BF16)
        j = (y - k) & 3
        far, pair = (j >> 1) ^ place_ref[4], pl.ds(2 * (j & 1), 2)
        keep = both_ref[:, pl.ds(pl.multiple_of(96 * core, 32), 96)]
        send = both_ref[:, pl.ds(pl.multiple_of(96 * (1 - core), 32), 96)]

        @pl.when(far == 0)
        def _():
            keep_ref[pair] = keep
            send_ref[pair] = send

        @pl.when(far == 1)
        def _():
            keep_far_ref[pair] = keep
            send_far_ref[pair] = send

        term = dot(w_mine_ref[k], both_ref[core], 0, 0) + dot(w_theirs_ref[k], both_ref[1 - core], 0, 0)
        if n == 0:
            acc_ref[...] = term
        elif n < 3:
            acc_ref[...] += term
        else:
            pre_ref[...] = (acc_ref[...] + term).astype(BF16)


def forward_of(place, slots, adjacency, fetched, w_mine, w_theirs):
    _, rows, wide = adjacency[0].shape
    width = w_mine.shape[2]
    half = jax.ShapeDtypeStruct((4, 96, rows), BF16)
    return pl.pallas_call(
        forward_kernel,
        in_specs=[smem(), smem()] + [hbm()] * 5 + [vmem()] * 3,
        out_specs=[vmem()] * 5,
        out_shape=[half, half, half, half, jax.ShapeDtypeStruct((width, rows), BF16)],
        scratch_shapes=load_scratch(rows, wide)
        + [pltpu.VMEM((2, 192, rows), BF16), pltpu.VMEM((width, rows), F32)],
        compiler_params=params(),
        name="forward",
    )(place, slots, *adjacency, fetched, w_mine, w_theirs)


def activation_kernel(arrived_ref, bias_ref, cotangent_ref, act_ref, grad_ref):
    pre = bias_ref[...]
    for g in range(arrived_ref.shape[0]):
        pre = pre + arrived_ref[g].astype(F32)
    sigmoid = jax.nn.sigmoid(pre)
    act_ref[...] = (pre * sigmoid).astype(BF16)
    derivative = sigmoid * (1.0 + pre * (1.0 - sigmoid))
    grad = (cotangent_ref[...].astype(F32) * derivative).astype(BF16)
    for g in range(grad_ref.shape[0]):
        grad_ref[g] = grad


def activation_of(arrived, bias, cotangent):
    return pl.pallas_call(
        activation_kernel,
        in_specs=[vmem()] * 3,
        out_specs=[vmem()] * 2,
        out_shape=[
            jax.ShapeDtypeStruct(arrived.shape[1:], BF16),
            jax.ShapeDtypeStruct(arrived.shape, BF16),
        ],
        compiler_params=params(),
        name="activation",
    )(arrived, bias, cotangent)


def backward_kernel(
    place_ref, slot_ref, own_ref, back_ref, fore_ref, far0_ref, far1_ref, grad_ref, w_mine_ref, w_theirs_ref,
    out_ref, adj_buf, sems, both_ref, acc_ref,
):
    core = place_ref[2]
    loads = start_loads((own_ref, back_ref, fore_ref, far0_ref, far1_ref), adj_buf, sems)
    acc_ref[...] = jnp.zeros_like(acc_ref)
    for n, k in enumerate(ORDER):
        both_ref[core] = dot(w_mine_ref[k], grad_ref[...], 1, 0).astype(BF16)
        both_ref[1 - core] = dot(w_theirs_ref[k], grad_ref[...], 1, 0).astype(BF16)
        for load in loads[n]:
            load.wait()
        for p in range(2):
            for q in range(2):
                base = ((k * 2 + p) * 2 + q) * 8
                part = adj_buf[2 * n + p, q * BLK : (q + 1) * BLK, :]
                wide = dot(both_ref[p, :, q * BLK : (q + 1) * BLK], part, 1, 0)
                for s in range(8):
                    acc_ref[slot_ref[base + s]] += wide[:, s * BLK : (s + 1) * BLK]
    out_ref[...] = acc_ref[...].astype(BF16)


def backward_of(place, slots, adjacency, grads, w_mine, w_theirs, owners):
    _, rows, wide = adjacency[0].shape
    return pl.pallas_call(
        backward_kernel,
        in_specs=[smem(), smem()] + [hbm()] * 5 + [vmem()] * 3,
        out_specs=vmem(),
        out_shape=jax.ShapeDtypeStruct((owners, 192, BLK), BF16),
        scratch_shapes=load_scratch(rows, wide)
        + [pltpu.VMEM((2, 192, rows), BF16), pltpu.VMEM((owners, 192, BLK), F32)],
        compiler_params=params(),
        name="backward",
    )(place, slots, *adjacency, grads, w_mine, w_theirs)


def weight_kernel(
    place_ref, own_ref, core_ref, far_ref, far_core_ref, grad_ref, core_grad_ref, far_grad_ref, far_core_grad_ref, *refs
):
    *out_refs, pieces_ref = refs
    z = place_ref[5]
    grads = jnp.concatenate(
        [grad_ref[...], core_grad_ref[...], far_grad_ref[...], far_core_grad_ref[...]], axis=1
    )
    for r in range(4):
        wide = jnp.concatenate([own_ref[r], core_ref[r], far_ref[r], far_core_ref[r]], axis=1)
        term = dot(wide, grads, 1, 1)
        for m in range(4):
            part = slice(24 * (r % 2), 24 * (r % 2) + 24)
            pieces_ref[4 * (r // 2) + m, part] = term[m * 24 : (m + 1) * 24]
    for k, out_ref in enumerate(out_refs):
        out_ref[...] = pieces_ref[z ^ k].astype(out_ref.dtype)


def weight_terms_of(place, *operands):
    width = operands[-1].shape[0]
    return pl.pallas_call(
        weight_kernel,
        in_specs=[smem()] + [vmem()] * 8,
        out_specs=[vmem()] * 8,
        out_shape=[jax.ShapeDtypeStruct((48, width), F32 if k == 0 else BF16) for k in range(8)],
        scratch_shapes=[pltpu.VMEM((8, 48, width), F32)],
        compiler_params=params(),
        name="weight_terms",
    )(place, *operands)


def owned_kernel(place_ref, table_ref, arrived_ref, out_ref):
    owner = place_ref[0]
    zero = jnp.zeros(arrived_ref.shape[1:], F32)
    sums = [zero, zero]
    for t in range(arrived_ref.shape[0]):
        k = table_ref[t, owner]
        v = arrived_ref[t].astype(F32)
        for b in range(2):
            sums[b] = sums[b] + jnp.where(k == b, v, zero)
    for b in range(2):
        turned = sums[b].T
        for g in range(out_ref.shape[0]):
            out_ref[g, b] = turned[g * 16 : (g + 1) * 16, :]


def owned_of(place, source_blocks, arrived, groups):
    return pl.pallas_call(
        owned_kernel,
        in_specs=[smem(), smem(), vmem()],
        out_specs=vmem(),
        out_shape=jax.ShapeDtypeStruct((groups, 2, BLK // groups, arrived.shape[1]), F32),
        compiler_params=params(),
        name="owned",
    )(place, source_blocks, arrived)


def step(value, by):
    return lax.ppermute(value, "y", [(i, (i + by) % 4) for i in range(4)])


def swap(value, axis, size=2, flip=1):
    return lax.ppermute(value, axis, [(i, i ^ flip) for i in range(size)])


def exchange(value, axis):
    return lax.all_to_all(value, axis, 0, 0, tiled=True)


def around(values, axis, size):
    return [
        lax.ppermute(v, axis, [(i, (i + k) % size) for i in range(size)])
        for k, v in enumerate(values, 1)
    ]


def to_owner():
    def place(y, xh, z, c):
        return ((y * 2 + xh) * 8 + z) * 2 + c
    moves = []
    for y in range(4):
        for xh in range(2):
            for z in range(8):
                for c in range(2):
                    m = 4 * c + z % 4
                    target = place(2 * xh + z // 4, y // 2, 4 * (y % 2) + m // 2, m % 2)
                    moves.append((place(y, xh, z, c), target))
    return moves


def per_device(
    features, weights, bias, cotangent, tile_values, tile_count, tile_slot, source_blocks
):
    groups = 8
    owners = source_blocks.shape[0]
    width = features.shape[1]
    xl, y, core = lax.axis_index("xl"), lax.axis_index("y"), lax.axis_index("core")
    owner = lax.axis_index(TGT)
    group = lax.axis_index(REL)
    xh, z = lax.axis_index("xh"), lax.axis_index("z")
    xh, z = lax.axis_index("xh"), lax.axis_index("z")
    place = in_hbm(jnp.stack([owner, 192 * y, core, y, xh, z]).astype(jnp.int32))

    own = adjacency_of(in_hbm(tile_values), in_hbm(tile_count))
    back, fore = step(own, 1), step(own, -1)
    features, weights, _ = lax.optimization_barrier((features, weights, own))
    source_blocks = in_hbm(source_blocks)
    outgoing = outgoing_of(in_hbm(features), source_blocks, place)
    fetched = resident(exchange(outgoing, TGT))

    own_slots = jnp.pad(tile_slot.reshape(1, 1, -1), ((0, 0), (0, 15), (0, width - 32))).astype(BF16)
    pieces = []
    for k in range(4):
        cut = lax.dynamic_slice(weights, (core, ((y + k) & 3) * 192 + 96 * xh, 0), (1, 96, width))
        pieces.append(jnp.concatenate([cut, own_slots], axis=1) if k else cut)
    came = around(pieces[1:], "y", 4)
    slots = jnp.concatenate([tile_slot.reshape(-1)] + [c[0, 96, :32].astype(jnp.int32) for c in came])
    share = width // groups
    bias_share = lax.dynamic_slice_in_dim(bias, group * share, share)
    bias_share = jnp.broadcast_to(bias_share[:, None], (share, features.shape[0]))
    cotangent_share = lax.dynamic_slice_in_dim(cotangent, group * share, share, 1).T
    back, fore, slots, bias_share, cotangent_share = lax.optimization_barrier(
        (back, fore, slots, bias_share, cotangent_share)
    )
    slots, bias_share, cotangent_share = in_hbm(slots), in_hbm(bias_share), in_hbm(cotangent_share)
    far0, far1 = step(back[:1], 1), step(fore[1:], -1)
    w_part = jnp.concatenate([pieces[0]] + [c[:, :96] for c in came], axis=0)
    w_other = swap(w_part, "xh")
    w_part, w_other, far0, far1 = lax.optimization_barrier((w_part, w_other, far0, far1))
    w_mine = jnp.concatenate(
        [jnp.where(xh == 0, w_part, w_other), jnp.where(xh == 0, w_other, w_part)], axis=1
    )
    w_mine, w_theirs = resident(w_mine), resident(swap(w_mine, "core"))
    adjacency = [in_hbm(a) for a in (own, back, fore, far0, far1)]

    own_terms, far_terms, for_core, for_far_core, part = forward_of(
        place, slots, adjacency, fetched, w_mine, w_theirs
    )
    of_core, of_far = swap(for_core, "core"), swap(far_terms, "xh")
    of_far_core = swap(for_far_core, "core")
    arrived, of_far_core = lax.optimization_barrier((exchange(part.reshape(groups, share, -1), REL), of_far_core))
    arrived = resident(arrived)
    activated, grad_copies = activation_of(arrived, bias_share, cotangent_share)
    output = activated.T
    of_far_core = swap(of_far_core, "xh")
    grads, of_core, of_far, of_far_core = lax.optimization_barrier(
        (exchange(grad_copies, REL).reshape(width, -1), of_core, of_far, of_far_core)
    )
    partial = backward_of(place, slots, adjacency, resident(grads), w_mine, w_theirs, owners)
    returned = resident(exchange(in_hbm(partial), TGT))
    cut = owned_of(place, source_blocks, returned, groups)
    columns = exchange(cut, REL).reshape(2, 4, 2, BLK // groups, 192).sum(axis=0)
    grad_features = columns.transpose(1, 2, 0, 3).reshape(2, BLK // groups, width)

    far_grads = swap(grads, "xh")
    piece, *others = weight_terms_of(
        place, own_terms, of_core, of_far, of_far_core,
        grads, swap(grads, "core"), far_grads, swap(far_grads, "core"),
    )
    for k, other in enumerate(others, 1):
        piece = piece + swap(other, "z", 8, k).astype(F32)
    grad_weights = lax.ppermute(piece.reshape(2, 24, width), ("y", *TGT), to_owner())
    return (output, grad_weights, grad_features)


def solution(mesh):
    fine = Mesh(mesh.devices.reshape(2, 4, 2, 8, 2), (*REL, *TGT))
    placed = (
        P(TGT, None),
        P(REL, None, None),
        P(),
        P(TGT, None),
        P(REL, TGT, None, None),
        P(REL, TGT),
        P(REL, TGT, None),
        P(),
    )
    return jax.shard_map(
        per_device,
        mesh=fine,
        in_specs=placed,
        out_specs=(P(TGT, REL), P(REL, TGT, None), P(TGT, REL, None)),
        check_vma=False,
    )
```

```python
import functools

import jax
import jax.numpy as jnp
from jax import lax
from jax.experimental import pallas as pl
from jax.experimental.pallas import tpu as pltpu
from jax.sharding import Mesh, PartitionSpec as P

F32 = jnp.float32
BF16 = jnp.bfloat16
BLK = 128
REL = ("xl", "y")
TGT = ("xh", "z", "core")
VMEM_LIMIT = 44 * 1024 * 1024


def in_hbm(value):
    return pltpu.with_memory_space_constraint(value, pltpu.MemorySpace.HBM)


def resident(value):
    return pltpu.with_memory_space_constraint(value, pltpu.MemorySpace.VMEM)


def params(*semantics):
    return pltpu.CompilerParams(
        dimension_semantics=semantics or None, vmem_limit_bytes=VMEM_LIMIT
    )


def smem():
    return pl.BlockSpec(memory_space=pltpu.MemorySpace.SMEM)


def vmem():
    return pl.BlockSpec(memory_space=pltpu.MemorySpace.VMEM)


def dot(a, b, ca, cb):
    return lax.dot_general(a, b, (((ca,), (cb,)), ((), ())), preferred_element_type=F32)


def adjacency_kernel(count_ref, values_ref, out_ref):
    count = count_ref[pl.program_id(0), pl.program_id(1)]
    slots = values_ref.shape[2]
    live, degree = [], None
    for s in range(slots):
        v = values_ref[0, :, s, :]
        v = jnp.where(s < count, v, jnp.zeros_like(v)).astype(F32)
        live.append(v)
        degree = v if degree is None else degree + v
    total = jnp.sum(degree, axis=1, keepdims=True)
    scale = 1.0 / jnp.sqrt(jnp.maximum(total, 1.0))
    for s in range(slots):
        out_ref[0, :, s * BLK : (s + 1) * BLK] = (live[s] * scale).astype(BF16)


def adjacency_of(tile_values, tile_count):
    rels, rows, slots, cols = tile_values.shape
    return pl.pallas_call(
        adjacency_kernel,
        grid=(rels, rows // BLK),
        in_specs=[smem(), pl.BlockSpec((1, BLK, slots, cols), lambda r, q: (r, q, 0, 0))],
        out_specs=pl.BlockSpec((1, BLK, slots * cols), lambda r, q: (r, q, 0)),
        out_shape=jax.ShapeDtypeStruct((rels, rows, slots * cols), BF16),
        compiler_params=params("arbitrary", "arbitrary"),
        name="adjacency",
    )(tile_count, tile_values)


def outgoing_kernel(place_ref, table_ref, features_ref, out_ref, turned_ref):
    owner, first = place_ref[0], place_ref[1]
    turned_ref[...] = features_ref[...].T
    piece = turned_ref[pl.ds(pl.multiple_of(first, 64), 192), :]
    block0, block1 = piece[:, :BLK], piece[:, BLK:]
    for t in range(out_ref.shape[0]):
        k = table_ref[t, owner]
        picked = jnp.where(k == 1, block1, block0)
        out_ref[t] = jnp.where(k >= 0, picked, jnp.zeros_like(picked))


def outgoing_of(features, source_blocks, place):
    rows, width = features.shape
    return pl.pallas_call(
        outgoing_kernel,
        in_specs=[smem(), smem(), vmem()],
        out_specs=vmem(),
        out_shape=jax.ShapeDtypeStruct((source_blocks.shape[0], 192, BLK), BF16),
        scratch_shapes=[pltpu.VMEM((width, rows), BF16)],
        compiler_params=params(),
        name="outgoing",
    )(place, source_blocks, features)


ORDER = (0, 1, 3, 2)


def start_loads(adj_refs, adj_buf, sems):
    own, back, fore, far0, far1 = adj_refs
    loads = []
    for n, ref in enumerate((own, back, fore)):
        loads.append([pltpu.make_async_copy(ref, adj_buf.at[pl.ds(2 * n, 2)], sems.at[n])])
    loads.append(
        [pltpu.make_async_copy(ref, adj_buf.at[pl.ds(6 + n, 1)], sems.at[3 + n]) for n, ref in enumerate((far0, far1))]
    )
    for group in loads:
        for load in group:
            load.start()
    return loads


def load_scratch(rows, wide):
    return [pltpu.VMEM((8, rows, wide), BF16), pltpu.SemaphoreType.DMA((5,))]


def hbm():
    return pl.BlockSpec(memory_space=pltpu.MemorySpace.HBM)


def forward_kernel(
    place_ref, slot_ref, own_ref, back_ref, fore_ref, far0_ref, far1_ref, fetched_ref, w_mine_ref, w_theirs_ref,
    keep_ref, keep_far_ref, send_ref, send_far_ref, pre_ref, adj_buf, sems, both_ref, acc_ref,
):
    core, y = place_ref[2], place_ref[3]
    loads = start_loads((own_ref, back_ref, fore_ref, far0_ref, far1_ref), adj_buf, sems)
    for n, k in enumerate(ORDER):
        for load in loads[n]:
            load.wait()
        for p in range(2):
            for q in range(2):
                base = ((k * 2 + p) * 2 + q) * 8
                wide = jnp.concatenate([fetched_ref[slot_ref[base + s]] for s in range(8)], axis=1)
                part = adj_buf[2 * n + p, q * BLK : (q + 1) * BLK, :]
                both_ref[p, :, q * BLK : (q + 1) * BLK] = dot(wide, part, 1, 1).astype(BF16)
        j = (y - k) & 3
        far, pair = (j >> 1) ^ place_ref[4], pl.ds(2 * (j & 1), 2)
        keep = both_ref[:, pl.ds(pl.multiple_of(96 * core, 32), 96)]
        send = both_ref[:, pl.ds(pl.multiple_of(96 * (1 - core), 32), 96)]

        @pl.when(far == 0)
        def _():
            keep_ref[pair] = keep
            send_ref[pair] = send

        @pl.when(far == 1)
        def _():
            keep_far_ref[pair] = keep
            send_far_ref[pair] = send

        term = dot(w_mine_ref[k], both_ref[core], 0, 0) + dot(w_theirs_ref[k], both_ref[1 - core], 0, 0)
        if n == 0:
            acc_ref[...] = term
        elif n < 3:
            acc_ref[...] += term
        else:
            pre_ref[...] = (acc_ref[...] + term).astype(BF16)


def forward_of(place, slots, adjacency, fetched, w_mine, w_theirs):
    _, rows, wide = adjacency[0].shape
    width = w_mine.shape[2]
    half = jax.ShapeDtypeStruct((4, 96, rows), BF16)
    return pl.pallas_call(
        forward_kernel,
        in_specs=[smem(), smem()] + [hbm()] * 5 + [vmem()] * 3,
        out_specs=[vmem()] * 5,
        out_shape=[half, half, half, half, jax.ShapeDtypeStruct((width, rows), BF16)],
        scratch_shapes=load_scratch(rows, wide)
        + [pltpu.VMEM((2, 192, rows), BF16), pltpu.VMEM((width, rows), F32)],
        compiler_params=params(),
        name="forward",
    )(place, slots, *adjacency, fetched, w_mine, w_theirs)


def activation_kernel(arrived_ref, bias_ref, cotangent_ref, act_ref, grad_ref):
    pre = bias_ref[...]
    for g in range(arrived_ref.shape[0]):
        pre = pre + arrived_ref[g].astype(F32)
    sigmoid = jax.nn.sigmoid(pre)
    act_ref[...] = (pre * sigmoid).astype(BF16)
    derivative = sigmoid * (1.0 + pre * (1.0 - sigmoid))
    grad = (cotangent_ref[...].astype(F32) * derivative).astype(BF16)
    for g in range(grad_ref.shape[0]):
        grad_ref[g] = grad


def activation_of(arrived, bias, cotangent):
    return pl.pallas_call(
        activation_kernel,
        in_specs=[vmem()] * 3,
        out_specs=[vmem()] * 2,
        out_shape=[
            jax.ShapeDtypeStruct(arrived.shape[1:], BF16),
            jax.ShapeDtypeStruct(arrived.shape, BF16),
        ],
        compiler_params=params(),
        name="activation",
    )(arrived, bias, cotangent)


def backward_kernel(
    place_ref, slot_ref, own_ref, back_ref, fore_ref, far0_ref, far1_ref, grad_ref, w_mine_ref, w_theirs_ref,
    out_ref, adj_buf, sems, both_ref, acc_ref,
):
    core = place_ref[2]
    loads = start_loads((own_ref, back_ref, fore_ref, far0_ref, far1_ref), adj_buf, sems)
    acc_ref[...] = jnp.zeros_like(acc_ref)
    for n, k in enumerate(ORDER):
        both_ref[core] = dot(w_mine_ref[k], grad_ref[...], 1, 0).astype(BF16)
        both_ref[1 - core] = dot(w_theirs_ref[k], grad_ref[...], 1, 0).astype(BF16)
        for load in loads[n]:
            load.wait()
        for p in range(2):
            for q in range(2):
                base = ((k * 2 + p) * 2 + q) * 8
                part = adj_buf[2 * n + p, q * BLK : (q + 1) * BLK, :]
                wide = dot(both_ref[p, :, q * BLK : (q + 1) * BLK], part, 1, 0)
                for s in range(8):
                    acc_ref[slot_ref[base + s]] += wide[:, s * BLK : (s + 1) * BLK]
    out_ref[...] = acc_ref[...].astype(BF16)


def backward_of(place, slots, adjacency, grads, w_mine, w_theirs, owners):
    _, rows, wide = adjacency[0].shape
    return pl.pallas_call(
        backward_kernel,
        in_specs=[smem(), smem()] + [hbm()] * 5 + [vmem()] * 3,
        out_specs=vmem(),
        out_shape=jax.ShapeDtypeStruct((owners, 192, BLK), BF16),
        scratch_shapes=load_scratch(rows, wide)
        + [pltpu.VMEM((2, 192, rows), BF16), pltpu.VMEM((owners, 192, BLK), F32)],
        compiler_params=params(),
        name="backward",
    )(place, slots, *adjacency, grads, w_mine, w_theirs)


def weight_kernel(
    place_ref, own_ref, core_ref, far_ref, far_core_ref, grad_ref, core_grad_ref, far_grad_ref, far_core_grad_ref, *refs
):
    *out_refs, pieces_ref = refs
    z = place_ref[5]
    grads = jnp.concatenate(
        [grad_ref[...], core_grad_ref[...], far_grad_ref[...], far_core_grad_ref[...]], axis=1
    )
    for r in range(4):
        wide = jnp.concatenate([own_ref[r], core_ref[r], far_ref[r], far_core_ref[r]], axis=1)
        term = dot(wide, grads, 1, 1)
        for m in range(4):
            part = slice(24 * (r % 2), 24 * (r % 2) + 24)
            pieces_ref[4 * (r // 2) + m, part] = term[m * 24 : (m + 1) * 24]
    for k, out_ref in enumerate(out_refs):
        out_ref[...] = pieces_ref[z ^ k].astype(out_ref.dtype)


def weight_terms_of(place, *operands):
    width = operands[-1].shape[0]
    return pl.pallas_call(
        weight_kernel,
        in_specs=[smem()] + [vmem()] * 8,
        out_specs=[vmem()] * 8,
        out_shape=[jax.ShapeDtypeStruct((48, width), F32 if k == 0 else BF16) for k in range(8)],
        scratch_shapes=[pltpu.VMEM((8, 48, width), F32)],
        compiler_params=params(),
        name="weight_terms",
        cost_estimate=pl.CostEstimate(flops=24500000000, transcendentals=0, bytes_accessed=0),
    )(place, *operands)


def owned_kernel(place_ref, table_ref, arrived_ref, out_ref):
    owner = place_ref[0]
    zero = jnp.zeros(arrived_ref.shape[1:], F32)
    sums = [zero, zero]
    for t in range(arrived_ref.shape[0]):
        k = table_ref[t, owner]
        v = arrived_ref[t].astype(F32)
        for b in range(2):
            sums[b] = sums[b] + jnp.where(k == b, v, zero)
    for b in range(2):
        turned = sums[b].T
        for g in range(out_ref.shape[0]):
            out_ref[g, b] = turned[g * 16 : (g + 1) * 16, :]


def owned_of(place, source_blocks, arrived, groups):
    return pl.pallas_call(
        owned_kernel,
        in_specs=[smem(), smem(), vmem()],
        out_specs=vmem(),
        out_shape=jax.ShapeDtypeStruct((groups, 2, BLK // groups, arrived.shape[1]), F32),
        compiler_params=params(),
        name="owned",
    )(place, source_blocks, arrived)


def step(value, by):
    return lax.ppermute(value, "y", [(i, (i + by) % 4) for i in range(4)])


def swap(value, axis, size=2, flip=1):
    return lax.ppermute(value, axis, [(i, i ^ flip) for i in range(size)])


def exchange(value, axis):
    return lax.all_to_all(value, axis, 0, 0, tiled=True)


def around(values, axis, size):
    return [
        lax.ppermute(v, axis, [(i, (i + k) % size) for i in range(size)])
        for k, v in enumerate(values, 1)
    ]


def to_owner():
    def place(y, xh, z, c):
        return ((y * 2 + xh) * 8 + z) * 2 + c
    moves = []
    for y in range(4):
        for xh in range(2):
            for z in range(8):
                for c in range(2):
                    m = 4 * c + z % 4
                    target = place(2 * xh + z // 4, y // 2, 4 * (y % 2) + m // 2, m % 2)
                    moves.append((place(y, xh, z, c), target))
    return moves


def per_device(
    features, weights, bias, cotangent, tile_values, tile_count, tile_slot, source_blocks
):
    groups = 8
    owners = source_blocks.shape[0]
    width = features.shape[1]
    xl, y, core = lax.axis_index("xl"), lax.axis_index("y"), lax.axis_index("core")
    owner = lax.axis_index(TGT)
    group = lax.axis_index(REL)
    xh, z = lax.axis_index("xh"), lax.axis_index("z")
    xh, z = lax.axis_index("xh"), lax.axis_index("z")
    place = in_hbm(jnp.stack([owner, 192 * y, core, y, xh, z]).astype(jnp.int32))

    own = adjacency_of(in_hbm(tile_values), in_hbm(tile_count))
    back, fore = step(own, 1), step(own, -1)
    features, weights, _ = lax.optimization_barrier((features, weights, own))
    source_blocks = in_hbm(source_blocks)
    outgoing = outgoing_of(in_hbm(features), source_blocks, place)
    fetched = resident(exchange(outgoing, TGT))

    own_slots = jnp.pad(tile_slot.reshape(1, 1, -1), ((0, 0), (0, 15), (0, width - 32))).astype(BF16)
    pieces = []
    for k in range(4):
        cut = lax.dynamic_slice(weights, (core, ((y + k) & 3) * 192 + 96 * xh, 0), (1, 96, width))
        pieces.append(jnp.concatenate([cut, own_slots], axis=1) if k else cut)
    came = around(pieces[1:], "y", 4)
    slots = jnp.concatenate([tile_slot.reshape(-1)] + [c[0, 96, :32].astype(jnp.int32) for c in came])
    share = width // groups
    bias_share = lax.dynamic_slice_in_dim(bias, group * share, share)
    bias_share = jnp.broadcast_to(bias_share[:, None], (share, features.shape[0]))
    cotangent_share = lax.dynamic_slice_in_dim(cotangent, group * share, share, 1).T
    back, fore, slots, bias_share, cotangent_share = lax.optimization_barrier(
        (back, fore, slots, bias_share, cotangent_share)
    )
    slots, bias_share, cotangent_share = in_hbm(slots), in_hbm(bias_share), in_hbm(cotangent_share)
    far0, far1 = step(back[:1], 1), step(fore[1:], -1)
    w_part = jnp.concatenate([pieces[0]] + [c[:, :96] for c in came], axis=0)
    w_other = swap(w_part, "xh")
    w_part, w_other, far0, far1 = lax.optimization_barrier((w_part, w_other, far0, far1))
    w_mine = jnp.concatenate(
        [jnp.where(xh == 0, w_part, w_other), jnp.where(xh == 0, w_other, w_part)], axis=1
    )
    w_mine, w_theirs = resident(w_mine), resident(swap(w_mine, "core"))
    adjacency = [in_hbm(a) for a in (own, back, fore, far0, far1)]

    own_terms, far_terms, for_core, for_far_core, part = forward_of(
        place, slots, adjacency, fetched, w_mine, w_theirs
    )
    of_core, of_far = swap(for_core, "core"), swap(far_terms, "xh")
    of_far_core = swap(for_far_core, "core")
    arrived, of_far, of_far_core = lax.optimization_barrier(
        (exchange(part.reshape(groups, share, -1), REL), of_far, of_far_core)
    )
    arrived = resident(arrived)
    activated, grad_copies = activation_of(arrived, bias_share, cotangent_share)
    output = activated.T
    of_far_core = swap(of_far_core, "xh")
    grads, of_core, of_far, of_far_core = lax.optimization_barrier(
        (exchange(grad_copies, REL).reshape(width, -1), of_core, of_far, of_far_core)
    )
    partial = backward_of(place, slots, adjacency, resident(grads), w_mine, w_theirs, owners)
    returned = resident(exchange(in_hbm(partial), TGT))
    cut = owned_of(place, source_blocks, returned, groups)
    columns = exchange(cut, REL).reshape(2, 4, 2, BLK // groups, 192).sum(axis=0)
    grad_features = columns.transpose(1, 2, 0, 3).reshape(2, BLK // groups, width)

    far_grads, _ = lax.optimization_barrier((swap(grads, "xh"), partial))
    piece, *others = weight_terms_of(
        place, own_terms, of_core, of_far, of_far_core,
        grads, swap(grads, "core"), far_grads, swap(far_grads, "core"),
    )
    for k, other in enumerate(others, 1):
        piece = piece + swap(other, "z", 8, k).astype(F32)
    grad_weights = lax.ppermute(piece.reshape(2, 24, width), ("y", *TGT), to_owner())
    return (output, grad_weights, grad_features)


def solution(mesh):
    fine = Mesh(mesh.devices.reshape(2, 4, 2, 8, 2), (*REL, *TGT))
    placed = (
        P(TGT, None),
        P(REL, None, None),
        P(),
        P(TGT, None),
        P(REL, TGT, None, None),
        P(REL, TGT),
        P(REL, TGT, None),
        P(),
    )
    return jax.shard_map(
        per_device,
        mesh=fine,
        in_specs=placed,
        out_specs=(P(TGT, REL), P(REL, TGT, None), P(TGT, REL, None)),
        check_vma=False,
    )
```

```python
import functools

import jax
import jax.numpy as jnp
from jax import lax
from jax.experimental import pallas as pl
from jax.experimental.pallas import tpu as pltpu
from jax.sharding import Mesh, PartitionSpec as P

F32 = jnp.float32
BF16 = jnp.bfloat16
BLK = 128
REL = ("xl", "y")
TGT = ("xh", "z", "core")
VMEM_LIMIT = 44 * 1024 * 1024


def in_hbm(value):
    return pltpu.with_memory_space_constraint(value, pltpu.MemorySpace.HBM)


def resident(value):
    return pltpu.with_memory_space_constraint(value, pltpu.MemorySpace.VMEM)


def params(*semantics):
    return pltpu.CompilerParams(
        dimension_semantics=semantics or None, vmem_limit_bytes=VMEM_LIMIT
    )


def smem():
    return pl.BlockSpec(memory_space=pltpu.MemorySpace.SMEM)


def vmem():
    return pl.BlockSpec(memory_space=pltpu.MemorySpace.VMEM)


def dot(a, b, ca, cb):
    return lax.dot_general(a, b, (((ca,), (cb,)), ((), ())), preferred_element_type=F32)


def adjacency_kernel(count_ref, values_ref, out_ref):
    count = count_ref[pl.program_id(0), pl.program_id(1)]
    slots = values_ref.shape[2]
    live, degree = [], None
    for s in range(slots):
        v = values_ref[0, :, s, :]
        v = jnp.where(s < count, v, jnp.zeros_like(v)).astype(F32)
        live.append(v)
        degree = v if degree is None else degree + v
    total = jnp.sum(degree, axis=1, keepdims=True)
    scale = 1.0 / jnp.sqrt(jnp.maximum(total, 1.0))
    for s in range(slots):
        out_ref[0, :, s * BLK : (s + 1) * BLK] = (live[s] * scale).astype(BF16)


def adjacency_of(tile_values, tile_count):
    rels, rows, slots, cols = tile_values.shape
    return pl.pallas_call(
        adjacency_kernel,
        grid=(rels, rows // BLK),
        in_specs=[smem(), pl.BlockSpec((1, BLK, slots, cols), lambda r, q: (r, q, 0, 0))],
        out_specs=pl.BlockSpec((1, BLK, slots * cols), lambda r, q: (r, q, 0)),
        out_shape=jax.ShapeDtypeStruct((rels, rows, slots * cols), BF16),
        compiler_params=params("arbitrary", "arbitrary"),
        name="adjacency",
    )(tile_count, tile_values)


def outgoing_kernel(place_ref, table_ref, features_ref, out_ref, turned_ref):
    owner, first = place_ref[0], place_ref[1]
    turned_ref[...] = features_ref[...].T
    piece = turned_ref[pl.ds(pl.multiple_of(first, 64), 192), :]
    block0, block1 = piece[:, :BLK], piece[:, BLK:]
    for t in range(out_ref.shape[0]):
        k = table_ref[t, owner]
        picked = jnp.where(k == 1, block1, block0)
        out_ref[t] = jnp.where(k >= 0, picked, jnp.zeros_like(picked))


def outgoing_of(features, source_blocks, place):
    rows, width = features.shape
    return pl.pallas_call(
        outgoing_kernel,
        in_specs=[smem(), smem(), vmem()],
        out_specs=vmem(),
        out_shape=jax.ShapeDtypeStruct((source_blocks.shape[0], 192, BLK), BF16),
        scratch_shapes=[pltpu.VMEM((width, rows), BF16)],
        compiler_params=params(),
        name="outgoing",
    )(place, source_blocks, features)


ORDER = (0, 1, 3, 2)


def start_loads(adj_refs, adj_buf, sems):
    own, back, fore, far0, far1 = adj_refs
    loads = []
    for n, ref in enumerate((own, back, fore)):
        loads.append([pltpu.make_async_copy(ref, adj_buf.at[pl.ds(2 * n, 2)], sems.at[n])])
    loads.append(
        [pltpu.make_async_copy(ref, adj_buf.at[pl.ds(6 + n, 1)], sems.at[3 + n]) for n, ref in enumerate((far0, far1))]
    )
    for group in loads:
        for load in group:
            load.start()
    return loads


def load_scratch(rows, wide):
    return [pltpu.VMEM((8, rows, wide), BF16), pltpu.SemaphoreType.DMA((5,))]


def hbm():
    return pl.BlockSpec(memory_space=pltpu.MemorySpace.HBM)


def forward_kernel(
    place_ref, slot_ref, own_ref, back_ref, fore_ref, far0_ref, far1_ref, fetched_ref, w_mine_ref, w_theirs_ref,
    keep_ref, keep_far_ref, send_ref, send_far_ref, pre_ref, adj_buf, sems, both_ref, acc_ref,
):
    core, y = place_ref[2], place_ref[3]
    loads = start_loads((own_ref, back_ref, fore_ref, far0_ref, far1_ref), adj_buf, sems)
    for n, k in enumerate(ORDER):
        for load in loads[n]:
            load.wait()
        for p in range(2):
            for q in range(2):
                base = ((k * 2 + p) * 2 + q) * 8
                wide = jnp.concatenate([fetched_ref[slot_ref[base + s]] for s in range(8)], axis=1)
                part = adj_buf[2 * n + p, q * BLK : (q + 1) * BLK, :]
                both_ref[p, :, q * BLK : (q + 1) * BLK] = dot(wide, part, 1, 1).astype(BF16)
        j = (y - k) & 3
        far, pair = (j >> 1) ^ place_ref[4], pl.ds(2 * (j & 1), 2)
        keep = both_ref[:, pl.ds(pl.multiple_of(96 * core, 32), 96)]
        send = both_ref[:, pl.ds(pl.multiple_of(96 * (1 - core), 32), 96)]

        @pl.when(far == 0)
        def _():
            keep_ref[pair] = keep
            send_ref[pair] = send

        @pl.when(far == 1)
        def _():
            keep_far_ref[pair] = keep
            send_far_ref[pair] = send

        term = dot(w_mine_ref[k], both_ref[core], 0, 0) + dot(w_theirs_ref[k], both_ref[1 - core], 0, 0)
        if n == 0:
            acc_ref[...] = term
        elif n < 3:
            acc_ref[...] += term
        else:
            pre_ref[...] = (acc_ref[...] + term).astype(BF16)


def forward_of(place, slots, adjacency, fetched, w_mine, w_theirs):
    _, rows, wide = adjacency[0].shape
    width = w_mine.shape[2]
    half = pltpu.MemorySpace.HBM((4, 96, rows), BF16)
    return pl.pallas_call(
        forward_kernel,
        in_specs=[smem(), smem()] + [hbm()] * 5 + [vmem()] * 3,
        out_specs=[vmem()] * 5,
        out_shape=[half, half, half, half, jax.ShapeDtypeStruct((width, rows), BF16)],
        scratch_shapes=load_scratch(rows, wide)
        + [pltpu.VMEM((2, 192, rows), BF16), pltpu.VMEM((width, rows), F32)],
        compiler_params=params(),
        name="forward",
    )(place, slots, *adjacency, fetched, w_mine, w_theirs)


def activation_kernel(arrived_ref, bias_ref, cotangent_ref, act_ref, grad_ref):
    pre = bias_ref[...]
    for g in range(arrived_ref.shape[0]):
        pre = pre + arrived_ref[g].astype(F32)
    sigmoid = jax.nn.sigmoid(pre)
    act_ref[...] = (pre * sigmoid).astype(BF16)
    derivative = sigmoid * (1.0 + pre * (1.0 - sigmoid))
    grad = (cotangent_ref[...].astype(F32) * derivative).astype(BF16)
    for g in range(grad_ref.shape[0]):
        grad_ref[g] = grad


def activation_of(arrived, bias, cotangent):
    return pl.pallas_call(
        activation_kernel,
        in_specs=[vmem()] * 3,
        out_specs=[vmem()] * 2,
        out_shape=[
            jax.ShapeDtypeStruct(arrived.shape[1:], BF16),
            jax.ShapeDtypeStruct(arrived.shape, BF16),
        ],
        compiler_params=params(),
        name="activation",
    )(arrived, bias, cotangent)


def backward_kernel(
    place_ref, slot_ref, own_ref, back_ref, fore_ref, far0_ref, far1_ref, grad_ref, w_mine_ref, w_theirs_ref,
    out_ref, adj_buf, sems, both_ref, acc_ref,
):
    core = place_ref[2]
    loads = start_loads((own_ref, back_ref, fore_ref, far0_ref, far1_ref), adj_buf, sems)
    acc_ref[...] = jnp.zeros_like(acc_ref)
    for n, k in enumerate(ORDER):
        both_ref[core] = dot(w_mine_ref[k], grad_ref[...], 1, 0).astype(BF16)
        both_ref[1 - core] = dot(w_theirs_ref[k], grad_ref[...], 1, 0).astype(BF16)
        for load in loads[n]:
            load.wait()
        for p in range(2):
            for q in range(2):
                base = ((k * 2 + p) * 2 + q) * 8
                part = adj_buf[2 * n + p, q * BLK : (q + 1) * BLK, :]
                wide = dot(both_ref[p, :, q * BLK : (q + 1) * BLK], part, 1, 0)
                for s in range(8):
                    acc_ref[slot_ref[base + s]] += wide[:, s * BLK : (s + 1) * BLK]
    out_ref[...] = acc_ref[...].astype(BF16)


def backward_of(place, slots, adjacency, grads, w_mine, w_theirs, owners):
    _, rows, wide = adjacency[0].shape
    return pl.pallas_call(
        backward_kernel,
        in_specs=[smem(), smem()] + [hbm()] * 5 + [vmem()] * 3,
        out_specs=vmem(),
        out_shape=jax.ShapeDtypeStruct((owners, 192, BLK), BF16),
        scratch_shapes=load_scratch(rows, wide)
        + [pltpu.VMEM((2, 192, rows), BF16), pltpu.VMEM((owners, 192, BLK), F32)],
        compiler_params=params(),
        name="backward",
    )(place, slots, *adjacency, grads, w_mine, w_theirs)


def weight_kernel(
    place_ref, own_ref, core_ref, far_ref, far_core_ref, grad_ref, core_grad_ref, far_grad_ref, far_core_grad_ref, *refs
):
    *out_refs, pieces_ref = refs
    z = place_ref[5]
    grads = jnp.concatenate(
        [grad_ref[...], core_grad_ref[...], far_grad_ref[...], far_core_grad_ref[...]], axis=1
    )
    for r in range(4):
        wide = jnp.concatenate([own_ref[r], core_ref[r], far_ref[r], far_core_ref[r]], axis=1)
        term = dot(wide, grads, 1, 1)
        for m in range(4):
            part = slice(24 * (r % 2), 24 * (r % 2) + 24)
            pieces_ref[4 * (r // 2) + m, part] = term[m * 24 : (m + 1) * 24]
    for k, out_ref in enumerate(out_refs):
        out_ref[...] = pieces_ref[z ^ k].astype(out_ref.dtype)


def weight_terms_of(place, *operands):
    width = operands[-1].shape[0]
    return pl.pallas_call(
        weight_kernel,
        in_specs=[smem()] + [vmem()] * 8,
        out_specs=[vmem()] * 8,
        out_shape=[jax.ShapeDtypeStruct((48, width), F32 if k == 0 else BF16) for k in range(8)],
        scratch_shapes=[pltpu.VMEM((8, 48, width), F32)],
        compiler_params=params(),
        name="weight_terms",
        cost_estimate=pl.CostEstimate(flops=24500000000, transcendentals=0, bytes_accessed=0),
    )(place, *operands)


def owned_kernel(place_ref, table_ref, arrived_ref, out_ref):
    owner = place_ref[0]
    zero = jnp.zeros(arrived_ref.shape[1:], F32)
    sums = [zero, zero]
    for t in range(arrived_ref.shape[0]):
        k = table_ref[t, owner]
        v = arrived_ref[t].astype(F32)
        for b in range(2):
            sums[b] = sums[b] + jnp.where(k == b, v, zero)
    for b in range(2):
        turned = sums[b].T
        for g in range(out_ref.shape[0]):
            out_ref[g, b] = turned[g * 16 : (g + 1) * 16, :]


def owned_of(place, source_blocks, arrived, groups):
    return pl.pallas_call(
        owned_kernel,
        in_specs=[smem(), smem(), vmem()],
        out_specs=vmem(),
        out_shape=jax.ShapeDtypeStruct((groups, 2, BLK // groups, arrived.shape[1]), F32),
        compiler_params=params(),
        name="owned",
    )(place, source_blocks, arrived)


def step(value, by):
    return lax.ppermute(value, "y", [(i, (i + by) % 4) for i in range(4)])


def swap(value, axis, size=2, flip=1):
    return lax.ppermute(value, axis, [(i, i ^ flip) for i in range(size)])


def exchange(value, axis):
    return lax.all_to_all(value, axis, 0, 0, tiled=True)


def around(values, axis, size):
    return [
        lax.ppermute(v, axis, [(i, (i + k) % size) for i in range(size)])
        for k, v in enumerate(values, 1)
    ]


def to_owner():
    def place(y, xh, z, c):
        return ((y * 2 + xh) * 8 + z) * 2 + c
    moves = []
    for y in range(4):
        for xh in range(2):
            for z in range(8):
                for c in range(2):
                    m = 4 * c + z % 4
                    target = place(2 * xh + z // 4, y // 2, 4 * (y % 2) + m // 2, m % 2)
                    moves.append((place(y, xh, z, c), target))
    return moves


def per_device(
    features, weights, bias, cotangent, tile_values, tile_count, tile_slot, source_blocks
):
    groups = 8
    owners = source_blocks.shape[0]
    width = features.shape[1]
    xl, y, core = lax.axis_index("xl"), lax.axis_index("y"), lax.axis_index("core")
    owner = lax.axis_index(TGT)
    group = lax.axis_index(REL)
    xh, z = lax.axis_index("xh"), lax.axis_index("z")
    xh, z = lax.axis_index("xh"), lax.axis_index("z")
    place = in_hbm(jnp.stack([owner, 192 * y, core, y, xh, z]).astype(jnp.int32))

    own = adjacency_of(in_hbm(tile_values), in_hbm(tile_count))
    back, fore = step(own, 1), step(own, -1)
    features, weights, _ = lax.optimization_barrier((features, weights, own))
    source_blocks = in_hbm(source_blocks)
    outgoing = outgoing_of(in_hbm(features), source_blocks, place)
    fetched = resident(exchange(outgoing, TGT))

    own_slots = jnp.pad(tile_slot.reshape(1, 1, -1), ((0, 0), (0, 15), (0, width - 32))).astype(BF16)
    pieces = []
    for k in range(4):
        cut = lax.dynamic_slice(weights, (core, ((y + k) & 3) * 192 + 96 * xh, 0), (1, 96, width))
        pieces.append(jnp.concatenate([cut, own_slots], axis=1) if k else cut)
    came = around(pieces[1:], "y", 4)
    slots = jnp.concatenate([tile_slot.reshape(-1)] + [c[0, 96, :32].astype(jnp.int32) for c in came])
    share = width // groups
    bias_share = lax.dynamic_slice_in_dim(bias, group * share, share)
    bias_share = jnp.broadcast_to(bias_share[:, None], (share, features.shape[0]))
    cotangent_share = lax.dynamic_slice_in_dim(cotangent, group * share, share, 1).T
    back, fore, slots, bias_share, cotangent_share = lax.optimization_barrier(
        (back, fore, slots, bias_share, cotangent_share)
    )
    slots, bias_share, cotangent_share = in_hbm(slots), in_hbm(bias_share), in_hbm(cotangent_share)
    far0, far1 = step(back[:1], 1), step(fore[1:], -1)
    w_part = jnp.concatenate([pieces[0]] + [c[:, :96] for c in came], axis=0)
    w_other = swap(w_part, "xh")
    w_part, w_other, far0, far1 = lax.optimization_barrier((w_part, w_other, far0, far1))
    w_mine = jnp.concatenate(
        [jnp.where(xh == 0, w_part, w_other), jnp.where(xh == 0, w_other, w_part)], axis=1
    )
    w_mine, w_theirs = resident(w_mine), resident(swap(w_mine, "core"))
    adjacency = [in_hbm(a) for a in (own, back, fore, far0, far1)]

    own_terms, far_terms, for_core, for_far_core, part = forward_of(
        place, slots, adjacency, fetched, w_mine, w_theirs
    )
    of_core, of_far = swap(for_core, "core"), swap(far_terms, "xh")
    of_far_core = swap(for_far_core, "core")
    arrived, of_far_core = lax.optimization_barrier((exchange(part.reshape(groups, share, -1), REL), of_far_core))
    arrived = resident(arrived)
    activated, grad_copies = activation_of(arrived, bias_share, cotangent_share)
    output = activated.T
    of_far_core = swap(of_far_core, "xh")
    grad_copies, of_far = lax.optimization_barrier((grad_copies, of_far))
    grads, of_core, of_far_core = lax.optimization_barrier(
        (exchange(grad_copies, REL).reshape(width, -1), of_core, of_far_core)
    )
    of_core, of_far, of_far_core = in_hbm(of_core), in_hbm(of_far), in_hbm(of_far_core)
    partial = backward_of(place, slots, adjacency, resident(grads), w_mine, w_theirs, owners)
    returned = resident(exchange(in_hbm(partial), TGT))
    cut = owned_of(place, source_blocks, returned, groups)
    columns = exchange(cut, REL).reshape(2, 4, 2, BLK // groups, 192).sum(axis=0)
    grad_features = columns.transpose(1, 2, 0, 3).reshape(2, BLK // groups, width)

    far_grads, _ = lax.optimization_barrier((swap(grads, "xh"), partial))
    piece, *others = weight_terms_of(
        place, own_terms, of_core, of_far, of_far_core,
        grads, swap(grads, "core"), far_grads, swap(far_grads, "core"),
    )
    for k, other in enumerate(others, 1):
        piece = piece + swap(other, "z", 8, k).astype(F32)
    grad_weights = lax.ppermute(piece.reshape(2, 24, width), ("y", *TGT), to_owner())
    return (output, grad_weights, grad_features)


def solution(mesh):
    fine = Mesh(mesh.devices.reshape(2, 4, 2, 8, 2), (*REL, *TGT))
    placed = (
        P(TGT, None),
        P(REL, None, None),
        P(),
        P(TGT, None),
        P(REL, TGT, None, None),
        P(REL, TGT),
        P(REL, TGT, None),
        P(),
    )
    return jax.shard_map(
        per_device,
        mesh=fine,
        in_specs=placed,
        out_specs=(P(TGT, REL), P(REL, TGT, None), P(TGT, REL, None)),
        check_vma=False,
    )
```

```python
import functools

import jax
import jax.numpy as jnp
from jax import lax
from jax.experimental import pallas as pl
from jax.experimental.pallas import tpu as pltpu
from jax.sharding import Mesh, PartitionSpec as P

F32 = jnp.float32
BF16 = jnp.bfloat16
BLK = 128
REL = ("xl", "y")
TGT = ("xh", "z", "core")
VMEM_LIMIT = 44 * 1024 * 1024


def in_hbm(value):
    return pltpu.with_memory_space_constraint(value, pltpu.MemorySpace.HBM)


def resident(value):
    return pltpu.with_memory_space_constraint(value, pltpu.MemorySpace.VMEM)


def params(*semantics):
    return pltpu.CompilerParams(
        dimension_semantics=semantics or None, vmem_limit_bytes=VMEM_LIMIT
    )


def smem():
    return pl.BlockSpec(memory_space=pltpu.MemorySpace.SMEM)


def vmem():
    return pl.BlockSpec(memory_space=pltpu.MemorySpace.VMEM)


def dot(a, b, ca, cb):
    return lax.dot_general(a, b, (((ca,), (cb,)), ((), ())), preferred_element_type=F32)


def adjacency_kernel(count_ref, values_ref, out_ref):
    count = count_ref[pl.program_id(0), pl.program_id(1)]
    slots = values_ref.shape[2]
    live, degree = [], None
    for s in range(slots):
        v = values_ref[0, :, s, :]
        v = jnp.where(s < count, v, jnp.zeros_like(v)).astype(F32)
        live.append(v)
        degree = v if degree is None else degree + v
    total = jnp.sum(degree, axis=1, keepdims=True)
    scale = 1.0 / jnp.sqrt(jnp.maximum(total, 1.0))
    for s in range(slots):
        out_ref[0, :, s * BLK : (s + 1) * BLK] = (live[s] * scale).astype(BF16)


def adjacency_of(tile_values, tile_count):
    rels, rows, slots, cols = tile_values.shape
    return pl.pallas_call(
        adjacency_kernel,
        grid=(rels, rows // BLK),
        in_specs=[smem(), pl.BlockSpec((1, BLK, slots, cols), lambda r, q: (r, q, 0, 0))],
        out_specs=pl.BlockSpec((1, BLK, slots * cols), lambda r, q: (r, q, 0)),
        out_shape=jax.ShapeDtypeStruct((rels, rows, slots * cols), BF16),
        compiler_params=params("arbitrary", "arbitrary"),
        name="adjacency",
    )(tile_count, tile_values)


def outgoing_kernel(place_ref, table_ref, features_ref, out_ref, turned_ref):
    owner, first = place_ref[0], place_ref[1]
    turned_ref[...] = features_ref[...].T
    piece = turned_ref[pl.ds(pl.multiple_of(first, 64), 192), :]
    block0, block1 = piece[:, :BLK], piece[:, BLK:]
    for t in range(out_ref.shape[0]):
        k = table_ref[t, owner]
        picked = jnp.where(k == 1, block1, block0)
        out_ref[t] = jnp.where(k >= 0, picked, jnp.zeros_like(picked))


def outgoing_of(features, source_blocks, place):
    rows, width = features.shape
    return pl.pallas_call(
        outgoing_kernel,
        in_specs=[smem(), smem(), vmem()],
        out_specs=vmem(),
        out_shape=jax.ShapeDtypeStruct((source_blocks.shape[0], 192, BLK), BF16),
        scratch_shapes=[pltpu.VMEM((width, rows), BF16)],
        compiler_params=params(),
        name="outgoing",
    )(place, source_blocks, features)


ORDER = (0, 1, 3, 2)


def start_loads(adj_refs, adj_buf, sems):
    own, back, fore, far0, far1 = adj_refs
    loads = []
    for n, ref in enumerate((own, back, fore)):
        loads.append([pltpu.make_async_copy(ref, adj_buf.at[pl.ds(2 * n, 2)], sems.at[n])])
    loads.append(
        [pltpu.make_async_copy(ref, adj_buf.at[pl.ds(6 + n, 1)], sems.at[3 + n]) for n, ref in enumerate((far0, far1))]
    )
    for group in loads:
        for load in group:
            load.start()
    return loads


def load_scratch(rows, wide):
    return [pltpu.VMEM((8, rows, wide), BF16), pltpu.SemaphoreType.DMA((5,))]


def hbm():
    return pl.BlockSpec(memory_space=pltpu.MemorySpace.HBM)


def join_kernel(own_ref, own_slots_ref, came1_ref, came2_ref, came3_ref, part_ref, slots_ref):
    part_ref[0] = own_ref[0]
    slots_ref[0:1] = own_slots_ref[0, :, :BLK].astype(F32).astype(jnp.int32)[0:1]
    for k, ref in enumerate((came1_ref, came2_ref, came3_ref), 1):
        part_ref[k] = ref[0, :96]
        slots_ref[k : k + 1] = ref[0, 96:, :BLK].astype(F32).astype(jnp.int32)[0:1]


def join(own, own_slots, came):
    return pl.pallas_call(
        join_kernel,
        in_specs=[vmem()] * 5,
        out_specs=[vmem(), vmem()],
        out_shape=[
            jax.ShapeDtypeStruct((4, *own.shape[1:]), BF16),
            jax.ShapeDtypeStruct((4, BLK), jnp.int32),
        ],
        compiler_params=params(),
        name="join",
    )(own, own_slots, *came)


def forward_kernel(
    place_ref, slot_ref, own_ref, back_ref, fore_ref, far0_ref, far1_ref, fetched_ref, w_mine_ref, w_theirs_ref,
    keep_ref, keep_far_ref, send_ref, send_far_ref, pre_ref, adj_buf, sems, both_ref, acc_ref,
):
    core, y = place_ref[2], place_ref[3]
    loads = start_loads((own_ref, back_ref, fore_ref, far0_ref, far1_ref), adj_buf, sems)
    for n, k in enumerate(ORDER):
        for load in loads[n]:
            load.wait()
        for p in range(2):
            for q in range(2):
                base = (p * 2 + q) * 8
                wide = jnp.concatenate([fetched_ref[slot_ref[k, base + s]] for s in range(8)], axis=1)
                part = adj_buf[2 * n + p, q * BLK : (q + 1) * BLK, :]
                both_ref[p, :, q * BLK : (q + 1) * BLK] = dot(wide, part, 1, 1).astype(BF16)
        j = (y - k) & 3
        far, pair = (j >> 1) ^ place_ref[4], pl.ds(2 * (j & 1), 2)
        keep = both_ref[:, pl.ds(pl.multiple_of(96 * core, 32), 96)]
        send = both_ref[:, pl.ds(pl.multiple_of(96 * (1 - core), 32), 96)]

        @pl.when(far == 0)
        def _():
            keep_ref[pair] = keep
            send_ref[pair] = send

        @pl.when(far == 1)
        def _():
            keep_far_ref[pair] = keep
            send_far_ref[pair] = send

        term = dot(w_mine_ref[k], both_ref[core], 0, 0) + dot(w_theirs_ref[k], both_ref[1 - core], 0, 0)
        if n == 0:
            acc_ref[...] = term
        elif n < 3:
            acc_ref[...] += term
        else:
            pre_ref[...] = (acc_ref[...] + term).astype(BF16)


def forward_of(place, slots, adjacency, fetched, w_mine, w_theirs):
    _, rows, wide = adjacency[0].shape
    width = w_mine.shape[2]
    half = pltpu.MemorySpace.HBM((4, 96, rows), BF16)
    return pl.pallas_call(
        forward_kernel,
        in_specs=[smem(), smem()] + [hbm()] * 5 + [vmem()] * 3,
        out_specs=[vmem()] * 5,
        out_shape=[half, half, half, half, jax.ShapeDtypeStruct((width, rows), BF16)],
        scratch_shapes=load_scratch(rows, wide)
        + [pltpu.VMEM((2, 192, rows), BF16), pltpu.VMEM((width, rows), F32)],
        compiler_params=params(),
        name="forward",
    )(place, slots, *adjacency, fetched, w_mine, w_theirs)


def activation_kernel(arrived_ref, bias_ref, cotangent_ref, act_ref, grad_ref):
    pre = bias_ref[...]
    for g in range(arrived_ref.shape[0]):
        pre = pre + arrived_ref[g].astype(F32)
    sigmoid = jax.nn.sigmoid(pre)
    act_ref[...] = (pre * sigmoid).astype(BF16)
    derivative = sigmoid * (1.0 + pre * (1.0 - sigmoid))
    grad = (cotangent_ref[...].astype(F32) * derivative).astype(BF16)
    for g in range(grad_ref.shape[0]):
        grad_ref[g] = grad


def activation_of(arrived, bias, cotangent):
    return pl.pallas_call(
        activation_kernel,
        in_specs=[vmem()] * 3,
        out_specs=[vmem()] * 2,
        out_shape=[
            jax.ShapeDtypeStruct(arrived.shape[1:], BF16),
            jax.ShapeDtypeStruct(arrived.shape, BF16),
        ],
        compiler_params=params(),
        name="activation",
    )(arrived, bias, cotangent)


def backward_kernel(
    place_ref, slot_ref, own_ref, back_ref, fore_ref, far0_ref, far1_ref, grad_ref, w_mine_ref, w_theirs_ref,
    out_ref, adj_buf, sems, both_ref, acc_ref,
):
    core = place_ref[2]
    loads = start_loads((own_ref, back_ref, fore_ref, far0_ref, far1_ref), adj_buf, sems)
    acc_ref[...] = jnp.zeros_like(acc_ref)
    for n, k in enumerate(ORDER):
        both_ref[core] = dot(w_mine_ref[k], grad_ref[...], 1, 0).astype(BF16)
        both_ref[1 - core] = dot(w_theirs_ref[k], grad_ref[...], 1, 0).astype(BF16)
        for load in loads[n]:
            load.wait()
        for p in range(2):
            for q in range(2):
                base = (p * 2 + q) * 8
                part = adj_buf[2 * n + p, q * BLK : (q + 1) * BLK, :]
                wide = dot(both_ref[p, :, q * BLK : (q + 1) * BLK], part, 1, 0)
                for s in range(8):
                    acc_ref[slot_ref[k, base + s]] += wide[:, s * BLK : (s + 1) * BLK]
    out_ref[...] = acc_ref[...].astype(BF16)


def backward_of(place, slots, adjacency, grads, w_mine, w_theirs, owners):
    _, rows, wide = adjacency[0].shape
    return pl.pallas_call(
        backward_kernel,
        in_specs=[smem(), smem()] + [hbm()] * 5 + [vmem()] * 3,
        out_specs=vmem(),
        out_shape=jax.ShapeDtypeStruct((owners, 192, BLK), BF16),
        scratch_shapes=load_scratch(rows, wide)
        + [pltpu.VMEM((2, 192, rows), BF16), pltpu.VMEM((owners, 192, BLK), F32)],
        compiler_params=params(),
        name="backward",
    )(place, slots, *adjacency, grads, w_mine, w_theirs)


def weight_kernel(
    place_ref, own_ref, core_ref, far_ref, far_core_ref, grad_ref, core_grad_ref, far_grad_ref, far_core_grad_ref, *refs
):
    *out_refs, pieces_ref = refs
    z = place_ref[5]
    grads = jnp.concatenate(
        [grad_ref[...], core_grad_ref[...], far_grad_ref[...], far_core_grad_ref[...]], axis=1
    )
    for r in range(4):
        wide = jnp.concatenate([own_ref[r], core_ref[r], far_ref[r], far_core_ref[r]], axis=1)
        term = dot(wide, grads, 1, 1)
        for m in range(4):
            part = slice(24 * (r % 2), 24 * (r % 2) + 24)
            pieces_ref[4 * (r // 2) + m, part] = term[m * 24 : (m + 1) * 24]
    for k, out_ref in enumerate(out_refs):
        out_ref[...] = pieces_ref[z ^ k].astype(out_ref.dtype)


def weight_terms_of(place, *operands):
    width = operands[-1].shape[0]
    return pl.pallas_call(
        weight_kernel,
        in_specs=[smem()] + [vmem()] * 8,
        out_specs=[vmem()] * 8,
        out_shape=[jax.ShapeDtypeStruct((48, width), F32 if k == 0 else BF16) for k in range(8)],
        scratch_shapes=[pltpu.VMEM((8, 48, width), F32)],
        compiler_params=params(),
        name="weight_terms",
        cost_estimate=pl.CostEstimate(flops=24500000000, transcendentals=0, bytes_accessed=0),
    )(place, *operands)


def owned_kernel(place_ref, table_ref, arrived_ref, out_ref):
    owner = place_ref[0]
    zero = jnp.zeros(arrived_ref.shape[1:], F32)
    sums = [zero, zero]
    for t in range(arrived_ref.shape[0]):
        k = table_ref[t, owner]
        v = arrived_ref[t].astype(F32)
        for b in range(2):
            sums[b] = sums[b] + jnp.where(k == b, v, zero)
    for b in range(2):
        turned = sums[b].T
        for g in range(out_ref.shape[0]):
            out_ref[g, b] = turned[g * 16 : (g + 1) * 16, :]


def owned_of(place, source_blocks, arrived, groups):
    return pl.pallas_call(
        owned_kernel,
        in_specs=[smem(), smem(), vmem()],
        out_specs=vmem(),
        out_shape=jax.ShapeDtypeStruct((groups, 2, BLK // groups, arrived.shape[1]), F32),
        compiler_params=params(),
        name="owned",
    )(place, source_blocks, arrived)


def step(value, by):
    return lax.ppermute(value, "y", [(i, (i + by) % 4) for i in range(4)])


def swap(value, axis, size=2, flip=1):
    return lax.ppermute(value, axis, [(i, i ^ flip) for i in range(size)])


def exchange(value, axis):
    return lax.all_to_all(value, axis, 0, 0, tiled=True)


def around(values, axis, size):
    return [
        lax.ppermute(v, axis, [(i, (i + k) % size) for i in range(size)])
        for k, v in enumerate(values, 1)
    ]


def to_owner():
    def place(y, xh, z, c):
        return ((y * 2 + xh) * 8 + z) * 2 + c
    moves = []
    for y in range(4):
        for xh in range(2):
            for z in range(8):
                for c in range(2):
                    m = 4 * c + z % 4
                    target = place(2 * xh + z // 4, y // 2, 4 * (y % 2) + m // 2, m % 2)
                    moves.append((place(y, xh, z, c), target))
    return moves


def per_device(
    features, weights, bias, cotangent, tile_values, tile_count, tile_slot, source_blocks
):
    groups = 8
    owners = source_blocks.shape[0]
    width = features.shape[1]
    xl, y, core = lax.axis_index("xl"), lax.axis_index("y"), lax.axis_index("core")
    owner = lax.axis_index(TGT)
    group = lax.axis_index(REL)
    xh, z = lax.axis_index("xh"), lax.axis_index("z")
    xh, z = lax.axis_index("xh"), lax.axis_index("z")
    place = in_hbm(jnp.stack([owner, 192 * y, core, y, xh, z]).astype(jnp.int32))

    own = adjacency_of(in_hbm(tile_values), in_hbm(tile_count))
    back, fore = step(own, 1), step(own, -1)
    features, weights, _ = lax.optimization_barrier((features, weights, own))
    source_blocks = in_hbm(source_blocks)
    outgoing = outgoing_of(in_hbm(features), source_blocks, place)
    fetched = resident(exchange(outgoing, TGT))

    own_slots = jnp.pad(tile_slot.reshape(1, 1, -1), ((0, 0), (0, 15), (0, width - 32))).astype(BF16)
    pieces = []
    for k in range(4):
        cut = lax.dynamic_slice(weights, (core, ((y + k) & 3) * 192 + 96 * xh, 0), (1, 96, width))
        pieces.append(jnp.concatenate([cut, own_slots], axis=1) if k else cut)
    came = around(pieces[1:], "y", 4)
    share = width // groups
    bias_share = lax.dynamic_slice_in_dim(bias, group * share, share)
    bias_share = jnp.broadcast_to(bias_share[:, None], (share, features.shape[0]))
    cotangent_share = lax.dynamic_slice_in_dim(cotangent, group * share, share, 1).T
    w_part, slots = join(pieces[0], own_slots, came)
    w_part, bias_share, cotangent_share = lax.optimization_barrier((w_part, bias_share, cotangent_share))
    slots, bias_share, cotangent_share = in_hbm(slots), in_hbm(bias_share), in_hbm(cotangent_share)
    far0, far1 = step(back[:1], 1), step(fore[1:], -1)
    w_other = swap(w_part, "xh")
    w_part, w_other, far0, far1 = lax.optimization_barrier((w_part, w_other, far0, far1))
    w_mine = jnp.concatenate(
        [jnp.where(xh == 0, w_part, w_other), jnp.where(xh == 0, w_other, w_part)], axis=1
    )
    w_mine, w_theirs = resident(w_mine), resident(swap(w_mine, "core"))
    adjacency = [in_hbm(a) for a in (own, back, fore, far0, far1)]

    own_terms, far_terms, for_core, for_far_core, part = forward_of(
        place, slots, adjacency, fetched, w_mine, w_theirs
    )
    of_core, of_far = swap(for_core, "core"), swap(far_terms, "xh")
    of_far_core = swap(for_far_core, "core")
    arrived, of_far_core = lax.optimization_barrier((exchange(part.reshape(groups, share, -1), REL), of_far_core))
    arrived = resident(arrived)
    activated, grad_copies = activation_of(arrived, bias_share, cotangent_share)
    output = activated.T
    of_far_core = swap(of_far_core, "xh")
    grad_copies, of_far = lax.optimization_barrier((grad_copies, of_far))
    grads, of_core, of_far_core = lax.optimization_barrier(
        (exchange(grad_copies, REL).reshape(width, -1), of_core, of_far_core)
    )
    of_core, of_far, of_far_core = in_hbm(of_core), in_hbm(of_far), in_hbm(of_far_core)
    partial = backward_of(place, slots, adjacency, resident(grads), w_mine, w_theirs, owners)
    returned = resident(exchange(in_hbm(partial), TGT))
    cut = owned_of(place, source_blocks, returned, groups)
    columns = exchange(cut, REL).reshape(2, 4, 2, BLK // groups, 192).sum(axis=0)
    grad_features = columns.transpose(1, 2, 0, 3).reshape(2, BLK // groups, width)

    far_grads, _ = lax.optimization_barrier((swap(grads, "xh"), partial))
    piece, *others = weight_terms_of(
        place, own_terms, of_core, of_far, of_far_core,
        grads, swap(grads, "core"), far_grads, swap(far_grads, "core"),
    )
    for k, other in enumerate(others, 1):
        piece = piece + swap(other, "z", 8, k).astype(F32)
    grad_weights = lax.ppermute(piece.reshape(2, 24, width), ("y", *TGT), to_owner())
    return (output, grad_weights, grad_features)


def solution(mesh):
    fine = Mesh(mesh.devices.reshape(2, 4, 2, 8, 2), (*REL, *TGT))
    placed = (
        P(TGT, None),
        P(REL, None, None),
        P(),
        P(TGT, None),
        P(REL, TGT, None, None),
        P(REL, TGT),
        P(REL, TGT, None),
        P(),
    )
    return jax.shard_map(
        per_device,
        mesh=fine,
        in_specs=placed,
        out_specs=(P(TGT, REL), P(REL, TGT, None), P(TGT, REL, None)),
        check_vma=False,
    )
```

```python
import functools

import jax
import jax.numpy as jnp
from jax import lax
from jax.experimental import pallas as pl
from jax.experimental.pallas import tpu as pltpu
from jax.sharding import Mesh, PartitionSpec as P

F32 = jnp.float32
BF16 = jnp.bfloat16
BLK = 128
REL = ("xl", "y")
TGT = ("xh", "z", "core")
VMEM_LIMIT = 44 * 1024 * 1024


def in_hbm(value):
    return pltpu.with_memory_space_constraint(value, pltpu.MemorySpace.HBM)


def resident(value):
    return pltpu.with_memory_space_constraint(value, pltpu.MemorySpace.VMEM)


def params(*semantics):
    return pltpu.CompilerParams(
        dimension_semantics=semantics or None, vmem_limit_bytes=VMEM_LIMIT
    )


def smem():
    return pl.BlockSpec(memory_space=pltpu.MemorySpace.SMEM)


def vmem():
    return pl.BlockSpec(memory_space=pltpu.MemorySpace.VMEM)


def dot(a, b, ca, cb):
    return lax.dot_general(a, b, (((ca,), (cb,)), ((), ())), preferred_element_type=F32)


def adjacency_kernel(count_ref, values_ref, out_ref):
    count = count_ref[pl.program_id(0), pl.program_id(1)]
    slots = values_ref.shape[2]
    live, degree = [], None
    for s in range(slots):
        v = values_ref[0, :, s, :]
        v = jnp.where(s < count, v, jnp.zeros_like(v)).astype(F32)
        live.append(v)
        degree = v if degree is None else degree + v
    total = jnp.sum(degree, axis=1, keepdims=True)
    scale = 1.0 / jnp.sqrt(jnp.maximum(total, 1.0))
    for s in range(slots):
        out_ref[0, :, s * BLK : (s + 1) * BLK] = (live[s] * scale).astype(BF16)


def adjacency_of(tile_values, tile_count):
    rels, rows, slots, cols = tile_values.shape
    return pl.pallas_call(
        adjacency_kernel,
        grid=(rels, rows // BLK),
        in_specs=[smem(), pl.BlockSpec((1, BLK, slots, cols), lambda r, q: (r, q, 0, 0))],
        out_specs=pl.BlockSpec((1, BLK, slots * cols), lambda r, q: (r, q, 0)),
        out_shape=jax.ShapeDtypeStruct((rels, rows, slots * cols), BF16),
        compiler_params=params("arbitrary", "arbitrary"),
        name="adjacency",
    )(tile_count, tile_values)


def outgoing_kernel(place_ref, table_ref, features_ref, out_ref, turned_ref):
    owner, first = place_ref[0], place_ref[1]
    turned_ref[...] = features_ref[...].T
    piece = turned_ref[pl.ds(pl.multiple_of(first, 64), 192), :]
    block0, block1 = piece[:, :BLK], piece[:, BLK:]
    for t in range(out_ref.shape[0]):
        k = table_ref[t, owner]
        picked = jnp.where(k == 1, block1, block0)
        out_ref[t] = jnp.where(k >= 0, picked, jnp.zeros_like(picked))


def outgoing_of(features, source_blocks, place):
    rows, width = features.shape
    return pl.pallas_call(
        outgoing_kernel,
        in_specs=[smem(), smem(), vmem()],
        out_specs=vmem(),
        out_shape=jax.ShapeDtypeStruct((source_blocks.shape[0], 192, BLK), BF16),
        scratch_shapes=[pltpu.VMEM((width, rows), BF16)],
        compiler_params=params(),
        name="outgoing",
    )(place, source_blocks, features)


ORDER = (0, 1, 3, 2)


def start_loads(adj_refs, adj_buf, sems):
    own, back, fore, far0, far1 = adj_refs
    loads = []
    for n, ref in enumerate((own, back, fore)):
        loads.append([pltpu.make_async_copy(ref, adj_buf.at[pl.ds(2 * n, 2)], sems.at[n])])
    loads.append(
        [pltpu.make_async_copy(ref, adj_buf.at[pl.ds(6 + n, 1)], sems.at[3 + n]) for n, ref in enumerate((far0, far1))]
    )
    for group in loads:
        for load in group:
            load.start()
    return loads


def load_scratch(rows, wide):
    return [pltpu.VMEM((8, rows, wide), BF16), pltpu.SemaphoreType.DMA((5,))]


def hbm():
    return pl.BlockSpec(memory_space=pltpu.MemorySpace.HBM)


def join_kernel(own_slots_ref, came1_ref, came2_ref, came3_ref, part_ref, slots_ref):
    slots_ref[0:1] = own_slots_ref[0, :, :BLK].astype(F32).astype(jnp.int32)[0:1]
    for k, ref in enumerate((came1_ref, came2_ref, came3_ref), 1):
        part_ref[k - 1] = ref[0, :96]
        slots_ref[k : k + 1] = ref[0, 96:, :BLK].astype(F32).astype(jnp.int32)[0:1]


def join(own_slots, came):
    return pl.pallas_call(
        join_kernel,
        in_specs=[vmem()] * 4,
        out_specs=[vmem(), vmem()],
        out_shape=[
            jax.ShapeDtypeStruct((3, 96, came[0].shape[2]), BF16),
            jax.ShapeDtypeStruct((4, BLK), jnp.int32),
        ],
        compiler_params=params(),
        name="join",
    )(own_slots, *came)


def forward_kernel(
    place_ref, slot_ref, own_ref, back_ref, fore_ref, far0_ref, far1_ref, fetched_ref, w_mine_ref, w_theirs_ref,
    keep_ref, keep_far_ref, send_ref, send_far_ref, pre_ref, adj_buf, sems, both_ref, acc_ref,
):
    core, y = place_ref[2], place_ref[3]
    loads = start_loads((own_ref, back_ref, fore_ref, far0_ref, far1_ref), adj_buf, sems)
    for n, k in enumerate(ORDER):
        for load in loads[n]:
            load.wait()
        for p in range(2):
            for q in range(2):
                base = (p * 2 + q) * 8
                wide = jnp.concatenate([fetched_ref[slot_ref[k, base + s]] for s in range(8)], axis=1)
                part = adj_buf[2 * n + p, q * BLK : (q + 1) * BLK, :]
                both_ref[p, :, q * BLK : (q + 1) * BLK] = dot(wide, part, 1, 1).astype(BF16)
        j = (y - k) & 3
        far, pair = (j >> 1) ^ place_ref[4], pl.ds(2 * (j & 1), 2)
        keep = both_ref[:, pl.ds(pl.multiple_of(96 * core, 32), 96)]
        send = both_ref[:, pl.ds(pl.multiple_of(96 * (1 - core), 32), 96)]

        @pl.when(far == 0)
        def _():
            keep_ref[pair] = keep
            send_ref[pair] = send

        @pl.when(far == 1)
        def _():
            keep_far_ref[pair] = keep
            send_far_ref[pair] = send

        term = dot(w_mine_ref[k], both_ref[core], 0, 0) + dot(w_theirs_ref[k], both_ref[1 - core], 0, 0)
        if n == 0:
            acc_ref[...] = term
        elif n < 3:
            acc_ref[...] += term
        else:
            pre_ref[...] = (acc_ref[...] + term).astype(BF16)


def forward_of(place, slots, adjacency, fetched, w_mine, w_theirs):
    _, rows, wide = adjacency[0].shape
    width = w_mine.shape[2]
    half = pltpu.MemorySpace.HBM((4, 96, rows), BF16)
    return pl.pallas_call(
        forward_kernel,
        in_specs=[smem(), smem()] + [hbm()] * 5 + [vmem()] * 3,
        out_specs=[vmem()] * 5,
        out_shape=[half, half, half, half, jax.ShapeDtypeStruct((width, rows), BF16)],
        scratch_shapes=load_scratch(rows, wide)
        + [pltpu.VMEM((2, 192, rows), BF16), pltpu.VMEM((width, rows), F32)],
        compiler_params=params(),
        name="forward",
    )(place, slots, *adjacency, fetched, w_mine, w_theirs)


def activation_kernel(arrived_ref, bias_ref, cotangent_ref, act_ref, grad_ref):
    pre = bias_ref[...]
    for g in range(arrived_ref.shape[0]):
        pre = pre + arrived_ref[g].astype(F32)
    sigmoid = jax.nn.sigmoid(pre)
    act_ref[...] = (pre * sigmoid).astype(BF16)
    derivative = sigmoid * (1.0 + pre * (1.0 - sigmoid))
    grad = (cotangent_ref[...].astype(F32) * derivative).astype(BF16)
    for g in range(grad_ref.shape[0]):
        grad_ref[g] = grad


def activation_of(arrived, bias, cotangent):
    return pl.pallas_call(
        activation_kernel,
        in_specs=[vmem()] * 3,
        out_specs=[vmem()] * 2,
        out_shape=[
            jax.ShapeDtypeStruct(arrived.shape[1:], BF16),
            jax.ShapeDtypeStruct(arrived.shape, BF16),
        ],
        compiler_params=params(),
        name="activation",
    )(arrived, bias, cotangent)


def backward_kernel(
    place_ref, slot_ref, own_ref, back_ref, fore_ref, far0_ref, far1_ref, grad_ref, w_mine_ref, w_theirs_ref,
    out_ref, adj_buf, sems, both_ref, acc_ref,
):
    core = place_ref[2]
    loads = start_loads((own_ref, back_ref, fore_ref, far0_ref, far1_ref), adj_buf, sems)
    acc_ref[...] = jnp.zeros_like(acc_ref)
    for n, k in enumerate(ORDER):
        both_ref[core] = dot(w_mine_ref[k], grad_ref[...], 1, 0).astype(BF16)
        both_ref[1 - core] = dot(w_theirs_ref[k], grad_ref[...], 1, 0).astype(BF16)
        for load in loads[n]:
            load.wait()
        for p in range(2):
            for q in range(2):
                base = (p * 2 + q) * 8
                part = adj_buf[2 * n + p, q * BLK : (q + 1) * BLK, :]
                wide = dot(both_ref[p, :, q * BLK : (q + 1) * BLK], part, 1, 0)
                for s in range(8):
                    acc_ref[slot_ref[k, base + s]] += wide[:, s * BLK : (s + 1) * BLK]
    out_ref[...] = acc_ref[...].astype(BF16)


def backward_of(place, slots, adjacency, grads, w_mine, w_theirs, owners):
    _, rows, wide = adjacency[0].shape
    return pl.pallas_call(
        backward_kernel,
        in_specs=[smem(), smem()] + [hbm()] * 5 + [vmem()] * 3,
        out_specs=vmem(),
        out_shape=jax.ShapeDtypeStruct((owners, 192, BLK), BF16),
        scratch_shapes=load_scratch(rows, wide)
        + [pltpu.VMEM((2, 192, rows), BF16), pltpu.VMEM((owners, 192, BLK), F32)],
        compiler_params=params(),
        name="backward",
    )(place, slots, *adjacency, grads, w_mine, w_theirs)


def weight_kernel(
    place_ref, own_ref, core_ref, far_ref, far_core_ref, grad_ref, core_grad_ref, far_grad_ref, far_core_grad_ref, *refs
):
    *out_refs, pieces_ref = refs
    z = place_ref[5]
    grads = jnp.concatenate(
        [grad_ref[...], core_grad_ref[...], far_grad_ref[...], far_core_grad_ref[...]], axis=1
    )
    for r in range(4):
        wide = jnp.concatenate([own_ref[r], core_ref[r], far_ref[r], far_core_ref[r]], axis=1)
        term = dot(wide, grads, 1, 1)
        for m in range(4):
            part = slice(24 * (r % 2), 24 * (r % 2) + 24)
            pieces_ref[4 * (r // 2) + m, part] = term[m * 24 : (m + 1) * 24]
    for k, out_ref in enumerate(out_refs):
        out_ref[...] = pieces_ref[z ^ k].astype(out_ref.dtype)


def weight_terms_of(place, *operands):
    width = operands[-1].shape[0]
    return pl.pallas_call(
        weight_kernel,
        in_specs=[smem()] + [vmem()] * 8,
        out_specs=[vmem()] * 8,
        out_shape=[jax.ShapeDtypeStruct((48, width), F32 if k == 0 else BF16) for k in range(8)],
        scratch_shapes=[pltpu.VMEM((8, 48, width), F32)],
        compiler_params=params(),
        name="weight_terms",
        cost_estimate=pl.CostEstimate(flops=24500000000, transcendentals=0, bytes_accessed=0),
    )(place, *operands)


def owned_kernel(place_ref, table_ref, arrived_ref, out_ref):
    owner = place_ref[0]
    zero = jnp.zeros(arrived_ref.shape[1:], F32)
    sums = [zero, zero]
    for t in range(arrived_ref.shape[0]):
        k = table_ref[t, owner]
        v = arrived_ref[t].astype(F32)
        for b in range(2):
            sums[b] = sums[b] + jnp.where(k == b, v, zero)
    for b in range(2):
        turned = sums[b].T
        for g in range(out_ref.shape[0]):
            out_ref[g, b] = turned[g * 16 : (g + 1) * 16, :]


def owned_of(place, source_blocks, arrived, groups):
    return pl.pallas_call(
        owned_kernel,
        in_specs=[smem(), smem(), vmem()],
        out_specs=vmem(),
        out_shape=jax.ShapeDtypeStruct((groups, 2, BLK // groups, arrived.shape[1]), F32),
        compiler_params=params(),
        name="owned",
    )(place, source_blocks, arrived)


def step(value, by):
    return lax.ppermute(value, "y", [(i, (i + by) % 4) for i in range(4)])


def swap(value, axis, size=2, flip=1):
    return lax.ppermute(value, axis, [(i, i ^ flip) for i in range(size)])


def exchange(value, axis):
    return lax.all_to_all(value, axis, 0, 0, tiled=True)


def around(values, axis, size):
    return [
        lax.ppermute(v, axis, [(i, (i + k) % size) for i in range(size)])
        for k, v in enumerate(values, 1)
    ]


def to_owner():
    def place(y, xh, z, c):
        return ((y * 2 + xh) * 8 + z) * 2 + c
    moves = []
    for y in range(4):
        for xh in range(2):
            for z in range(8):
                for c in range(2):
                    m = 4 * c + z % 4
                    target = place(2 * xh + z // 4, y // 2, 4 * (y % 2) + m // 2, m % 2)
                    moves.append((place(y, xh, z, c), target))
    return moves


def per_device(
    features, weights, bias, cotangent, tile_values, tile_count, tile_slot, source_blocks
):
    groups = 8
    owners = source_blocks.shape[0]
    width = features.shape[1]
    xl, y, core = lax.axis_index("xl"), lax.axis_index("y"), lax.axis_index("core")
    owner = lax.axis_index(TGT)
    group = lax.axis_index(REL)
    xh, z = lax.axis_index("xh"), lax.axis_index("z")
    xh, z = lax.axis_index("xh"), lax.axis_index("z")
    place = in_hbm(jnp.stack([owner, 192 * y, core, y, xh, z]).astype(jnp.int32))

    own = adjacency_of(in_hbm(tile_values), in_hbm(tile_count))
    back, fore = step(own, 1), step(own, -1)
    features, weights, _ = lax.optimization_barrier((features, weights, own))
    source_blocks = in_hbm(source_blocks)
    outgoing = outgoing_of(in_hbm(features), source_blocks, place)
    fetched = resident(exchange(outgoing, TGT))

    own_slots = jnp.pad(tile_slot.reshape(1, 1, -1), ((0, 0), (0, 15), (0, width - 32))).astype(BF16)
    pieces = []
    for k in range(4):
        cut = lax.dynamic_slice(weights, (core, ((y + k) & 3) * 192 + 96 * xh, 0), (1, 96, width))
        pieces.append(jnp.concatenate([cut, own_slots], axis=1) if k else cut)
    came = around(pieces[1:], "y", 4)
    share = width // groups
    bias_share = lax.dynamic_slice_in_dim(bias, group * share, share)
    bias_share = jnp.broadcast_to(bias_share[:, None], (share, features.shape[0]))
    cotangent_share = lax.dynamic_slice_in_dim(cotangent, group * share, share, 1).T
    own_other = swap(pieces[0], "xh")
    w_rest, slots = join(own_slots, came)
    w_rest, own_other = lax.optimization_barrier((w_rest, own_other))
    w_rest, bias_share, cotangent_share = lax.optimization_barrier((w_rest, bias_share, cotangent_share))
    slots, bias_share, cotangent_share = in_hbm(slots), in_hbm(bias_share), in_hbm(cotangent_share)
    far0, far1 = step(back[:1], 1), step(fore[1:], -1)
    w_part = jnp.concatenate([pieces[0], w_rest])
    w_other = jnp.concatenate([own_other, swap(w_rest, "xh")])
    w_part, w_other, far0, far1 = lax.optimization_barrier((w_part, w_other, far0, far1))
    w_mine = jnp.concatenate(
        [jnp.where(xh == 0, w_part, w_other), jnp.where(xh == 0, w_other, w_part)], axis=1
    )
    w_mine, w_theirs = resident(w_mine), resident(swap(w_mine, "core"))
    adjacency = [in_hbm(a) for a in (own, back, fore, far0, far1)]

    own_terms, far_terms, for_core, for_far_core, part = forward_of(
        place, slots, adjacency, fetched, w_mine, w_theirs
    )
    of_core, of_far = swap(for_core, "core"), swap(far_terms, "xh")
    of_far_core = swap(for_far_core, "core")
    arrived, of_far_core = lax.optimization_barrier((exchange(part.reshape(groups, share, -1), REL), of_far_core))
    arrived = resident(arrived)
    activated, grad_copies = activation_of(arrived, bias_share, cotangent_share)
    output = activated.T
    of_far_core = swap(of_far_core, "xh")
    grad_copies, of_far = lax.optimization_barrier((grad_copies, of_far))
    grads, of_core, of_far_core = lax.optimization_barrier(
        (exchange(grad_copies, REL).reshape(width, -1), of_core, of_far_core)
    )
    of_core, of_far, of_far_core = in_hbm(of_core), in_hbm(of_far), in_hbm(of_far_core)
    partial = backward_of(place, slots, adjacency, resident(grads), w_mine, w_theirs, owners)
    returned = resident(exchange(in_hbm(partial), TGT))
    cut = owned_of(place, source_blocks, returned, groups)
    columns = exchange(cut, REL).reshape(2, 4, 2, BLK // groups, 192).sum(axis=0)
    grad_features = columns.transpose(1, 2, 0, 3).reshape(2, BLK // groups, width)

    far_grads, _ = lax.optimization_barrier((swap(grads, "xh"), partial))
    piece, *others = weight_terms_of(
        place, own_terms, of_core, of_far, of_far_core,
        grads, swap(grads, "core"), far_grads, swap(far_grads, "core"),
    )
    for k, other in enumerate(others, 1):
        piece = piece + swap(other, "z", 8, k).astype(F32)
    grad_weights = lax.ppermute(piece.reshape(2, 24, width), ("y", *TGT), to_owner())
    return (output, grad_weights, grad_features)


def solution(mesh):
    fine = Mesh(mesh.devices.reshape(2, 4, 2, 8, 2), (*REL, *TGT))
    placed = (
        P(TGT, None),
        P(REL, None, None),
        P(),
        P(TGT, None),
        P(REL, TGT, None, None),
        P(REL, TGT),
        P(REL, TGT, None),
        P(),
    )
    return jax.shard_map(
        per_device,
        mesh=fine,
        in_specs=placed,
        out_specs=(P(TGT, REL), P(REL, TGT, None), P(TGT, REL, None)),
        check_vma=False,
    )
```

```python
import functools

import jax
import jax.numpy as jnp
from jax import lax
from jax.experimental import pallas as pl
from jax.experimental.pallas import tpu as pltpu
from jax.sharding import Mesh, PartitionSpec as P

F32 = jnp.float32
BF16 = jnp.bfloat16
BLK = 128
REL = ("xl", "y")
TGT = ("xh", "z", "core")
VMEM_LIMIT = 44 * 1024 * 1024


def in_hbm(value):
    return pltpu.with_memory_space_constraint(value, pltpu.MemorySpace.HBM)


def resident(value):
    return pltpu.with_memory_space_constraint(value, pltpu.MemorySpace.VMEM)


def params(*semantics):
    return pltpu.CompilerParams(
        dimension_semantics=semantics or None, vmem_limit_bytes=VMEM_LIMIT
    )


def smem():
    return pl.BlockSpec(memory_space=pltpu.MemorySpace.SMEM)


def vmem():
    return pl.BlockSpec(memory_space=pltpu.MemorySpace.VMEM)


def dot(a, b, ca, cb):
    return lax.dot_general(a, b, (((ca,), (cb,)), ((), ())), preferred_element_type=F32)


def adjacency_kernel(count_ref, values_ref, out_ref):
    count = count_ref[pl.program_id(0), pl.program_id(1)]
    slots = values_ref.shape[2]
    live, degree = [], None
    for s in range(slots):
        v = values_ref[0, :, s, :]
        v = jnp.where(s < count, v, jnp.zeros_like(v)).astype(F32)
        live.append(v)
        degree = v if degree is None else degree + v
    total = jnp.sum(degree, axis=1, keepdims=True)
    scale = 1.0 / jnp.sqrt(jnp.maximum(total, 1.0))
    for s in range(slots):
        out_ref[0, :, s * BLK : (s + 1) * BLK] = (live[s] * scale).astype(BF16)


def adjacency_of(tile_values, tile_count):
    rels, rows, slots, cols = tile_values.shape
    return pl.pallas_call(
        adjacency_kernel,
        grid=(rels, rows // BLK),
        in_specs=[smem(), pl.BlockSpec((1, BLK, slots, cols), lambda r, q: (r, q, 0, 0))],
        out_specs=pl.BlockSpec((1, BLK, slots * cols), lambda r, q: (r, q, 0)),
        out_shape=jax.ShapeDtypeStruct((rels, rows, slots * cols), BF16),
        compiler_params=params("arbitrary", "arbitrary"),
        name="adjacency",
    )(tile_count, tile_values)


def outgoing_kernel(place_ref, table_ref, features_ref, out_ref, turned_ref):
    owner, first = place_ref[0], place_ref[1]
    turned_ref[...] = features_ref[...].T
    piece = turned_ref[pl.ds(pl.multiple_of(first, 64), 192), :]
    block0, block1 = piece[:, :BLK], piece[:, BLK:]
    for t in range(out_ref.shape[0]):
        k = table_ref[t, owner]
        picked = jnp.where(k == 1, block1, block0)
        out_ref[t] = jnp.where(k >= 0, picked, jnp.zeros_like(picked))


def outgoing_of(features, source_blocks, place):
    rows, width = features.shape
    return pl.pallas_call(
        outgoing_kernel,
        in_specs=[smem(), smem(), vmem()],
        out_specs=vmem(),
        out_shape=jax.ShapeDtypeStruct((source_blocks.shape[0], 192, BLK), BF16),
        scratch_shapes=[pltpu.VMEM((width, rows), BF16)],
        compiler_params=params(),
        name="outgoing",
    )(place, source_blocks, features)


ORDER = (0, 1, 3, 2)


def start_loads(adj_refs, adj_buf, sems):
    own, back, fore, far0, far1 = adj_refs
    loads = []
    for n, ref in enumerate((own, back, fore)):
        loads.append([pltpu.make_async_copy(ref, adj_buf.at[pl.ds(2 * n, 2)], sems.at[n])])
    loads.append(
        [pltpu.make_async_copy(ref, adj_buf.at[pl.ds(6 + n, 1)], sems.at[3 + n]) for n, ref in enumerate((far0, far1))]
    )
    for group in loads:
        for load in group:
            load.start()
    return loads


def load_scratch(rows, wide):
    return [pltpu.VMEM((8, rows, wide), BF16), pltpu.SemaphoreType.DMA((5,))]


def hbm():
    return pl.BlockSpec(memory_space=pltpu.MemorySpace.HBM)


def join_kernel(own_ref, own_slots_ref, came1_ref, came2_ref, came3_ref, part_ref, slots_ref):
    part_ref[0] = own_ref[0]
    slots_ref[0:1] = own_slots_ref[0, :, :BLK].astype(F32).astype(jnp.int32)[0:1]
    for k, ref in enumerate((came1_ref, came2_ref, came3_ref), 1):
        part_ref[k] = ref[0, :96]
        slots_ref[k : k + 1] = ref[0, 96:, :BLK].astype(F32).astype(jnp.int32)[0:1]


def join(own, own_slots, came):
    return pl.pallas_call(
        join_kernel,
        in_specs=[vmem()] * 5,
        out_specs=[vmem(), vmem()],
        out_shape=[
            jax.ShapeDtypeStruct((4, *own.shape[1:]), BF16),
            jax.ShapeDtypeStruct((4, BLK), jnp.int32),
        ],
        compiler_params=params(),
        name="join",
    )(own, own_slots, *came)


def forward_kernel(
    place_ref, slot_ref, own_ref, back_ref, fore_ref, far0_ref, far1_ref, fetched_ref, w_mine_ref, w_theirs_ref,
    keep_ref, keep_far_ref, send_ref, send_far_ref, pre_ref, adj_buf, sems, both_ref, acc_ref,
):
    core, y = place_ref[2], place_ref[3]
    loads = start_loads((own_ref, back_ref, fore_ref, far0_ref, far1_ref), adj_buf, sems)
    for n, k in enumerate(ORDER):
        for load in loads[n]:
            load.wait()
        for p in range(2):
            for q in range(2):
                base = (p * 2 + q) * 8
                wide = jnp.concatenate([fetched_ref[slot_ref[k, base + s]] for s in range(8)], axis=1)
                part = adj_buf[2 * n + p, q * BLK : (q + 1) * BLK, :]
                both_ref[p, :, q * BLK : (q + 1) * BLK] = dot(wide, part, 1, 1).astype(BF16)
        j = (y - k) & 3
        far, pair = (j >> 1) ^ place_ref[4], pl.ds(2 * (j & 1), 2)
        keep = both_ref[:, pl.ds(pl.multiple_of(96 * core, 32), 96)]
        send = both_ref[:, pl.ds(pl.multiple_of(96 * (1 - core), 32), 96)]

        @pl.when(far == 0)
        def _():
            keep_ref[pair] = keep
            send_ref[pair] = send

        @pl.when(far == 1)
        def _():
            keep_far_ref[pair] = keep
            send_far_ref[pair] = send

        term = dot(w_mine_ref[k], both_ref[core], 0, 0) + dot(w_theirs_ref[k], both_ref[1 - core], 0, 0)
        if n == 0:
            acc_ref[...] = term
        elif n < 3:
            acc_ref[...] += term
        else:
            pre_ref[...] = (acc_ref[...] + term).astype(BF16)


def forward_of(place, slots, adjacency, fetched, w_mine, w_theirs):
    _, rows, wide = adjacency[0].shape
    width = w_mine.shape[2]
    half = pltpu.MemorySpace.HBM((4, 96, rows), BF16)
    return pl.pallas_call(
        forward_kernel,
        in_specs=[smem(), smem()] + [hbm()] * 5 + [vmem()] * 3,
        out_specs=[vmem()] * 5,
        out_shape=[half, half, half, half, jax.ShapeDtypeStruct((width, rows), BF16)],
        scratch_shapes=load_scratch(rows, wide)
        + [pltpu.VMEM((2, 192, rows), BF16), pltpu.VMEM((width, rows), F32)],
        compiler_params=params(),
        name="forward",
    )(place, slots, *adjacency, fetched, w_mine, w_theirs)


def activation_kernel(arrived_ref, bias_ref, cotangent_ref, act_ref, grad_ref):
    pre = bias_ref[...]
    for g in range(arrived_ref.shape[0]):
        pre = pre + arrived_ref[g].astype(F32)
    sigmoid = jax.nn.sigmoid(pre)
    act_ref[...] = (pre * sigmoid).astype(BF16)
    derivative = sigmoid * (1.0 + pre * (1.0 - sigmoid))
    grad = (cotangent_ref[...].astype(F32) * derivative).astype(BF16)
    for g in range(grad_ref.shape[0]):
        grad_ref[g] = grad


def activation_of(arrived, bias, cotangent):
    return pl.pallas_call(
        activation_kernel,
        in_specs=[vmem()] * 3,
        out_specs=[vmem()] * 2,
        out_shape=[
            jax.ShapeDtypeStruct(arrived.shape[1:], BF16),
            jax.ShapeDtypeStruct(arrived.shape, BF16),
        ],
        compiler_params=params(),
        name="activation",
    )(arrived, bias, cotangent)


def backward_kernel(
    place_ref, slot_ref, own_ref, back_ref, fore_ref, far0_ref, far1_ref, grad_ref, w_mine_ref, w_theirs_ref,
    out_ref, adj_buf, sems, both_ref, acc_ref,
):
    core = place_ref[2]
    loads = start_loads((own_ref, back_ref, fore_ref, far0_ref, far1_ref), adj_buf, sems)
    acc_ref[...] = jnp.zeros_like(acc_ref)
    for n, k in enumerate(ORDER):
        both_ref[core] = dot(w_mine_ref[k], grad_ref[...], 1, 0).astype(BF16)
        both_ref[1 - core] = dot(w_theirs_ref[k], grad_ref[...], 1, 0).astype(BF16)
        for load in loads[n]:
            load.wait()
        for p in range(2):
            for q in range(2):
                base = (p * 2 + q) * 8
                part = adj_buf[2 * n + p, q * BLK : (q + 1) * BLK, :]
                wide = dot(both_ref[p, :, q * BLK : (q + 1) * BLK], part, 1, 0)
                for s in range(8):
                    acc_ref[slot_ref[k, base + s]] += wide[:, s * BLK : (s + 1) * BLK]
    out_ref[...] = acc_ref[...].astype(BF16)


def backward_of(place, slots, adjacency, grads, w_mine, w_theirs, owners):
    _, rows, wide = adjacency[0].shape
    return pl.pallas_call(
        backward_kernel,
        in_specs=[smem(), smem()] + [hbm()] * 5 + [vmem()] * 3,
        out_specs=vmem(),
        out_shape=jax.ShapeDtypeStruct((owners, 192, BLK), BF16),
        scratch_shapes=load_scratch(rows, wide)
        + [pltpu.VMEM((2, 192, rows), BF16), pltpu.VMEM((owners, 192, BLK), F32)],
        compiler_params=params(),
        name="backward",
    )(place, slots, *adjacency, grads, w_mine, w_theirs)


def weight_kernel(
    place_ref, own_ref, core_ref, far_ref, far_core_ref, grad_ref, core_grad_ref, far_grad_ref, far_core_grad_ref, *refs
):
    *out_refs, pieces_ref = refs
    z = place_ref[5]
    grads = jnp.concatenate(
        [grad_ref[...], core_grad_ref[...], far_grad_ref[...], far_core_grad_ref[...]], axis=1
    )
    for r in range(4):
        wide = jnp.concatenate([own_ref[r], core_ref[r], far_ref[r], far_core_ref[r]], axis=1)
        term = dot(wide, grads, 1, 1)
        for m in range(4):
            part = slice(24 * (r % 2), 24 * (r % 2) + 24)
            pieces_ref[4 * (r // 2) + m, part] = term[m * 24 : (m + 1) * 24]
    for k, out_ref in enumerate(out_refs):
        out_ref[...] = pieces_ref[z ^ k].astype(out_ref.dtype)


def weight_terms_of(place, *operands):
    width = operands[-1].shape[0]
    return pl.pallas_call(
        weight_kernel,
        in_specs=[smem()] + [vmem()] * 8,
        out_specs=[vmem()] * 8,
        out_shape=[jax.ShapeDtypeStruct((48, width), F32 if k == 0 else BF16) for k in range(8)],
        scratch_shapes=[pltpu.VMEM((8, 48, width), F32)],
        compiler_params=params(),
        name="weight_terms",
        cost_estimate=pl.CostEstimate(flops=24500000000, transcendentals=0, bytes_accessed=0),
    )(place, *operands)


def owned_kernel(place_ref, table_ref, arrived_ref, out_ref):
    owner = place_ref[0]
    zero = jnp.zeros(arrived_ref.shape[1:], F32)
    sums = [zero, zero]
    for t in range(arrived_ref.shape[0]):
        k = table_ref[t, owner]
        v = arrived_ref[t].astype(F32)
        for b in range(2):
            sums[b] = sums[b] + jnp.where(k == b, v, zero)
    for b in range(2):
        turned = sums[b].T
        for g in range(out_ref.shape[0]):
            out_ref[g, b] = turned[g * 16 : (g + 1) * 16, :]


def owned_of(place, source_blocks, arrived, groups):
    return pl.pallas_call(
        owned_kernel,
        in_specs=[smem(), smem(), vmem()],
        out_specs=vmem(),
        out_shape=jax.ShapeDtypeStruct((groups, 2, BLK // groups, arrived.shape[1]), F32),
        compiler_params=params(),
        name="owned",
    )(place, source_blocks, arrived)


def step(value, by):
    return lax.ppermute(value, "y", [(i, (i + by) % 4) for i in range(4)])


def swap(value, axis, size=2, flip=1):
    return lax.ppermute(value, axis, [(i, i ^ flip) for i in range(size)])


def exchange(value, axis):
    return lax.all_to_all(value, axis, 0, 0, tiled=True)


def around(values, axis, size):
    return [
        lax.ppermute(v, axis, [(i, (i + k) % size) for i in range(size)])
        for k, v in enumerate(values, 1)
    ]


def to_owner():
    def place(y, xh, z, c):
        return ((y * 2 + xh) * 8 + z) * 2 + c
    moves = []
    for y in range(4):
        for xh in range(2):
            for z in range(8):
                for c in range(2):
                    m = 4 * c + z % 4
                    target = place(2 * xh + z // 4, y // 2, 4 * (y % 2) + m // 2, m % 2)
                    moves.append((place(y, xh, z, c), target))
    return moves


def per_device(
    features, weights, bias, cotangent, tile_values, tile_count, tile_slot, source_blocks
):
    groups = 8
    owners = source_blocks.shape[0]
    width = features.shape[1]
    xl, y, core = lax.axis_index("xl"), lax.axis_index("y"), lax.axis_index("core")
    owner = lax.axis_index(TGT)
    group = lax.axis_index(REL)
    xh, z = lax.axis_index("xh"), lax.axis_index("z")
    xh, z = lax.axis_index("xh"), lax.axis_index("z")
    place = in_hbm(jnp.stack([owner, 192 * y, core, y, xh, z]).astype(jnp.int32))

    own = adjacency_of(in_hbm(tile_values), in_hbm(tile_count))
    back, fore = step(own, 1), step(own, -1)
    features, weights, _ = lax.optimization_barrier((features, weights, own))
    source_blocks = in_hbm(source_blocks)
    outgoing = outgoing_of(in_hbm(features), source_blocks, place)
    fetched = resident(exchange(outgoing, TGT))

    own_slots = jnp.pad(tile_slot.reshape(1, 1, -1), ((0, 0), (0, 15), (0, width - 32))).astype(BF16)
    pieces = []
    for k in range(4):
        cut = lax.dynamic_slice(weights, (core, ((y + k) & 3) * 192 + 96 * xh, 0), (1, 96, width))
        pieces.append(jnp.concatenate([cut, own_slots], axis=1) if k else cut)
    came = around(pieces[1:], "y", 4)
    share = width // groups
    bias_share = lax.dynamic_slice_in_dim(bias, group * share, share)
    bias_share = jnp.broadcast_to(bias_share[:, None], (share, features.shape[0]))
    cotangent_share = lax.dynamic_slice_in_dim(cotangent, group * share, share, 1).T
    w_part, slots = join(pieces[0], own_slots, came)
    w_part, bias_share, cotangent_share = lax.optimization_barrier((w_part, bias_share, cotangent_share))
    slots, bias_share, cotangent_share = in_hbm(slots), in_hbm(bias_share), in_hbm(cotangent_share)
    far0, far1 = step(back[:1], 1), step(fore[1:], -1)
    w_other = swap(w_part, "xh")
    w_part, w_other, far0, far1 = lax.optimization_barrier((w_part, w_other, far0, far1))
    w_mine = jnp.concatenate(
        [jnp.where(xh == 0, w_part, w_other), jnp.where(xh == 0, w_other, w_part)], axis=1
    )
    w_mine, w_theirs = resident(w_mine), resident(swap(w_mine, "core"))
    adjacency = [in_hbm(a) for a in (own, back, fore, far0, far1)]

    own_terms, far_terms, for_core, for_far_core, part = forward_of(
        place, slots, adjacency, fetched, w_mine, w_theirs
    )
    of_core, of_far = swap(for_core, "core"), swap(far_terms, "xh")
    of_far_core = swap(for_far_core, "core")
    arrived, of_far_core = lax.optimization_barrier((exchange(part.reshape(groups, share, -1), REL), of_far_core))
    arrived = resident(arrived)
    activated, grad_copies = activation_of(arrived, bias_share, cotangent_share)
    output = activated.T
    of_far_core = swap(of_far_core, "xh")
    grad_copies, of_far = lax.optimization_barrier((grad_copies, of_far))
    grads, of_core = lax.optimization_barrier((exchange(grad_copies, REL).reshape(width, -1), of_core))
    of_core, of_far, of_far_core = in_hbm(of_core), in_hbm(of_far), in_hbm(of_far_core)
    partial = backward_of(place, slots, adjacency, resident(grads), w_mine, w_theirs, owners)
    returned = resident(exchange(in_hbm(partial), TGT))
    cut = owned_of(place, source_blocks, returned, groups)
    columns = exchange(cut, REL).reshape(2, 4, 2, BLK // groups, 192).sum(axis=0)
    grad_features = columns.transpose(1, 2, 0, 3).reshape(2, BLK // groups, width)

    far_grads, _ = lax.optimization_barrier((swap(grads, "xh"), partial))
    piece, *others = weight_terms_of(
        place, own_terms, of_core, of_far, of_far_core,
        grads, swap(grads, "core"), far_grads, swap(far_grads, "core"),
    )
    for k, other in enumerate(others, 1):
        piece = piece + swap(other, "z", 8, k).astype(F32)
    grad_weights = lax.ppermute(piece.reshape(2, 24, width), ("y", *TGT), to_owner())
    return (output, grad_weights, grad_features)


def solution(mesh):
    fine = Mesh(mesh.devices.reshape(2, 4, 2, 8, 2), (*REL, *TGT))
    placed = (
        P(TGT, None),
        P(REL, None, None),
        P(),
        P(TGT, None),
        P(REL, TGT, None, None),
        P(REL, TGT),
        P(REL, TGT, None),
        P(),
    )
    return jax.shard_map(
        per_device,
        mesh=fine,
        in_specs=placed,
        out_specs=(P(TGT, REL), P(REL, TGT, None), P(TGT, REL, None)),
        check_vma=False,
    )
```
